128 devices in a mesh: pipe: 2 (over core), tok: 64 (over y, z, x).
Axes of the slice: x: 4, y: 4, z: 4, core: 2. Of those that a mesh axis runs over, the one named last changes fastest.
Arguments:
- features: bfloat16 [2, 16384, 256], P(None, 'tok'), may hold values from -6 to 6
- coarse: bfloat16 [2, 4096, 256], P(None, 'tok'), may hold values from -6 to 6
- parent: int32 [2, 16384], P(None, 'tok'), may hold values from -1 to 4095, as said below
- counts: int32 [2, 64], replicated, may hold values from 1 to 256, 12288 in all within a row
- target: float32 [2, 16384], P(None, 'tok'), may hold values from -6 to 6
- gain_attn: float32 [2, 256], P('pipe'), may hold values from 0.25 to 1.75
- w_qkv: bfloat16 [2, 256, 768], P('pipe'), may hold values from -0.375 to 0.375
- w_out: bfloat16 [2, 256, 256], P('pipe'), may hold values from -0.375 to 0.375
- gain_mlp: float32 [2, 256], P('pipe'), may hold values from 0.25 to 1.75
- w_up: bfloat16 [2, 256, 1024], P('pipe'), may hold values from -0.375 to 0.375
- w_down: bfloat16 [2, 1024, 256], P('pipe'), may hold values from -0.1875 to 0.1875
- w_sdf: float32 [256], replicated, may hold values from -0.375 to 0.375
Outputs:
- loss: float32 [], replicated
- grad_sdf: float32 [256], replicated
- grad_gain_attn: float32 [2, 256], P('pipe')
- grad_qkv: float32 [2, 256, 768], P('pipe')
- grad_out: float32 [2, 256, 256], P('pipe')
- grad_gain_mlp: float32 [2, 256], P('pipe')
- grad_up: float32 [2, 256, 1024], P('pipe')
- grad_down: float32 [2, 1024, 256], P('pipe')
The draws below stay inside these ranges and needn't reach their ends.
Inputs may be any that keep to these rules, and one draw needn't show every extreme that they name: parent never falls along the tokens of a micro-batch; the tokens of shard d (rows d * 256 to (d + 1) * 256 - 1) have parents d * 64 - 1 to (d + 1) * 64 - 1, the first token of every shard has parent d * 64 - 1, and every parent has a child.
All inputs are finite; a program needn't handle non-finite values.
Results may differ from the reference program's by a relative error of at most 0.005.
Values may be sent and summed in bfloat16 or wider, within the bound.
No kernel may reach another device: no remote copies, remote signals or barrier semaphores. Data moves between devices by JAX's collectives and lax.ppermute only.
A program may use at most 128 MiB of HBM per device.

```python
import math
import jax
import jax.numpy as jnp
import numpy as np
from jax import lax

C = 256
H = 8
FF = 1024
WIN = 32
MICRO = 2
TOK_DEV = 256
TOKENS = 16384
PIECE = 4
PAR_DEV = 64
PAR_TOTAL = 4096
VALID = 12288
N_PIPE = 2
N_TOK = 64


def draw_parent(key, part):
    shard_count = TOKENS // TOK_DEV

    def one_shard(shard_key, shard_idx):
        chosen = jax.random.permutation(shard_key, TOK_DEV - 1) + 1
        starts = jnp.zeros((TOK_DEV,), jnp.int32).at[chosen[:PAR_DEV]].set(1)
        local_parent = jnp.cumsum(starts) - 1
        return (local_parent + shard_idx * PAR_DEV).astype(jnp.int32)
    shard_keys = jax.random.split(jax.random.fold_in(key, 17), MICRO * shard_count)
    shard_ids = jnp.tile(jnp.arange(shard_count, dtype=jnp.int32), MICRO)
    drawn = jax.vmap(one_shard)(shard_keys, shard_ids)
    return drawn.reshape(MICRO, TOKENS)


def level_of(rng, extent, cuts, low, largest):
    gain = 1.0
    for dim, shards_of in cuts:
        heights = jax.random.uniform(jax.random.fold_in(jax.random.fold_in(rng, 6), dim), (shards_of,), jnp.float32, low / len(cuts), largest / len(cuts))
        gain = gain * jnp.repeat(jnp.exp(heights), extent[dim] // shards_of).reshape((-1,) + (1,) * (len(extent) - 1 - dim))
    return gain


def length_profile(number_of, total, bound, slope):
    weights = [(1 << 20) // math.isqrt(grade ** slope) + 1 for grade in range(2, number_of + 1)]
    rest, given = total - bound - (number_of - 1), [1] * (number_of - 1)
    while rest > 0:
        free = [i for i in range(number_of - 1) if given[i] < bound]
        pool, budget = sum([weights[i] for i in free]), rest
        for i in free:
            extra = min(bound - given[i], max(1, budget * weights[i] // pool), rest)
            given[i] = given[i] + extra
            rest = rest - extra
    return np.array([bound] + given)


def uneven(stream_key, number_of, total, most, slope):
    if number_of == 2:
        one = jax.random.randint(stream_key, (), max(1, total - most), min(most, total - 1) + 1)
        return jnp.stack([one, total - one])
    sizes = jnp.asarray(length_profile(number_of, total, most, slope), jnp.int32)
    twos = (number_of - 1) // 2
    source_of, sink = sizes[1:1 + 2 * twos:2], sizes[2:2 + 2 * twos:2]
    room = jnp.minimum(source_of - 1, most - sink)
    shifted = jax.random.randint(jax.random.fold_in(stream_key, 1), (twos,), 0, 1 << 20) % (room + 1)
    sizes = sizes.at[1:1 + 2 * twos:2].set(source_of - shifted).at[2:2 + 2 * twos:2].set(sink + shifted)
    return sizes[jax.random.permutation(jax.random.fold_in(stream_key, 2), number_of)]


def normal_values(own_key, extent, spread, limit, cuts=(), kind=jnp.bfloat16):
    values = spread * jax.random.normal(own_key, extent, jnp.float32)
    if cuts:
        values = values * level_of(own_key, extent, cuts, -0.22, 0.18)
    return jnp.clip(values, -limit, limit).astype(kind)


def setup_inputs(seed: int = 0) -> dict:
    keys = jax.random.split(jax.random.key(seed), 13)
    return {
        "features": normal_values(keys[0], (MICRO, TOKENS, C), 1.0, 6.0, ((1, 64),)),
        "coarse": normal_values(keys[1], (MICRO, PAR_TOTAL, C), 1.0, 6.0, ((1, 64),)),
        "parent": draw_parent(jax.random.fold_in(keys[12], 71), 0),
        "counts": jax.vmap(lambda own: uneven(own, N_TOK, VALID, TOK_DEV, 2))(jax.random.split(keys[3], MICRO)).reshape((MICRO, N_TOK)).astype(jnp.int32),
        "target": normal_values(keys[4], (MICRO, TOKENS), 1.0, 6.0, ((1, 64),), jnp.float32),
        "gain_attn": jnp.clip(1.0 + 0.15 * jax.random.normal(keys[5], (N_PIPE, C), jnp.float32), 0.25, 1.75),
        "w_qkv": normal_values(keys[6], (N_PIPE, C, 3 * C), C ** -0.5, 0.375, ((0, 2),)),
        "w_out": normal_values(keys[7], (N_PIPE, C, C), C ** -0.5, 0.375, ((0, 2),)),
        "gain_mlp": jnp.clip(1.0 + 0.15 * jax.random.normal(keys[8], (N_PIPE, C), jnp.float32), 0.25, 1.75),
        "w_up": normal_values(keys[9], (N_PIPE, C, FF), C ** -0.5, 0.375, ((0, 2),)),
        "w_down": normal_values(keys[10], (N_PIPE, FF, C), FF ** -0.5, 0.1875, ((0, 2),)),
        "w_sdf": normal_values(keys[11], (C,), C ** -0.5, 0.375, (), jnp.float32),
    }


def norm_gain(values, gain_vec):
    mean_sq = lax.optimization_barrier(jnp.mean(values * values, axis=-1, keepdims=True))
    return values * lax.rsqrt(mean_sq + 1e-06) * gain_vec

def attend(packed, keys_ok):
    token_count = packed.shape[0]
    model_width = packed.shape[1] // 3
    head_size = model_width // H
    blocks = packed.astype(jnp.float32).reshape(token_count // WIN, WIN, 3, H, head_size)
    query_part = blocks[:, :, 0]
    key_part = blocks[:, :, 1]
    value_part = blocks[:, :, 2]
    scores = jnp.einsum('wqhd,wkhd->whqk', query_part, key_part, precision=lax.Precision.HIGHEST) * head_size ** (-0.5)
    allowed = keys_ok.reshape(token_count // WIN, 1, 1, WIN)
    scores = jnp.where(allowed, scores, -1e+30)
    attn_weights = jax.nn.softmax(scores, axis=-1).astype(jnp.bfloat16)
    attn_weights = lax.optimization_barrier(attn_weights).astype(jnp.float32)
    mixed_out = jnp.einsum('whqk,wkhd->wqhd', attn_weights, value_part, precision=lax.Precision.HIGHEST)
    return mixed_out.reshape(token_count, model_width)

def matmul(left, right):
    return jnp.dot(left, right, preferred_element_type=jnp.float32)

def block_forward(block_in, keys_ok, params, order, back_order):
    gain_one, qkv_weight, out_weight, gain_two, up_weight, down_weight = params
    normed = norm_gain(block_in.astype(jnp.float32), gain_one).astype(jnp.bfloat16)
    packed = matmul(normed, qkv_weight).astype(jnp.bfloat16)
    packed_win = packed[order]
    mixed_out = attend(packed_win, keys_ok).astype(jnp.bfloat16)[back_order]
    after_attn = block_in.astype(jnp.float32) + matmul(mixed_out, out_weight)
    normed_two = norm_gain(after_attn, gain_two).astype(jnp.bfloat16)
    upward = matmul(normed_two, up_weight)
    hidden = jax.nn.gelu(upward).astype(jnp.bfloat16)
    block_out = (after_attn + matmul(hidden, down_weight)).astype(jnp.bfloat16)
    saved = (block_in, normed, packed_win, mixed_out, after_attn, normed_two, upward, hidden)
    return (block_out, saved)

def block_backward(out_grad, saved, keys_ok, params, order, back_order):
    gain_one, qkv_weight, out_weight, gain_two, up_weight, down_weight = params
    block_in, normed, packed_win, mixed_out, after_attn, normed_two, upward, hidden = saved
    grad_down = matmul(hidden.T, out_grad)
    hidden_grad = matmul(out_grad, down_weight.T).astype(jnp.bfloat16)
    gelu_back = jax.vjp(jax.nn.gelu, upward)[1]
    up_grad = gelu_back(hidden_grad.astype(jnp.float32))[0].astype(jnp.bfloat16)
    grad_up = matmul(normed_two.T, up_grad)
    normed_two_grad = matmul(up_grad, up_weight.T).astype(jnp.bfloat16)
    norm_back = jax.vjp(norm_gain, after_attn, gain_two)[1]
    attn_res_grad, grad_gain_two = norm_back(normed_two_grad.astype(jnp.float32))
    after_grad = out_grad.astype(jnp.float32) + attn_res_grad
    after_grad_low = after_grad.astype(jnp.bfloat16)
    grad_out = matmul(mixed_out.T, after_grad_low)
    mixed_grad = matmul(after_grad_low, out_weight.T).astype(jnp.bfloat16)
    attn_back = jax.vjp(lambda packed_in: attend(packed_in, keys_ok), packed_win)[1]
    packed_grad_win = attn_back(mixed_grad[order].astype(jnp.float32))[0]
    packed_grad = packed_grad_win[back_order]
    grad_qkv = matmul(normed.T, packed_grad)
    normed_grad = matmul(packed_grad, qkv_weight.T).astype(jnp.bfloat16)
    in_back = jax.vjp(norm_gain, block_in.astype(jnp.float32), gain_one)[1]
    in_res_grad, grad_gain_one = in_back(normed_grad.astype(jnp.float32))
    in_grad = (after_grad + in_res_grad).astype(jnp.bfloat16)
    return (in_grad, (grad_gain_one, grad_qkv, grad_out, grad_gain_two, grad_up, grad_down))

def reference(features, coarse, parent, counts, target, gain_attn, w_qkv, w_out, gain_mlp, w_up, w_down, w_sdf):
    padded = jnp.concatenate([jnp.zeros((MICRO, 1, C), jnp.bfloat16), coarse], axis=1)
    lifted = jnp.take_along_axis(padded, (parent + 1)[:, :, None], axis=1)
    embedded = (features.astype(jnp.float32) + lifted.astype(jnp.float32)).astype(jnp.bfloat16)
    global_row = jnp.arange(TOKENS, dtype=jnp.int32)
    dest_part = global_row // TOK_DEV
    src_part = global_row % TOK_DEV // PIECE
    offset_part = global_row % PIECE
    order = src_part * TOK_DEV + dest_part * PIECE + offset_part
    in_shard = global_row % TOK_DEV
    back_order = in_shard // PIECE * TOK_DEV + global_row // TOK_DEV * PIECE + in_shard % PIECE
    plain_order = global_row
    section_params = [(gain_attn[k], w_qkv[k], w_out[k], gain_mlp[k], w_up[k], w_down[k]) for k in range(2)]
    grad_totals = [tuple((jnp.zeros(p.shape, jnp.float32) for p in section_params[k])) for k in range(2)]
    loss_total = jnp.zeros((), jnp.float32)
    sdf_total = jnp.zeros((C,), jnp.float32)
    for micro_idx in range(MICRO):
        valid = in_shard < jnp.take(counts[micro_idx], global_row // TOK_DEV)
        keys_dilated = valid[order]
        keys_plain = valid
        section_zero, saved_zero = block_forward(embedded[micro_idx], keys_dilated, section_params[0], order, back_order)
        section_one, saved_one = block_forward(section_zero, keys_plain, section_params[1], plain_order, plain_order)
        predicted = lax.optimization_barrier(jnp.sum(section_one.astype(jnp.float32) * w_sdf, axis=-1))
        residue = jnp.where(valid, predicted - target[micro_idx], 0.0)
        slope_term = 2.0 * residue / jnp.sqrt(jnp.float32(VALID))
        loss_total = loss_total + jnp.sum(residue * residue)
        sdf_total = sdf_total + lax.optimization_barrier(jnp.sum(slope_term[:, None] * section_one.astype(jnp.float32), axis=0))
        head_grad = (slope_term[:, None] * w_sdf).astype(jnp.bfloat16)
        grad_mid, grads_one = block_backward(head_grad, saved_one, keys_plain, section_params[1], plain_order, plain_order)
        unused_grad, grads_zero = block_backward(grad_mid, saved_zero, keys_dilated, section_params[0], order, back_order)
        grad_totals[0] = tuple((a + b for a, b in zip(grad_totals[0], grads_zero)))
        grad_totals[1] = tuple((a + b for a, b in zip(grad_totals[1], grads_one)))
    loss = loss_total / (MICRO * VALID)
    stacked = [jnp.stack([grad_totals[0][k], grad_totals[1][k]]) for k in range(6)]
    return (loss, sdf_total, stacked[0], stacked[1], stacked[2], stacked[3], stacked[4], stacked[5])
```

```python
import functools
import math

import jax
import jax.numpy as jnp
from jax import lax
from jax.experimental import pallas as pl
from jax.experimental.pallas import tpu as pltpu
from jax.sharding import PartitionSpec as P

H = 8
WIN = 32
GROUP = 8
ROWS = 256
WIDTH = 256
FF = 1024
HEAD = WIDTH // H
EPS = 1e-06
CHUNK = 96
CHUNK_PAD = 104
SEND_ROWS = 40
BF = jnp.bfloat16
F32 = jnp.float32


def nn(a, b):
    return jnp.dot(a, b, preferred_element_type=F32)


def nt(a, b):
    return lax.dot_general(a, b, (((1,), (1,)), ((), ())), preferred_element_type=F32)


def tn(a, b):
    return lax.dot_general(a, b, (((0,), (0,)), ((), ())), preferred_element_type=F32)


def iota(shape, dim):
    return lax.broadcasted_iota(jnp.int32, shape, dim)


def split_two(value):
    high = value.astype(BF)
    low = (value - high.astype(F32)).astype(BF)
    return high, low


def embed_kernel(features_ref, coarse_ref, rim_ref, parent_ref, target_ref, out_ref):
    micro = lax.axis_index("pipe")
    shard = lax.axis_index("tok")
    local = parent_ref[pl.ds(micro, 1), :] - shard * coarse_ref.shape[1]
    own_hot = jnp.where(iota((64, ROWS), 0) == local, 1.0, 0.0).astype(BF)
    rim_hot = jnp.where((iota((16, ROWS), 0) == 0) & (local == -1), 1.0, 0.0).astype(BF)
    rim = jnp.broadcast_to(rim_ref[micro], (16, WIDTH))
    lifted = tn(own_hot, coarse_ref[micro]) + tn(rim_hot, rim)
    embedded = (features_ref[micro].astype(F32) + lifted).astype(BF)
    target = jnp.broadcast_to(target_ref[pl.ds(micro, 1), :], (8, ROWS))
    high = target.astype(BF).astype(F32)
    middle = (target - high).astype(BF).astype(F32)
    low = target - high - middle
    row = iota((8, ROWS), 0)
    extra = jnp.where(row == 0, high, jnp.where(row == 1, middle, jnp.where(row == 2, low, 0.0)))
    extra = extra.astype(BF)
    for part in range(GROUP):
        out_ref[part, 0:WIN, :] = embedded[part * WIN : (part + 1) * WIN]
        out_ref[part, WIN:SEND_ROWS, :] = extra


def group_max(values):
    lane = iota(values.shape, 1)
    for step in (1, 2, 4, 8, 16):
        ahead = pltpu.roll(values, values.shape[1] - step, 1)
        behind = pltpu.roll(values, step, 1)
        values = jnp.maximum(values, jnp.where((lane & step) == 0, ahead, behind))
    return values


def group_sum(values, same_head):
    high, low = split_two(values)
    return nn(high, same_head) + nn(low, same_head)


def step_kernel(
    counts_ref, received_ref, sdf_ref, gains_own_ref, gains_far_ref,
    qkv_own, qkv_far, out_own, out_far, up_own, up_far, down_own, down_far,
    keep_ref, send_ref,
    w_qkv, w_out, w_up, w_down,
    x_buf, inv_one, normed_buf, packed_buf, prob_buf, mixed_buf, after_buf, inv_two,
    normed_two_buf, slope_buf, hidden_buf, out_buf, mask_buf, grads, score_buf, dpacked_buf,
    load_sem, store_sem,
):
    micro = lax.axis_index("pipe")
    shard = lax.axis_index("tok")
    part = lax.rem(shard, GROUP)
    first = shard - part
    loads = []
    for number, (own, far, held) in enumerate(
        ((qkv_own, qkv_far, w_qkv), (out_own, out_far, w_out), (up_own, up_far, w_up), (down_own, down_far, w_down))
    ):
        loads.append(pltpu.make_async_copy(own.at[0], held.at[micro], load_sem.at[2 * number]))
        loads.append(pltpu.make_async_copy(far.at[0], held.at[1 - micro], load_sem.at[2 * number + 1]))
    for load in loads:
        load.start()

    own_is_first = micro == 0

    def gain(section, which):
        own = gains_own_ref[which : which + 1, :]
        far = gains_far_ref[which : which + 1, :]
        mine = own_is_first if section == 0 else jnp.logical_not(own_is_first)
        return jnp.where(mine, own, far)

    row_i = iota((ROWS, WIDTH), 0)
    col_i = iota((ROWS, WIDTH), 1)
    same_head = jnp.where(row_i // WIN == col_i // HEAD, 1.0, 0.0).astype(BF)
    swapped = row_i % WIN // 4 * WIN + row_i // WIN * 4 + row_i % 4
    swap = jnp.where(swapped == col_i, 1.0, 0.0).astype(BF)

    def exchange(value):
        return nn(swap, value).astype(BF)

    lane = iota((1, WIDTH), 1)
    key = lane % WIN
    count_of = [counts_ref[micro, first + s] for s in range(GROUP)]
    lane_count = jnp.zeros((1, WIDTH), jnp.int32)
    for s in range(GROUP):
        lane_count = jnp.where(key // 4 == s, count_of[s], lane_count)
    for w in range(GROUP):
        dilated = part * WIN + w * 4 + key % 4 < lane_count
        plain = part * WIN + key < count_of[w]
        mask_buf[0, w : w + 1, :] = jnp.where(dilated, 1.0, 0.0)
        mask_buf[1, w : w + 1, :] = jnp.where(plain, 1.0, 0.0)

    def expand(value):
        return jnp.concatenate([value] * H, axis=0) * same_head

    def window(value, w):
        return value[w * WIN : (w + 1) * WIN]

    def store_grad(section, block, value):
        for i in range(GROUP):
            slab = block * GROUP + i
            base = slab % 3 * WIN
            grads[section, slab // 3, base : base + WIN, :] = window(value, i).astype(BF)

    def store_wide(section, block, value):
        store_grad(section, block, value[:, :128])
        store_grad(section, block + 1, value[:, 128:])

    def forward(k):
        x = x_buf[k].astype(F32)
        inv = lax.rsqrt(jnp.mean(x * x, axis=-1, keepdims=True) + EPS)
        inv_one[k] = inv
        normed = (x * inv * gain(k, 0)).astype(BF)
        normed_buf[k] = normed
        if k == 0:
            loads[0].wait()
            loads[1].wait()
        for j in range(3):
            packed_buf[k, j] = nn(normed, w_qkv[k, :, j * WIDTH : (j + 1) * WIDTH]).astype(BF)
        for w in range(GROUP):
            rows = slice(w * WIN, (w + 1) * WIN)
            scores = nt(packed_buf[k, 0, rows, :], expand(packed_buf[k, 1, rows, :]))
            score_buf[rows, :] = jnp.where(mask_buf[k, w : w + 1, :] > 0.5, scores * HEAD**-0.5, -1e30)
        scores = score_buf[...]
        weights = jnp.exp(scores - group_max(scores))
        prob = weights / group_sum(weights, same_head)
        prob_buf[k] = prob
        prob_low = prob.astype(BF)
        for w in range(GROUP):
            rows = slice(w * WIN, (w + 1) * WIN)
            mixed_buf[k, rows, :] = nn(window(prob_low, w), expand(packed_buf[k, 2, rows, :])).astype(BF)
        if k == 0:
            loads[2].wait()
            loads[3].wait()
        after = x + nn(mixed_buf[k], w_out[k])
        after_buf[k] = after
        inv = lax.rsqrt(jnp.mean(after * after, axis=-1, keepdims=True) + EPS)
        inv_two[k] = inv
        normed_two = (after * inv * gain(k, 1)).astype(BF)
        normed_two_buf[k] = normed_two
        if k == 0:
            for load in loads[4:]:
                load.wait()
        total = after
        for j in range(4):
            cols = slice(j * WIDTH, (j + 1) * WIDTH)
            up = nn(normed_two, w_up[k, :, cols])
            root = math.sqrt(2.0 / math.pi)
            square = up * up
            bent = jnp.tanh(root * (up + 0.044715 * (square * up)))
            half = 0.5 * (1.0 + bent)
            hidden = (up * half).astype(BF)
            hidden_buf[k, j] = hidden
            slope_buf[k, j] = half + (0.5 * root) * up * (1.0 - bent * bent) * (1.0 + (3 * 0.044715) * square)
            total = total + nn(hidden, w_down[k, cols, :])
        return total.astype(BF)

    def norm_back(grad, value, inv, gain_row):
        gain_grad = jnp.sum(grad * value * inv, axis=0, keepdims=True)
        scaled = grad * gain_row
        inner = jnp.mean(scaled * value, axis=-1, keepdims=True)
        return inv * (scaled - value * (inv * inv * inner)), gain_grad

    def backward(k, out_grad):
        back = None
        for j in range(4):
            cols = slice(j * WIDTH, (j + 1) * WIDTH)
            store_wide(k, 16 + 2 * j, tn(hidden_buf[k, j], out_grad))
            hidden_grad = nt(out_grad, w_down[k, cols, :]).astype(BF)
            up_grad = (slope_buf[k, j] * hidden_grad.astype(F32)).astype(BF)
            store_wide(k, 8 + 2 * j, tn(normed_two_buf[k], up_grad))
            term = nt(up_grad, w_up[k, :, cols])
            back = term if back is None else back + term
        normed_two_grad = back.astype(BF).astype(F32)
        res_grad, gain_two_grad = norm_back(normed_two_grad, after_buf[k], inv_two[k], gain(k, 1))
        after_grad = out_grad.astype(F32) + res_grad
        after_low = after_grad.astype(BF)
        store_wide(k, 6, tn(mixed_buf[k], after_low))
        mixed_grad = nt(after_low, w_out[k]).astype(BF)
        for w in range(GROUP):
            rows = slice(w * WIN, (w + 1) * WIN)
            score_buf[rows, :] = nt(window(mixed_grad, w), expand(packed_buf[k, 2, rows, :]))
        prob = prob_buf[k]
        prob_low = prob.astype(BF)
        prob_grad = score_buf[...].astype(BF).astype(F32)
        flow = prob * prob_grad
        score_grad = ((flow - prob * group_sum(flow, same_head)) * HEAD**-0.5).astype(BF)

        def fold(value):
            total = None
            for h in range(H):
                piece = jnp.where(col_i[:WIN] // HEAD == h, window(value, h), 0.0)
                total = piece if total is None else total + piece
            return total

        for w in range(GROUP):
            rows = slice(w * WIN, (w + 1) * WIN)
            grad_w = window(score_grad, w)
            dpacked_buf[0, rows, :] = nn(grad_w, expand(packed_buf[k, 1, rows, :])).astype(BF)
            dpacked_buf[1, rows, :] = fold(tn(grad_w, packed_buf[k, 0, rows, :])).astype(BF)
            dpacked_buf[2, rows, :] = fold(tn(window(prob_low, w), window(mixed_grad, w))).astype(BF)
        back = None
        for j in range(3):
            piece = dpacked_buf[j]
            store_wide(k, 2 * j, tn(normed_buf[k], piece))
            term = nt(piece, w_qkv[k, :, j * WIDTH : (j + 1) * WIDTH])
            back = term if back is None else back + term
        normed_grad = back.astype(BF).astype(F32)
        in_res, gain_one_grad = norm_back(normed_grad, x_buf[k].astype(F32), inv_one[k], gain(k, 0))
        return (after_grad + in_res).astype(BF), gain_one_grad, gain_two_grad

    received = received_ref[:, 0:WIN, :].reshape(ROWS, WIDTH)
    x_buf[0] = exchange(received)
    x_buf[1] = exchange(forward(0))
    section_one = forward(1).astype(F32)

    pieces = []
    lane_w = iota((WIN, WIDTH), 1)
    row_w = iota((WIN, WIDTH), 0)
    valid_pieces = []
    for s in range(GROUP):
        parts = received_ref[s, WIN : WIN + 8, :].astype(F32)
        line = parts[0:1] + parts[1:2] + parts[2:3]
        chosen = jnp.where(lane_w == part * WIN + row_w, line, 0.0)
        pieces.append(jnp.sum(chosen, axis=-1, keepdims=True))
        valid_pieces.append(part * WIN + iota((WIN, 1), 0) < count_of[s])
    target = jnp.concatenate(pieces, axis=0)
    valid = jnp.concatenate([jnp.where(v, 1.0, 0.0) for v in valid_pieces], axis=0)
    sdf = sdf_ref[...]
    predicted = jnp.sum(section_one * sdf, axis=-1, keepdims=True)
    residue = jnp.where(valid > 0.5, predicted - target, 0.0)
    slope = 2.0 * residue / math.sqrt(3 * ROWS * 64 // 4)
    loss = jnp.sum(residue * residue, axis=0, keepdims=True)
    sdf_grad = jnp.sum(slope * section_one, axis=0, keepdims=True)
    head_grad = (slope * sdf).astype(BF)
    middle_grad, one_one, one_two = backward(1, head_grad)
    unused, zero_one, zero_two = backward(0, exchange(middle_grad))
    del unused
    loss_row = jnp.broadcast_to(loss, (1, 128))
    stat_row = iota((8, 128), 0)
    for k, (gain_one, gain_two) in enumerate(((zero_one, zero_two), (one_one, one_two))):
        lines = []
        for line in (gain_one, gain_two, sdf_grad):
            lines += [line[:, :128], line[:, 128:]]
        lines.append(loss_row)
        grads[k, :, CHUNK:CHUNK_PAD, :] = jnp.zeros((64, CHUNK_PAD - CHUNK, 128), BF)
        for c, line in enumerate(lines):
            high, low = split_two(line)
            both = jnp.where(stat_row == 0, high.astype(F32), jnp.where(stat_row == 1, low.astype(F32), 0.0))
            grads[k, c, CHUNK:CHUNK_PAD, :] = both.astype(BF)
    stores = [
        pltpu.make_async_copy(grads.at[micro], keep_ref, store_sem.at[0]),
        pltpu.make_async_copy(grads.at[1 - micro], send_ref, store_sem.at[1]),
    ]
    for store in stores:
        store.start()
    for store in stores:
        store.wait()


def add_kernel(keep_ref, far_ref, out_ref):
    for c in range(0, 64, 8):
        total = keep_ref[c : c + 8].astype(F32) + far_ref[c : c + 8].astype(F32)
        out_ref[c : c + 8, 0:CHUNK, :] = total[:, :CHUNK].astype(BF)
        stat = total[:, CHUNK : CHUNK + 1] + total[:, CHUNK + 1 : CHUNK + 2]
        out_ref[c : c + 8, CHUNK:CHUNK_PAD, :] = stat_rows(stat, (8, 8, 128), 1)


def stat_rows(stat, shape, dim):
    high, low = split_two(stat)
    row = iota(shape, dim)
    both = jnp.where(row == 0, high.astype(F32), jnp.where(row == 1, low.astype(F32), 0.0))
    return both.astype(BF)


def sum_kernel(in_ref, out_ref):
    total = in_ref[0].astype(F32)
    for c in range(1, 64):
        total = total + in_ref[c].astype(F32)
    stat = total[CHUNK : CHUNK + 1] + total[CHUNK + 1 : CHUNK + 2]
    main = total[:CHUNK].astype(BF)
    tail = stat_rows(stat, (8, 128), 0)
    for c in range(64):
        out_ref[c, 0:CHUNK, :] = main
        out_ref[c, CHUNK:CHUNK_PAD, :] = tail


def unpack_kernel(in_ref, loss_ref, sdf_ref, gain_one_ref, qkv_ref, out_ref, gain_two_ref, up_ref, down_ref):
    for block in range(24):
        for i in range(GROUP):
            slab = block * GROUP + i
            base = slab % 3 * WIN
            piece = in_ref[slab // 3, base : base + WIN, :].astype(F32)
            rows = slice(i * WIN, (i + 1) * WIN)
            if block < 6:
                qkv_ref[0, rows, block * 128 : (block + 1) * 128] = piece
            elif block < 8:
                out_ref[0, rows, (block - 6) * 128 : (block - 5) * 128] = piece
            elif block < 16:
                up_ref[0, rows, (block - 8) * 128 : (block - 7) * 128] = piece
            else:
                j, side = divmod(block - 16, 2)
                down_ref[0, j * 256 + i * WIN : j * 256 + (i + 1) * WIN, side * 128 : (side + 1) * 128] = piece
    lines = []
    for c in range(7):
        pair = in_ref[c, CHUNK:CHUNK_PAD, :].astype(F32)
        lines.append(pair[0:1] + pair[1:2])
    for ref, c in ((gain_one_ref, 0), (gain_two_ref, 2), (sdf_ref, 4)):
        ref[0:1, 0:128] = lines[c]
        ref[0:1, 128:256] = lines[c + 1]
    loss_ref[0:1, :] = lines[6] / (2 * 12288)


def swap_pipe(value):
    return lax.ppermute(value, "pipe", [(0, 1), (1, 0)])


VMEM = pl.BlockSpec(memory_space=pltpu.VMEM)
SMEM = pl.BlockSpec(memory_space=pltpu.SMEM)
ANY = pl.BlockSpec(memory_space=pl.ANY)


def shards(
    features, coarse, parent, counts, target, gain_attn, w_qkv, w_out, gain_mlp, w_up, w_down, w_sdf
):
    rank_count = lax.axis_size("tok")
    rim = lax.ppermute(coarse[:, -1:, :], "tok", [(i, i + 1) for i in range(rank_count - 1)])
    gains = jnp.concatenate([gain_attn, gain_mlp], axis=0)
    gains_far = swap_pipe(gains)
    qkv_far, out_far, up_far, down_far = (swap_pipe(w) for w in (w_qkv, w_out, w_up, w_down))
    outgoing = pl.pallas_call(
        embed_kernel,
        out_shape=jax.ShapeDtypeStruct((GROUP, SEND_ROWS, WIDTH), BF),
        in_specs=[VMEM] * 5,
        out_specs=VMEM,
        name="embed",
    )(features, coarse, rim, parent, target)
    groups = [[b * GROUP + i for i in range(GROUP)] for b in range(rank_count // GROUP)]
    received = lax.all_to_all(outgoing, "tok", 0, 0, axis_index_groups=groups, tiled=True)
    packet = jax.ShapeDtypeStruct((64, CHUNK_PAD, 128), BF)
    keep, send = pl.pallas_call(
        step_kernel,
        out_shape=(packet, packet),
        in_specs=[SMEM] + [VMEM] * 4 + [ANY] * 8,
        out_specs=(ANY, ANY),
        scratch_shapes=[
            pltpu.VMEM((2, WIDTH, 3 * WIDTH), BF),
            pltpu.VMEM((2, WIDTH, WIDTH), BF),
            pltpu.VMEM((2, WIDTH, FF), BF),
            pltpu.VMEM((2, FF, WIDTH), BF),
            pltpu.VMEM((2, ROWS, WIDTH), BF),
            pltpu.VMEM((2, ROWS, 1), F32),
            pltpu.VMEM((2, ROWS, WIDTH), BF),
            pltpu.VMEM((2, 3, ROWS, WIDTH), BF),
            pltpu.VMEM((2, ROWS, WIDTH), F32),
            pltpu.VMEM((2, ROWS, WIDTH), BF),
            pltpu.VMEM((2, ROWS, WIDTH), F32),
            pltpu.VMEM((2, ROWS, 1), F32),
            pltpu.VMEM((2, ROWS, WIDTH), BF),
            pltpu.VMEM((2, 4, ROWS, WIDTH), F32),
            pltpu.VMEM((2, 4, ROWS, WIDTH), BF),
            pltpu.VMEM((ROWS, WIDTH), BF),
            pltpu.VMEM((2, GROUP, WIDTH), F32),
            pltpu.VMEM((2, 64, CHUNK_PAD, 128), BF),
            pltpu.VMEM((ROWS, WIDTH), F32),
            pltpu.VMEM((3, ROWS, WIDTH), BF),
            pltpu.SemaphoreType.DMA((8,)),
            pltpu.SemaphoreType.DMA((2,)),
        ],
        name="step",
    )(counts, received, w_sdf[None], gains, gains_far, w_qkv, qkv_far, w_out, out_far, w_up, up_far, w_down, down_far)
    far = swap_pipe(send)
    total = pl.pallas_call(
        add_kernel, out_shape=packet, in_specs=[VMEM] * 2, out_specs=VMEM, name="add"
    )(keep, far)
    shares = lax.all_to_all(total, "tok", 0, 0, tiled=True)
    summed = pl.pallas_call(
        sum_kernel, out_shape=packet, in_specs=[VMEM], out_specs=VMEM, name="sum"
    )(shares)
    gathered = lax.all_to_all(summed, "tok", 0, 0, tiled=True)
    loss, sdf, gain_one, qkv, out, gain_two, up, down = pl.pallas_call(
        unpack_kernel,
        out_shape=(
            jax.ShapeDtypeStruct((1, 128), F32),
            jax.ShapeDtypeStruct((1, WIDTH), F32),
            jax.ShapeDtypeStruct((1, WIDTH), F32),
            jax.ShapeDtypeStruct((1, WIDTH, 3 * WIDTH), F32),
            jax.ShapeDtypeStruct((1, WIDTH, WIDTH), F32),
            jax.ShapeDtypeStruct((1, WIDTH), F32),
            jax.ShapeDtypeStruct((1, WIDTH, FF), F32),
            jax.ShapeDtypeStruct((1, FF, WIDTH), F32),
        ),
        in_specs=[VMEM],
        out_specs=(VMEM,) * 8,
        name="unpack",
    )(gathered)
    return loss[0, 0], sdf[0], gain_one, qkv, out, gain_two, up, down


def solution(mesh):
    return jax.shard_map(
        shards,
        mesh=mesh,
        in_specs=(
            P(None, "tok", None),
            P(None, "tok", None),
            P(None, "tok"),
            P(),
            P(None, "tok"),
            P("pipe", None),
            P("pipe", None, None),
            P("pipe", None, None),
            P("pipe", None),
            P("pipe", None, None),
            P("pipe", None, None),
            P(),
        ),
        out_specs=(
            P(),
            P(),
            P("pipe", None),
            P("pipe", None, None),
            P("pipe", None, None),
            P("pipe", None),
            P("pipe", None, None),
            P("pipe", None, None),
        ),
        check_vma=False,
    )
```

```python
import functools
import math

import jax
import jax.numpy as jnp
from jax import lax
from jax.experimental import pallas as pl
from jax.experimental.pallas import tpu as pltpu
from jax.sharding import PartitionSpec as P

H = 8
WIN = 32
GROUP = 8
ROWS = 256
WIDTH = 256
FF = 1024
HEAD = WIDTH // H
EPS = 1e-06
CHUNK = 96
CHUNK_PAD = 104
SEND_ROWS = 40
BF = jnp.bfloat16
F32 = jnp.float32


def nn(a, b):
    return jnp.dot(a, b, preferred_element_type=F32)


def nt(a, b):
    return lax.dot_general(a, b, (((1,), (1,)), ((), ())), preferred_element_type=F32)


def tn(a, b):
    return lax.dot_general(a, b, (((0,), (0,)), ((), ())), preferred_element_type=F32)


def iota(shape, dim):
    return lax.broadcasted_iota(jnp.int32, shape, dim)


def split_two(value):
    high = value.astype(BF)
    low = (value - high.astype(F32)).astype(BF)
    return high, low


def embed_kernel(
    features_hbm, coarse_hbm, rim_ref, parent_hbm, target_hbm, out_ref,
    features_ref, coarse_ref, parent_ref, target_ref, load_sem,
):
    micro = lax.axis_index("pipe")
    shard = lax.axis_index("tok")
    loads = [
        pltpu.make_async_copy(source, held, load_sem.at[number])
        for number, (source, held) in enumerate(
            (
                (features_hbm.at[micro], features_ref),
                (coarse_hbm.at[micro], coarse_ref),
                (parent_hbm, parent_ref),
                (target_hbm, target_ref),
            )
        )
    ]
    for load in loads:
        load.start()
    for load in loads:
        load.wait()
    local = parent_ref[pl.ds(micro, 1), :] - shard * 64
    own_hot = jnp.where(iota((64, ROWS), 0) == local, 1.0, 0.0).astype(BF)
    rim_hot = jnp.where((iota((16, ROWS), 0) == 0) & (local == -1), 1.0, 0.0).astype(BF)
    rim = jnp.broadcast_to(rim_ref[micro], (16, WIDTH))
    lifted = tn(own_hot, coarse_ref[...]) + tn(rim_hot, rim)
    embedded = (features_ref[...].astype(F32) + lifted).astype(BF)
    target = jnp.broadcast_to(target_ref[pl.ds(micro, 1), :], (8, ROWS))
    high = target.astype(BF).astype(F32)
    middle = (target - high).astype(BF).astype(F32)
    low = target - high - middle
    row = iota((8, ROWS), 0)
    extra = jnp.where(row == 0, high, jnp.where(row == 1, middle, jnp.where(row == 2, low, 0.0)))
    extra = extra.astype(BF)
    for part in range(GROUP):
        out_ref[part, 0:WIN, :] = embedded[part * WIN : (part + 1) * WIN]
        out_ref[part, WIN:SEND_ROWS, :] = extra


def group_max(values):
    lane = iota(values.shape, 1)
    for step in (1, 2, 4, 8, 16):
        ahead = pltpu.roll(values, values.shape[1] - step, 1)
        behind = pltpu.roll(values, step, 1)
        values = jnp.maximum(values, jnp.where((lane & step) == 0, ahead, behind))
    return values


def group_sum(values, same_head):
    high, low = split_two(values)
    return nn(high, same_head) + nn(low, same_head)


def step_kernel(
    counts_hbm, received_ref, gain_far_one, gain_far_two, sdf_hbm, gain_own_one_hbm, gain_own_two_hbm,
    qkv_own, qkv_far, out_own, out_far, up_own, up_far, down_own, down_far,
    keep_ref, send_ref,
    w_qkv, w_out, w_up, w_down,
    x_buf, inv_one, normed_buf, packed_buf, prob_buf, mixed_buf, after_buf, inv_two,
    normed_two_buf, slope_buf, hidden_buf, mask_buf, grads, score_buf, dpacked_buf,
    sdf_ref, gain_own_one, gain_own_two, counts_ref, load_sem, store_sem,
):
    micro = lax.axis_index("pipe")
    shard = lax.axis_index("tok")
    part = lax.rem(shard, GROUP)
    first = shard - part
    loads = []
    for number, (own, far, held) in enumerate(
        ((qkv_own, qkv_far, w_qkv), (out_own, out_far, w_out), (up_own, up_far, w_up), (down_own, down_far, w_down))
    ):
        loads.append(pltpu.make_async_copy(own.at[0], held.at[micro], load_sem.at[2 * number]))
        loads.append(pltpu.make_async_copy(far.at[0], held.at[1 - micro], load_sem.at[2 * number + 1]))
    small = [
        pltpu.make_async_copy(source, held, load_sem.at[8 + number])
        for number, (source, held) in enumerate(
            (
                (sdf_hbm, sdf_ref),
                (gain_own_one_hbm, gain_own_one),
                (gain_own_two_hbm, gain_own_two),
                (counts_hbm, counts_ref),
            )
        )
    ]
    for load in small + loads:
        load.start()
    for load in small:
        load.wait()

    own_is_first = micro == 0

    def gain(section, which):
        own = (gain_own_one, gain_own_two)[which][...]
        far = (gain_far_one, gain_far_two)[which][...]
        mine = own_is_first if section == 0 else jnp.logical_not(own_is_first)
        return jnp.where(mine, own, far)

    row_i = iota((ROWS, WIDTH), 0)
    col_i = iota((ROWS, WIDTH), 1)
    same_head = jnp.where(row_i // WIN == col_i // HEAD, 1.0, 0.0).astype(BF)
    swapped = row_i % WIN // 4 * WIN + row_i // WIN * 4 + row_i % 4
    swap = jnp.where(swapped == col_i, 1.0, 0.0).astype(BF)

    def exchange(value):
        return nn(swap, value).astype(BF)

    lane = iota((1, WIDTH), 1)
    key = lane % WIN
    count_of = [counts_ref[micro, first + s] for s in range(GROUP)]
    lane_count = jnp.zeros((1, WIDTH), jnp.int32)
    for s in range(GROUP):
        lane_count = jnp.where(key // 4 == s, count_of[s], lane_count)
    for w in range(GROUP):
        dilated = part * WIN + w * 4 + key % 4 < lane_count
        plain = part * WIN + key < count_of[w]
        mask_buf[0, w : w + 1, :] = jnp.where(dilated, 1.0, 0.0)
        mask_buf[1, w : w + 1, :] = jnp.where(plain, 1.0, 0.0)

    def expand(value):
        return jnp.concatenate([value] * H, axis=0) * same_head

    def window(value, w):
        return value[w * WIN : (w + 1) * WIN]

    def store_grad(section, block, value):
        for i in range(GROUP):
            slab = block * GROUP + i
            base = slab % 3 * WIN
            grads[section, slab // 3, base : base + WIN, :] = window(value, i).astype(BF)

    def store_wide(section, block, value):
        store_grad(section, block, value[:, :128])
        store_grad(section, block + 1, value[:, 128:])

    def forward(k):
        x = x_buf[k].astype(F32)
        inv = lax.rsqrt(jnp.mean(x * x, axis=-1, keepdims=True) + EPS)
        inv_one[k] = inv
        normed = (x * inv * gain(k, 0)).astype(BF)
        normed_buf[k] = normed
        if k == 0:
            loads[0].wait()
            loads[1].wait()
        for j in range(3):
            packed_buf[k, j] = nn(normed, w_qkv[k, :, j * WIDTH : (j + 1) * WIDTH]).astype(BF)
        for w in range(GROUP):
            rows = slice(w * WIN, (w + 1) * WIN)
            scores = nt(packed_buf[k, 0, rows, :], expand(packed_buf[k, 1, rows, :]))
            score_buf[rows, :] = jnp.where(mask_buf[k, w : w + 1, :] > 0.5, scores * HEAD**-0.5, -1e30)
        scores = score_buf[...]
        weights = jnp.exp(scores - group_max(scores))
        prob = weights / group_sum(weights, same_head)
        prob_buf[k] = prob
        prob_low = prob.astype(BF)
        for w in range(GROUP):
            rows = slice(w * WIN, (w + 1) * WIN)
            mixed_buf[k, rows, :] = nn(window(prob_low, w), expand(packed_buf[k, 2, rows, :])).astype(BF)
        if k == 0:
            loads[2].wait()
            loads[3].wait()
        after = x + nn(mixed_buf[k], w_out[k])
        after_buf[k] = after
        inv = lax.rsqrt(jnp.mean(after * after, axis=-1, keepdims=True) + EPS)
        inv_two[k] = inv
        normed_two = (after * inv * gain(k, 1)).astype(BF)
        normed_two_buf[k] = normed_two
        if k == 0:
            for load in loads[4:]:
                load.wait()
        total = after
        for j in range(4):
            cols = slice(j * WIDTH, (j + 1) * WIDTH)
            up = nn(normed_two, w_up[k, :, cols])
            root = math.sqrt(2.0 / math.pi)
            square = up * up
            bent = jnp.tanh(root * (up + 0.044715 * (square * up)))
            half = 0.5 * (1.0 + bent)
            hidden = (up * half).astype(BF)
            hidden_buf[k, j] = hidden
            slope_buf[k, j] = half + (0.5 * root) * up * (1.0 - bent * bent) * (1.0 + (3 * 0.044715) * square)
            total = total + nn(hidden, w_down[k, cols, :])
        return total.astype(BF)

    def norm_back(grad, value, inv, gain_row):
        gain_grad = jnp.sum(grad * value * inv, axis=0, keepdims=True)
        scaled = grad * gain_row
        inner = jnp.mean(scaled * value, axis=-1, keepdims=True)
        return inv * (scaled - value * (inv * inv * inner)), gain_grad

    def backward(k, out_grad):
        back = None
        for j in range(4):
            cols = slice(j * WIDTH, (j + 1) * WIDTH)
            store_wide(k, 16 + 2 * j, tn(hidden_buf[k, j], out_grad))
            hidden_grad = nt(out_grad, w_down[k, cols, :]).astype(BF)
            up_grad = (slope_buf[k, j] * hidden_grad.astype(F32)).astype(BF)
            store_wide(k, 8 + 2 * j, tn(normed_two_buf[k], up_grad))
            term = nt(up_grad, w_up[k, :, cols])
            back = term if back is None else back + term
        normed_two_grad = back.astype(BF).astype(F32)
        res_grad, gain_two_grad = norm_back(normed_two_grad, after_buf[k], inv_two[k], gain(k, 1))
        after_grad = out_grad.astype(F32) + res_grad
        after_low = after_grad.astype(BF)
        store_wide(k, 6, tn(mixed_buf[k], after_low))
        mixed_grad = nt(after_low, w_out[k]).astype(BF)
        for w in range(GROUP):
            rows = slice(w * WIN, (w + 1) * WIN)
            score_buf[rows, :] = nt(window(mixed_grad, w), expand(packed_buf[k, 2, rows, :]))
        prob = prob_buf[k]
        prob_low = prob.astype(BF)
        prob_grad = score_buf[...].astype(BF).astype(F32)
        flow = prob * prob_grad
        score_grad = ((flow - prob * group_sum(flow, same_head)) * HEAD**-0.5).astype(BF)

        def fold(value):
            total = None
            for h in range(H):
                piece = jnp.where(col_i[:WIN] // HEAD == h, window(value, h), 0.0)
                total = piece if total is None else total + piece
            return total

        for w in range(GROUP):
            rows = slice(w * WIN, (w + 1) * WIN)
            grad_w = window(score_grad, w)
            dpacked_buf[0, rows, :] = nn(grad_w, expand(packed_buf[k, 1, rows, :])).astype(BF)
            dpacked_buf[1, rows, :] = fold(tn(grad_w, packed_buf[k, 0, rows, :])).astype(BF)
            dpacked_buf[2, rows, :] = fold(tn(window(prob_low, w), window(mixed_grad, w))).astype(BF)
        back = None
        for j in range(3):
            piece = dpacked_buf[j]
            store_wide(k, 2 * j, tn(normed_buf[k], piece))
            term = nt(piece, w_qkv[k, :, j * WIDTH : (j + 1) * WIDTH])
            back = term if back is None else back + term
        normed_grad = back.astype(BF).astype(F32)
        in_res, gain_one_grad = norm_back(normed_grad, x_buf[k].astype(F32), inv_one[k], gain(k, 0))
        return (after_grad + in_res).astype(BF), gain_one_grad, gain_two_grad

    received = received_ref[:, 0:WIN, :].reshape(ROWS, WIDTH)
    x_buf[0] = exchange(received)
    x_buf[1] = exchange(forward(0))
    section_one = forward(1).astype(F32)

    pieces = []
    lane_w = iota((WIN, WIDTH), 1)
    row_w = iota((WIN, WIDTH), 0)
    valid_pieces = []
    for s in range(GROUP):
        parts = received_ref[s, WIN : WIN + 8, :].astype(F32)
        line = parts[0:1] + parts[1:2] + parts[2:3]
        chosen = jnp.where(lane_w == part * WIN + row_w, line, 0.0)
        pieces.append(jnp.sum(chosen, axis=-1, keepdims=True))
        valid_pieces.append(part * WIN + iota((WIN, 1), 0) < count_of[s])
    target = jnp.concatenate(pieces, axis=0)
    valid = jnp.concatenate([jnp.where(v, 1.0, 0.0) for v in valid_pieces], axis=0)
    sdf = sdf_ref[...]
    predicted = jnp.sum(section_one * sdf, axis=-1, keepdims=True)
    residue = jnp.where(valid > 0.5, predicted - target, 0.0)
    slope = 2.0 * residue / math.sqrt(3 * ROWS * 64 // 4)
    loss = jnp.sum(residue * residue, axis=0, keepdims=True)
    sdf_grad = jnp.sum(slope * section_one, axis=0, keepdims=True)
    head_grad = (slope * sdf).astype(BF)
    middle_grad, one_one, one_two = backward(1, head_grad)
    unused, zero_one, zero_two = backward(0, exchange(middle_grad))
    del unused
    loss_row = jnp.broadcast_to(loss, (1, 128))
    stat_row = iota((8, 128), 0)
    for k, (gain_one, gain_two) in enumerate(((zero_one, zero_two), (one_one, one_two))):
        lines = []
        for line in (gain_one, gain_two, sdf_grad):
            lines += [line[:, :128], line[:, 128:]]
        lines.append(loss_row)
        grads[k, :, CHUNK:CHUNK_PAD, :] = jnp.zeros((64, CHUNK_PAD - CHUNK, 128), BF)
        for c, line in enumerate(lines):
            high, low = split_two(line)
            both = jnp.where(
                stat_row == 2 * micro, high.astype(F32), jnp.where(stat_row == 2 * micro + 1, low.astype(F32), 0.0)
            )
            grads[k, c, CHUNK:CHUNK_PAD, :] = both.astype(BF)
    stores = [
        pltpu.make_async_copy(grads.at[micro], keep_ref, store_sem.at[0]),
        pltpu.make_async_copy(grads.at[1 - micro], send_ref, store_sem.at[1]),
    ]
    for store in stores:
        store.start()
    for store in stores:
        store.wait()


def unpack_kernel(
    in_ref, loss_ref, sdf_ref, gain_one_ref, qkv_hbm, out_hbm, gain_two_ref, up_hbm, down_hbm,
    qkv_ref, out_ref, up_ref, down_ref, store_sem,
):
    stores = []

    def store(source, target):
        copy = pltpu.make_async_copy(source, target, store_sem.at[len(stores)])
        copy.start()
        stores.append(copy)

    for block in range(24):
        for i in range(GROUP):
            slab = block * GROUP + i
            base = slab % 3 * WIN
            piece = in_ref[slab // 3, base : base + WIN, :].astype(F32)
            rows = slice(i * WIN, (i + 1) * WIN)
            if block < 6:
                qkv_ref[rows, block * 128 : (block + 1) * 128] = piece
            elif block < 8:
                out_ref[rows, (block - 6) * 128 : (block - 5) * 128] = piece
            elif block < 16:
                up_ref[rows, (block - 8) * 128 : (block - 7) * 128] = piece
            else:
                j, side = divmod(block - 16, 2)
                down_ref[j * 256 + i * WIN : j * 256 + (i + 1) * WIN, side * 128 : (side + 1) * 128] = piece
        if block == 5:
            store(qkv_ref, qkv_hbm.at[0])
        elif block == 7:
            store(out_ref, out_hbm.at[0])
        elif block == 15:
            store(up_ref, up_hbm.at[0])
        elif block > 15 and block % 2 == 1:
            rows = slice((block - 17) // 2 * 256, (block - 15) // 2 * 256)
            store(down_ref.at[rows], down_hbm.at[0, rows])
    lines = []
    for c in range(7):
        pair = in_ref[c, CHUNK:CHUNK_PAD, :].astype(F32)
        lines.append(pair[0:1] + pair[1:2])
    for ref, c in ((gain_one_ref, 0), (gain_two_ref, 2), (sdf_ref, 4)):
        ref[0:1, 0:128] = lines[c]
        ref[0:1, 128:256] = lines[c + 1]
    loss_ref[0:1, :] = lines[6] / (2 * 12288)
    for copy in stores:
        copy.wait()


def fix(value):
    return pltpu.with_memory_space_constraint(value, pltpu.HBM)


def swap_pipe(value):
    return lax.ppermute(value, "pipe", [(0, 1), (1, 0)])


VMEM = pl.BlockSpec(memory_space=pltpu.VMEM)
ANY = pl.BlockSpec(memory_space=pl.ANY)
HBM = pl.BlockSpec(memory_space=pltpu.HBM)


def shards(
    features, coarse, parent, counts, target, gain_attn, w_qkv, w_out, gain_mlp, w_up, w_down, w_sdf
):
    rank_count = lax.axis_size("tok")
    rim = lax.ppermute(coarse[:, -1:, :], "tok", [(i, i + 1) for i in range(rank_count - 1)])
    gains_far = [swap_pipe(g) for g in (gain_attn, gain_mlp)]
    qkv_far, out_far, up_far, down_far = (swap_pipe(w) for w in (w_qkv, w_out, w_up, w_down))
    outgoing = pl.pallas_call(
        embed_kernel,
        out_shape=jax.ShapeDtypeStruct((GROUP, SEND_ROWS, WIDTH), BF),
        in_specs=[HBM, HBM, VMEM, HBM, HBM],
        out_specs=VMEM,
        scratch_shapes=[
            pltpu.VMEM((ROWS, WIDTH), BF),
            pltpu.VMEM((64, WIDTH), BF),
            pltpu.VMEM((2, ROWS), jnp.int32),
            pltpu.VMEM((2, ROWS), F32),
            pltpu.SemaphoreType.DMA((4,)),
        ],
        name="embed",
        compiler_params=pltpu.CompilerParams(vmem_limit_bytes=4 * 2**20),
    )(fix(features), fix(coarse), rim, fix(parent), fix(target))
    groups = [[b * GROUP + i for i in range(GROUP)] for b in range(rank_count // GROUP)]
    received = lax.all_to_all(outgoing, "tok", 0, 0, axis_index_groups=groups, tiled=True)
    packet = jax.ShapeDtypeStruct((64, CHUNK_PAD, 128), BF)
    keep, send = pl.pallas_call(
        step_kernel,
        out_shape=(packet, packet),
        in_specs=[HBM] + [VMEM] * 3 + [HBM] * 3 + [HBM, ANY] * 4,
        out_specs=(ANY, ANY),
        scratch_shapes=[
            pltpu.VMEM((2, WIDTH, 3 * WIDTH), BF),
            pltpu.VMEM((2, WIDTH, WIDTH), BF),
            pltpu.VMEM((2, WIDTH, FF), BF),
            pltpu.VMEM((2, FF, WIDTH), BF),
            pltpu.VMEM((2, ROWS, WIDTH), BF),
            pltpu.VMEM((2, ROWS, 1), F32),
            pltpu.VMEM((2, ROWS, WIDTH), BF),
            pltpu.VMEM((2, 3, ROWS, WIDTH), BF),
            pltpu.VMEM((2, ROWS, WIDTH), F32),
            pltpu.VMEM((2, ROWS, WIDTH), BF),
            pltpu.VMEM((2, ROWS, WIDTH), F32),
            pltpu.VMEM((2, ROWS, 1), F32),
            pltpu.VMEM((2, ROWS, WIDTH), BF),
            pltpu.VMEM((2, 4, ROWS, WIDTH), F32),
            pltpu.VMEM((2, 4, ROWS, WIDTH), BF),
            pltpu.VMEM((2, GROUP, WIDTH), F32),
            pltpu.VMEM((2, 64, CHUNK_PAD, 128), BF),
            pltpu.VMEM((ROWS, WIDTH), F32),
            pltpu.VMEM((3, ROWS, WIDTH), BF),
            pltpu.VMEM((1, WIDTH), F32),
            pltpu.VMEM((1, WIDTH), F32),
            pltpu.VMEM((1, WIDTH), F32),
            pltpu.SMEM((2, 64), jnp.int32),
            pltpu.SemaphoreType.DMA((12,)),
            pltpu.SemaphoreType.DMA((2,)),
        ],
        name="step",
        compiler_params=pltpu.CompilerParams(vmem_limit_bytes=32 * 2**20),
    )(fix(counts), received, *gains_far, fix(w_sdf[None]), fix(gain_attn), fix(gain_mlp), fix(w_qkv), qkv_far, fix(w_out), out_far, fix(w_up), up_far, fix(w_down), down_far)
    far = swap_pipe(send)
    total = (keep.astype(F32) + far.astype(F32)).astype(BF)
    shares = lax.all_to_all(total, "tok", 0, 0, tiled=True)
    summed = jnp.sum(shares.astype(F32), axis=0)
    stat = jnp.sum(summed[CHUNK : CHUNK + 4], axis=0, keepdims=True)
    high = lax.reduce_precision(stat, 8, 7)
    row = iota((CHUNK_PAD, 128), 0)
    tail = jnp.where(row == CHUNK, high, jnp.where(row == CHUNK + 1, stat - high, 0.0))
    summed = jnp.where(row < CHUNK, summed, tail).astype(BF)
    gathered = lax.all_to_all(
        jnp.broadcast_to(summed[None], (rank_count, CHUNK_PAD, 128)), "tok", 0, 0, tiled=True
    )
    loss, sdf, gain_one, qkv, out, gain_two, up, down = pl.pallas_call(
        unpack_kernel,
        out_shape=(
            jax.ShapeDtypeStruct((1, 128), F32),
            jax.ShapeDtypeStruct((1, WIDTH), F32),
            jax.ShapeDtypeStruct((1, WIDTH), F32),
            jax.ShapeDtypeStruct((1, WIDTH, 3 * WIDTH), F32),
            jax.ShapeDtypeStruct((1, WIDTH, WIDTH), F32),
            jax.ShapeDtypeStruct((1, WIDTH), F32),
            jax.ShapeDtypeStruct((1, WIDTH, FF), F32),
            jax.ShapeDtypeStruct((1, FF, WIDTH), F32),
        ),
        in_specs=[VMEM],
        out_specs=(VMEM, VMEM, VMEM, HBM, HBM, VMEM, HBM, HBM),
        scratch_shapes=[
            pltpu.VMEM((WIDTH, 3 * WIDTH), F32),
            pltpu.VMEM((WIDTH, WIDTH), F32),
            pltpu.VMEM((WIDTH, FF), F32),
            pltpu.VMEM((FF, WIDTH), F32),
            pltpu.SemaphoreType.DMA((7,)),
        ],
        name="unpack",
        compiler_params=pltpu.CompilerParams(vmem_limit_bytes=16 * 2**20),
    )(gathered)
    return loss[0, 0], sdf[0], gain_one, qkv, out, gain_two, up, down


def solution(mesh):
    return jax.shard_map(
        shards,
        mesh=mesh,
        in_specs=(
            P(None, "tok", None),
            P(None, "tok", None),
            P(None, "tok"),
            P(),
            P(None, "tok"),
            P("pipe", None),
            P("pipe", None, None),
            P("pipe", None, None),
            P("pipe", None),
            P("pipe", None, None),
            P("pipe", None, None),
            P(),
        ),
        out_specs=(
            P(),
            P(),
            P("pipe", None),
            P("pipe", None, None),
            P("pipe", None, None),
            P("pipe", None),
            P("pipe", None, None),
            P("pipe", None, None),
        ),
        check_vma=False,
    )
```

```python
import functools
import math

import jax
import jax.numpy as jnp
from jax import lax
from jax.experimental import pallas as pl
from jax.experimental.pallas import tpu as pltpu
from jax.sharding import PartitionSpec as P

H = 8
WIN = 32
GROUP = 8
ROWS = 256
WIDTH = 256
FF = 1024
HEAD = WIDTH // H
EPS = 1e-06
CHUNK = 80
CHUNK_PAD = 88
SLAB = 16
STAT_AT = 49
SEND_ROWS = 40
BF = jnp.bfloat16
F32 = jnp.float32


def nn(a, b):
    return jnp.dot(a, b, preferred_element_type=F32)


def nt(a, b):
    return lax.dot_general(a, b, (((1,), (1,)), ((), ())), preferred_element_type=F32)


def tn(a, b):
    return lax.dot_general(a, b, (((0,), (0,)), ((), ())), preferred_element_type=F32)


def iota(shape, dim):
    return lax.broadcasted_iota(jnp.int32, shape, dim)


def split_two(value):
    high = value.astype(BF)
    low = (value - high.astype(F32)).astype(BF)
    return high, low


def embed_kernel(
    features_hbm, coarse_hbm, rim_ref, parent_hbm, target_hbm, out_ref,
    features_ref, coarse_ref, parent_ref, target_ref, load_sem,
):
    micro = lax.axis_index("pipe")
    shard = lax.axis_index("tok")
    loads = [
        pltpu.make_async_copy(source, held, load_sem.at[number])
        for number, (source, held) in enumerate(
            (
                (features_hbm.at[micro], features_ref),
                (coarse_hbm.at[micro], coarse_ref),
                (parent_hbm, parent_ref),
                (target_hbm, target_ref),
            )
        )
    ]
    for load in loads:
        load.start()
    for load in loads:
        load.wait()
    local = parent_ref[pl.ds(micro, 1), :] - shard * 64
    own_hot = jnp.where(iota((64, ROWS), 0) == local, 1.0, 0.0).astype(BF)
    rim_hot = jnp.where((iota((16, ROWS), 0) == 0) & (local == -1), 1.0, 0.0).astype(BF)
    rim = jnp.broadcast_to(rim_ref[micro], (16, WIDTH))
    lifted = tn(own_hot, coarse_ref[...]) + tn(rim_hot, rim)
    embedded = (features_ref[...].astype(F32) + lifted).astype(BF)
    target = jnp.broadcast_to(target_ref[pl.ds(micro, 1), :], (8, ROWS))
    high = target.astype(BF).astype(F32)
    middle = (target - high).astype(BF).astype(F32)
    low = target - high - middle
    row = iota((8, ROWS), 0)
    extra = jnp.where(row == 0, high, jnp.where(row == 1, middle, jnp.where(row == 2, low, 0.0)))
    extra = extra.astype(BF)
    for part in range(GROUP):
        out_ref[part, 0:WIN, :] = embedded[part * WIN : (part + 1) * WIN]
        out_ref[part, WIN:SEND_ROWS, :] = extra


def group_max(values):
    halves = []
    for side in range(2):
        half = values[:, side * 128 : (side + 1) * 128]
        lane = iota((1, 128), 1)
        for step in (1, 2, 4, 8, 16):
            ahead = pltpu.roll(half, 128 - step, 1)
            behind = pltpu.roll(half, step, 1)
            half = jnp.maximum(half, jnp.where((lane & step) == 0, ahead, behind))
        halves.append(half)
    return jnp.concatenate(halves, axis=1)


def group_sum(values, same_head):
    high, low = split_two(values)
    return nn(high, same_head) + nn(low, same_head)


def step_kernel(
    counts_hbm, received_ref, gain_far_one, gain_far_two, sdf_hbm, gain_own_one_hbm, gain_own_two_hbm,
    qkv_own, qkv_far, out_own, out_far, up_own, up_far, down_own, down_far,
    keep_ref, send_ref,
    w_qkv, w_out, w_up, w_down,
    x_buf, inv_one, normed_buf, packed_buf, prob_buf, mixed_buf, after_buf, inv_two,
    normed_two_buf, slope_buf, hidden_buf, mask_buf, grads, score_buf, dpacked_buf,
    sdf_ref, gain_own_one, gain_own_two, counts_ref, load_sem, store_sem,
):
    micro = lax.axis_index("pipe")
    shard = lax.axis_index("tok")
    part = lax.rem(shard, GROUP)
    first = shard - part
    loads = []
    for number, (own, far, held) in enumerate(
        ((qkv_own, qkv_far, w_qkv), (out_own, out_far, w_out), (up_own, up_far, w_up), (down_own, down_far, w_down))
    ):
        loads.append(pltpu.make_async_copy(own.at[0], held.at[micro], load_sem.at[2 * number]))
        loads.append(pltpu.make_async_copy(far.at[0], held.at[1 - micro], load_sem.at[2 * number + 1]))
    small = [
        pltpu.make_async_copy(source, held, load_sem.at[8 + number])
        for number, (source, held) in enumerate(
            (
                (sdf_hbm, sdf_ref),
                (gain_own_one_hbm, gain_own_one),
                (gain_own_two_hbm, gain_own_two),
                (counts_hbm, counts_ref),
            )
        )
    ]
    for load in small + loads:
        load.start()
    for load in small:
        load.wait()

    own_is_first = micro == 0

    def gain(section, which):
        own = (gain_own_one, gain_own_two)[which][...]
        far = (gain_far_one, gain_far_two)[which][...]
        mine = own_is_first if section == 0 else jnp.logical_not(own_is_first)
        return jnp.where(mine, own, far)

    row_i = iota((ROWS, WIDTH), 0)
    col_i = iota((ROWS, WIDTH), 1)
    same_head = jnp.where(row_i // WIN == col_i // HEAD, 1.0, 0.0).astype(BF)
    swapped = row_i % WIN // 4 * WIN + row_i // WIN * 4 + row_i % 4
    swap = jnp.where(swapped == col_i, 1.0, 0.0).astype(BF)

    def exchange(value):
        return nn(swap, value).astype(BF)

    lane = iota((1, WIDTH), 1)
    key = lane % WIN
    count_of = [counts_ref[micro, first + s] for s in range(GROUP)]
    lane_count = jnp.zeros((1, WIDTH), jnp.int32)
    for s in range(GROUP):
        lane_count = jnp.where(key // 4 == s, count_of[s], lane_count)
    for w in range(GROUP):
        dilated = part * WIN + w * 4 + key % 4 < lane_count
        plain = part * WIN + key < count_of[w]
        mask_buf[0, w : w + 1, :] = jnp.where(dilated, 1.0, 0.0)
        mask_buf[1, w : w + 1, :] = jnp.where(plain, 1.0, 0.0)

    def expand(value):
        return jnp.concatenate([value] * H, axis=0) * same_head

    def window(value, w):
        return value[w * WIN : (w + 1) * WIN]

    def store_grad(stream, place, value):
        for i in range(ROWS // SLAB):
            slab = place * (ROWS // SLAB) + i
            base = slab % 5 * SLAB
            grads[stream, slab // 5, base : base + SLAB, :] = value[i * SLAB : (i + 1) * SLAB].astype(BF)

    def store_wide(stream, place, value):
        store_grad(stream, place, value[:, :128])
        store_grad(stream, place + 1, value[:, 128:])

    stat_row = iota((8, 128), 0)
    for stream in range(2):
        grads[stream, :, CHUNK:CHUNK_PAD, :] = jnp.zeros((64, CHUNK_PAD - CHUNK, 128), BF)

    def store_stats(stream, lines):
        halves = []
        for line in lines:
            halves += [line[:, i : i + 128] for i in range(0, line.shape[1], 128)]
        for c, line in enumerate(halves):
            high, low = split_two(line)
            both = jnp.where(
                stat_row == 2 * micro, high.astype(F32), jnp.where(stat_row == 2 * micro + 1, low.astype(F32), 0.0)
            )
            grads[stream, STAT_AT + c, CHUNK:CHUNK_PAD, :] = both.astype(BF)

    stores = []

    def send_out(stream, first_chunk, last_chunk):
        number = len(stores)
        chunks = pl.ds(first_chunk, last_chunk - first_chunk)
        copies = [
            pltpu.make_async_copy(grads.at[stream, chunks], ref.at[chunks], store_sem.at[number])
            for ref in (keep_ref, send_ref)
        ]
        stores.append(copies[0])
        pl.when(micro == stream)(copies[0].start)
        pl.when(micro != stream)(copies[1].start)

    def forward(k):
        x = x_buf[k].astype(F32)
        inv = lax.rsqrt(jnp.mean(x * x, axis=-1, keepdims=True) + EPS)
        inv_one[k] = inv
        normed = (x * inv * gain(k, 0)).astype(BF)
        normed_buf[k] = normed
        if k == 0:
            loads[0].wait()
            loads[1].wait()
        for j in range(3):
            packed_buf[k, j] = nn(normed, w_qkv[k, :, j * WIDTH : (j + 1) * WIDTH]).astype(BF)
        for w in range(GROUP):
            rows = slice(w * WIN, (w + 1) * WIN)
            scores = nt(packed_buf[k, 0, rows, :], expand(packed_buf[k, 1, rows, :]))
            score_buf[rows, :] = jnp.where(mask_buf[k, w : w + 1, :] > 0.5, scores * HEAD**-0.5, -1e30)
        scores = score_buf[...]
        weights = jnp.exp(scores - group_max(scores))
        prob = weights / group_sum(weights, same_head)
        prob_buf[k] = prob
        prob_low = prob.astype(BF)
        for w in range(GROUP):
            rows = slice(w * WIN, (w + 1) * WIN)
            mixed_buf[k, rows, :] = nn(window(prob_low, w), expand(packed_buf[k, 2, rows, :])).astype(BF)
        if k == 0:
            loads[2].wait()
            loads[3].wait()
        after = x + nn(mixed_buf[k], w_out[k])
        after_buf[k] = after
        inv = lax.rsqrt(jnp.mean(after * after, axis=-1, keepdims=True) + EPS)
        inv_two[k] = inv
        normed_two = (after * inv * gain(k, 1)).astype(BF)
        normed_two_buf[k] = normed_two
        if k == 0:
            for load in loads[4:]:
                load.wait()
        total = after
        for j in range(4):
            cols = slice(j * WIDTH, (j + 1) * WIDTH)
            up = nn(normed_two, w_up[k, :, cols])
            root = math.sqrt(2.0 / math.pi)
            square = up * up
            half = 0.5 * jnp.tanh(up * (root + (root * 0.044715) * square)) + 0.5
            hidden = (up * half).astype(BF)
            hidden_buf[k, j] = hidden
            bend = up * (2 * root + (6 * root * 0.044715) * square)
            slope_buf[k, j] = half * (1.0 + bend * (1.0 - half))
            total = total + nn(hidden, w_down[k, cols, :])
        return total.astype(BF)

    def norm_back(grad, value, inv, gain_row):
        gain_grad = jnp.sum(grad * value * inv, axis=0, keepdims=True)
        scaled = grad * gain_row
        inner = jnp.mean(scaled * value, axis=-1, keepdims=True)
        return inv * (scaled - value * (inv * inv * inner)), gain_grad

    def backward(k, out_grad, slope, pulled):
        back = None
        down_lines = []
        places = {0: 6, 1: 10, 2: 0, 3: 2} if k == 0 else {0: 0, 1: 2, 2: 4, 3: 6}
        for j in (2, 3, 0, 1):
            cols = slice(j * WIDTH, (j + 1) * WIDTH)
            if k == 0:
                stream, place = (1, 12 + 2 * j) if j >= 2 else (0, 4 + 4 * j)
                out_low = out_grad.astype(BF)
                store_wide(stream, place, tn(hidden_buf[k, j], out_low))
                hidden_grad = nt(out_low, w_down[k, cols, :]).astype(BF).astype(F32)
            else:
                down_lines.append(jnp.sum(hidden_buf[k, j].astype(F32) * slope, axis=0, keepdims=True))
                hidden_grad = slope * pulled[j]
            up_grad = (slope_buf[k, j] * hidden_grad).astype(BF)
            store_wide(k, places[j], tn(normed_two_buf[k], up_grad))
            term = nt(up_grad, w_up[k, :, cols])
            back = term if back is None else back + term
            if k == 0 and j == 3:
                send_out(1, 51, 64)
        if k == 0:
            send_out(0, 0, 38)
        normed_two_grad = back.astype(BF).astype(F32)
        res_grad, gain_two_grad = norm_back(normed_two_grad, after_buf[k], inv_two[k], gain(k, 1))
        after_grad = out_grad + res_grad
        after_low = after_grad.astype(BF)
        store_wide(k, 12 if k == 0 else 8, tn(mixed_buf[k], after_low))
        mixed_grad = nt(after_low, w_out[k]).astype(BF)
        for w in range(GROUP):
            rows = slice(w * WIN, (w + 1) * WIN)
            score_buf[rows, :] = nt(window(mixed_grad, w), expand(packed_buf[k, 2, rows, :]))
        prob = prob_buf[k]
        prob_low = prob.astype(BF)
        prob_grad = score_buf[...].astype(BF).astype(F32)
        flow = prob * prob_grad
        score_grad = (flow - prob * group_sum(flow, same_head)) * HEAD**-0.5

        def fold(value):
            total = None
            for h in range(H):
                piece = jnp.where(col_i[:WIN] // HEAD == h, window(value, h), 0.0)
                total = piece if total is None else total + piece
            return total

        for w in range(GROUP):
            rows = slice(w * WIN, (w + 1) * WIN)
            grad_w = jnp.where(mask_buf[k, w : w + 1, :] > 0.5, window(score_grad, w), 0.0).astype(BF)
            dpacked_buf[0, rows, :] = nn(grad_w, expand(packed_buf[k, 1, rows, :])).astype(BF)
            dpacked_buf[1, rows, :] = fold(tn(grad_w, packed_buf[k, 0, rows, :])).astype(BF)
            dpacked_buf[2, rows, :] = fold(tn(window(prob_low, w), window(mixed_grad, w))).astype(BF)
        back = None
        for j in range(3):
            piece = dpacked_buf[j]
            store_wide(k, (14 if k == 0 else 10) + 2 * j, tn(normed_buf[k], piece))
            term = nt(piece, w_qkv[k, :, j * WIDTH : (j + 1) * WIDTH])
            back = term if back is None else back + term
        normed_grad = back.astype(BF).astype(F32)
        in_res, gain_one_grad = norm_back(normed_grad, x_buf[k].astype(F32), inv_one[k], gain(k, 0))
        return (after_grad + in_res).astype(BF), gain_one_grad, gain_two_grad, down_lines[2:] + down_lines[:2]

    received = received_ref[:, 0:WIN, :].reshape(ROWS, WIDTH)
    x_buf[0] = exchange(received)
    x_buf[1] = exchange(forward(0))
    section_one = forward(1).astype(F32)

    pieces = []
    lane_w = iota((WIN, WIDTH), 1)
    row_w = iota((WIN, WIDTH), 0)
    valid_pieces = []
    for s in range(GROUP):
        parts = received_ref[s, WIN : WIN + 8, :].astype(F32)
        line = parts[0:1] + parts[1:2] + parts[2:3]
        chosen = jnp.where(lane_w == part * WIN + row_w, line, 0.0)
        pieces.append(jnp.sum(chosen, axis=-1, keepdims=True))
        valid_pieces.append(part * WIN + iota((WIN, 1), 0) < count_of[s])
    target = jnp.concatenate(pieces, axis=0)
    valid = jnp.concatenate([jnp.where(v, 1.0, 0.0) for v in valid_pieces], axis=0)
    sdf = sdf_ref[...]
    predicted = jnp.sum(section_one * sdf, axis=-1, keepdims=True)
    residue = jnp.where(valid > 0.5, predicted - target, 0.0)
    slope = 2.0 * residue / math.sqrt(3 * ROWS * 64 // 4)
    loss = jnp.sum(residue * residue, axis=0, keepdims=True)
    sdf_grad = jnp.sum(slope * section_one, axis=0, keepdims=True)
    high = sdf.astype(BF).astype(F32)
    middle = (sdf - high).astype(BF).astype(F32)
    row = iota((16, WIDTH), 0)
    parts = jnp.where(row == 0, high, jnp.where(row == 1, middle, jnp.where(row == 2, sdf - high - middle, 0.0)))
    parts = parts.astype(BF)
    pulled = [
        jnp.sum(nt(parts, w_down[1, j * WIDTH : (j + 1) * WIDTH, :]), axis=0, keepdims=True) for j in range(4)
    ]
    loss_row = jnp.broadcast_to(loss, (1, 128))
    middle_grad, gain_one, gain_two, down_lines = backward(1, slope * sdf, slope, pulled)
    store_stats(1, [gain_one, gain_two, sdf_grad, loss_row] + down_lines)
    send_out(1, 0, 51)
    unused, gain_one, gain_two, none = backward(0, exchange(middle_grad).astype(F32), None, None)
    del unused, none
    store_stats(0, [gain_one, gain_two, sdf_grad, loss_row])
    send_out(0, 38, 64)
    for store in stores:
        store.wait()


def unpack_kernel(
    in_ref, moved_ref, sdf_row_ref, loss_ref, sdf_ref, gain_one_ref, qkv_hbm, out_hbm, gain_two_ref, up_hbm, down_hbm,
    qkv_ref, out_ref, up_ref, down_ref, store_sem,
):
    micro = lax.axis_index("pipe")
    stores = []

    def store(source, target):
        copy = pltpu.make_async_copy(source, target, store_sem.at[len(stores)])
        copy.start()
        stores.append(copy)

    def wide(source, first_chunk, place, target, base):
        for side in range(2):
            for i in range(ROWS // SLAB):
                slab = (place + side) * (ROWS // SLAB) + i
                low = slab % 5 * SLAB
                piece = source[slab // 5 - first_chunk, low : low + SLAB, :].astype(F32)
                target(i, side, piece, base)

    def into(ref, base):
        def put(i, side, piece, low):
            ref[low + i * SLAB : low + (i + 1) * SLAB, base + side * 128 : base + (side + 1) * 128] = piece

        return put

    def section(up_at, out_at, qkv_at):
        for j in range(4):
            wide(in_ref, 0, up_at[j], into(up_ref, j * WIDTH), 0)
        wide(in_ref, 0, out_at, into(out_ref, 0), 0)
        for j in range(3):
            wide(in_ref, 0, qkv_at + 2 * j, into(qkv_ref, j * WIDTH), 0)

    lines = []
    for c in range(15):
        pair = in_ref[STAT_AT + c, CHUNK:CHUNK_PAD, :].astype(F32)
        lines.append(pair[0:1] + pair[1:2])

    @pl.when(micro == 0)
    def _():
        section((6, 10, 0, 2), 12, 14)
        for j, place in ((0, 4), (1, 8)):
            wide(in_ref, 0, place, into(down_ref, 0), j * WIDTH)
        for j in (2, 3):
            wide(moved_ref, 51, 12 + 2 * j, into(down_ref, 0), j * WIDTH)

    @pl.when(micro == 1)
    def _():
        section((0, 2, 4, 6), 8, 10)
        diagonal = iota((128, 128), 0) == iota((128, 128), 1)
        for c in range(8):
            column = jnp.sum(jnp.where(diagonal, lines[7 + c], 0.0), axis=1, keepdims=True)
            down_ref[c * 128 : (c + 1) * 128, :] = column * sdf_row_ref[...]

    store(qkv_ref, qkv_hbm.at[0])
    store(out_ref, out_hbm.at[0])
    store(up_ref, up_hbm.at[0])
    store(down_ref, down_hbm.at[0])
    for ref, c in ((gain_one_ref, 0), (gain_two_ref, 2), (sdf_ref, 4)):
        ref[0:1, 0:128] = lines[c]
        ref[0:1, 128:256] = lines[c + 1]
    loss_ref[0:1, :] = lines[6] / (2 * 12288)
    for copy in stores:
        copy.wait()


def fix(value):
    return pltpu.with_memory_space_constraint(value, pltpu.HBM)


def swap_pipe(value):
    return lax.ppermute(value, "pipe", [(0, 1), (1, 0)])


VMEM = pl.BlockSpec(memory_space=pltpu.VMEM)
ANY = pl.BlockSpec(memory_space=pl.ANY)
HBM = pl.BlockSpec(memory_space=pltpu.HBM)


def shards(
    features, coarse, parent, counts, target, gain_attn, w_qkv, w_out, gain_mlp, w_up, w_down, w_sdf
):
    rank_count = lax.axis_size("tok")
    rim = lax.ppermute(coarse[:, -1:, :], "tok", [(i, i + 1) for i in range(rank_count - 1)])
    gains_far = [swap_pipe(g) for g in (gain_attn, gain_mlp)]
    qkv_far, out_far, up_far, down_far = (swap_pipe(w) for w in (w_qkv, w_out, w_up, w_down))
    outgoing = pl.pallas_call(
        embed_kernel,
        out_shape=jax.ShapeDtypeStruct((GROUP, SEND_ROWS, WIDTH), BF),
        in_specs=[HBM, HBM, VMEM, HBM, HBM],
        out_specs=VMEM,
        scratch_shapes=[
            pltpu.VMEM((ROWS, WIDTH), BF),
            pltpu.VMEM((64, WIDTH), BF),
            pltpu.VMEM((2, ROWS), jnp.int32),
            pltpu.VMEM((2, ROWS), F32),
            pltpu.SemaphoreType.DMA((4,)),
        ],
        name="embed",
        compiler_params=pltpu.CompilerParams(vmem_limit_bytes=4 * 2**20),
    )(fix(features), fix(coarse), rim, fix(parent), fix(target))
    groups = [[b * GROUP + i for i in range(GROUP)] for b in range(rank_count // GROUP)]
    received = lax.all_to_all(outgoing, "tok", 0, 0, axis_index_groups=groups, tiled=True)
    packet = jax.ShapeDtypeStruct((64, CHUNK_PAD, 128), BF)
    keep, send = pl.pallas_call(
        step_kernel,
        out_shape=(packet, packet),
        in_specs=[HBM] + [VMEM] * 3 + [HBM] * 3 + [HBM, ANY] * 4,
        out_specs=(ANY, ANY),
        scratch_shapes=[
            pltpu.VMEM((2, WIDTH, 3 * WIDTH), BF),
            pltpu.VMEM((2, WIDTH, WIDTH), BF),
            pltpu.VMEM((2, WIDTH, FF), BF),
            pltpu.VMEM((2, FF, WIDTH), BF),
            pltpu.VMEM((2, ROWS, WIDTH), BF),
            pltpu.VMEM((2, ROWS, 1), F32),
            pltpu.VMEM((2, ROWS, WIDTH), BF),
            pltpu.VMEM((2, 3, ROWS, WIDTH), BF),
            pltpu.VMEM((2, ROWS, WIDTH), F32),
            pltpu.VMEM((2, ROWS, WIDTH), BF),
            pltpu.VMEM((2, ROWS, WIDTH), F32),
            pltpu.VMEM((2, ROWS, 1), F32),
            pltpu.VMEM((2, ROWS, WIDTH), BF),
            pltpu.VMEM((2, 4, ROWS, WIDTH), F32),
            pltpu.VMEM((2, 4, ROWS, WIDTH), BF),
            pltpu.VMEM((2, GROUP, WIDTH), F32),
            pltpu.VMEM((2, 64, CHUNK_PAD, 128), BF),
            pltpu.VMEM((ROWS, WIDTH), F32),
            pltpu.VMEM((3, ROWS, WIDTH), BF),
            pltpu.VMEM((1, WIDTH), F32),
            pltpu.VMEM((1, WIDTH), F32),
            pltpu.VMEM((1, WIDTH), F32),
            pltpu.SMEM((2, 64), jnp.int32),
            pltpu.SemaphoreType.DMA((12,)),
            pltpu.SemaphoreType.DMA((4,)),
        ],
        name="step",
        compiler_params=pltpu.CompilerParams(vmem_limit_bytes=32 * 2**20),
    )(fix(counts), received, *gains_far, fix(w_sdf[None]), fix(gain_attn), fix(gain_mlp), fix(w_qkv), qkv_far, fix(w_out), out_far, fix(w_up), up_far, fix(w_down), down_far)
    far = swap_pipe(send)
    total = (keep.astype(F32) + far.astype(F32)).astype(BF)
    shares = lax.all_to_all(total, "tok", 0, 0, tiled=True)
    summed = jnp.sum(shares.astype(F32), axis=0)
    stat = jnp.sum(summed[CHUNK : CHUNK + 4], axis=0, keepdims=True)
    high = lax.reduce_precision(stat, 8, 7)
    row = iota((CHUNK_PAD, 128), 0)
    tail = jnp.where(row == CHUNK, high, jnp.where(row == CHUNK + 1, stat - high, 0.0))
    summed = jnp.where(row < CHUNK, summed, tail).astype(BF)
    gathered = lax.all_to_all(
        jnp.broadcast_to(summed[None], (rank_count, CHUNK_PAD, 128)), "tok", 0, 0, tiled=True
    )
    moved = lax.ppermute(gathered[51:64], "pipe", [(1, 0)])
    loss, sdf, gain_one, qkv, out, gain_two, up, down = pl.pallas_call(
        unpack_kernel,
        out_shape=(
            jax.ShapeDtypeStruct((1, 128), F32),
            jax.ShapeDtypeStruct((1, WIDTH), F32),
            jax.ShapeDtypeStruct((1, WIDTH), F32),
            jax.ShapeDtypeStruct((1, WIDTH, 3 * WIDTH), F32),
            jax.ShapeDtypeStruct((1, WIDTH, WIDTH), F32),
            jax.ShapeDtypeStruct((1, WIDTH), F32),
            jax.ShapeDtypeStruct((1, WIDTH, FF), F32),
            jax.ShapeDtypeStruct((1, FF, WIDTH), F32),
        ),
        in_specs=[VMEM, VMEM, VMEM],
        out_specs=(VMEM, VMEM, VMEM, HBM, HBM, VMEM, HBM, HBM),
        scratch_shapes=[
            pltpu.VMEM((WIDTH, 3 * WIDTH), F32),
            pltpu.VMEM((WIDTH, WIDTH), F32),
            pltpu.VMEM((WIDTH, FF), F32),
            pltpu.VMEM((FF, WIDTH), F32),
            pltpu.SemaphoreType.DMA((7,)),
        ],
        name="unpack",
        compiler_params=pltpu.CompilerParams(vmem_limit_bytes=16 * 2**20),
    )(gathered, moved, fix(w_sdf[None]))
    return loss[0, 0], sdf[0], gain_one, qkv, out, gain_two, up, down


def solution(mesh):
    return jax.shard_map(
        shards,
        mesh=mesh,
        in_specs=(
            P(None, "tok", None),
            P(None, "tok", None),
            P(None, "tok"),
            P(),
            P(None, "tok"),
            P("pipe", None),
            P("pipe", None, None),
            P("pipe", None, None),
            P("pipe", None),
            P("pipe", None, None),
            P("pipe", None, None),
            P(),
        ),
        out_specs=(
            P(),
            P(),
            P("pipe", None),
            P("pipe", None, None),
            P("pipe", None, None),
            P("pipe", None),
            P("pipe", None, None),
            P("pipe", None, None),
        ),
        check_vma=False,
    )
```

```python
import functools
import math

import jax
import jax.numpy as jnp
from jax import lax
from jax.experimental import pallas as pl
from jax.experimental.pallas import tpu as pltpu
from jax.sharding import PartitionSpec as P


H = 8
WIN = 32
GROUP = 8
ROWS = 256
WIDTH = 256
FF = 1024
HEAD = WIDTH // H
EPS = 1e-06
CHUNK = 80
CHUNK_PAD = 88
SLAB = 16
STAT_AT = 25
SEND_ROWS = 40
BF = jnp.bfloat16
F32 = jnp.float32


def nn(a, b):
    return jnp.dot(a, b, preferred_element_type=F32)


def nt(a, b):
    return lax.dot_general(a, b, (((1,), (1,)), ((), ())), preferred_element_type=F32)


def tn(a, b):
    return lax.dot_general(a, b, (((0,), (0,)), ((), ())), preferred_element_type=F32)


def iota(shape, dim):
    return lax.broadcasted_iota(jnp.int32, shape, dim)


def split_two(value):
    high = value.astype(BF)
    low = (value - high.astype(F32)).astype(BF)
    return high, low


def embed_kernel(
    features_hbm, coarse_hbm, rim_ref, parent_hbm, target_hbm, out_ref,
    features_ref, coarse_ref, parent_ref, target_ref, load_sem,
):
    micro = lax.axis_index("pipe")
    shard = lax.axis_index("tok")
    loads = [
        pltpu.make_async_copy(source, held, load_sem.at[number])
        for number, (source, held) in enumerate(
            (
                (features_hbm.at[micro], features_ref),
                (coarse_hbm.at[micro], coarse_ref),
                (parent_hbm, parent_ref),
                (target_hbm, target_ref),
            )
        )
    ]
    for load in loads:
        load.start()
    for load in loads:
        load.wait()
    local = parent_ref[pl.ds(micro, 1), :] - shard * 64
    own_hot = jnp.where(iota((64, ROWS), 0) == local, 1.0, 0.0).astype(BF)
    rim_hot = jnp.where((iota((16, ROWS), 0) == 0) & (local == -1), 1.0, 0.0).astype(BF)
    rim = jnp.broadcast_to(rim_ref[micro], (16, WIDTH))
    lifted = tn(own_hot, coarse_ref[...]) + tn(rim_hot, rim)
    embedded = (features_ref[...].astype(F32) + lifted).astype(BF)
    target = jnp.broadcast_to(target_ref[pl.ds(micro, 1), :], (8, ROWS))
    high = target.astype(BF).astype(F32)
    middle = (target - high).astype(BF).astype(F32)
    low = target - high - middle
    row = iota((8, ROWS), 0)
    extra = jnp.where(row == 0, high, jnp.where(row == 1, middle, jnp.where(row == 2, low, 0.0)))
    extra = extra.astype(BF)
    for part in range(GROUP):
        out_ref[part, 0:WIN, :] = embedded[part * WIN : (part + 1) * WIN]
        out_ref[part, WIN:SEND_ROWS, :] = extra


def group_max(values, same_head):
    lane = iota((1, 128), 1)
    halves = []
    for side in range(2):
        half = values[:, side * 128 : (side + 1) * 128]
        for step in (1, 2, 4, 8, 16):
            half = jnp.maximum(half, pltpu.roll(half, step, 1))
        halves.append(jnp.where(lane % WIN == WIN - 1, half, 0.0))
    return group_sum(jnp.concatenate(halves, axis=1), same_head)


def group_sum(values, same_head):
    high, low = split_two(values)
    return nn(high, same_head) + nn(low, same_head)


def step_kernel(
    counts_hbm, received_ref, gain_far_one, gain_far_two, sdf_hbm, gain_own_one_hbm, gain_own_two_hbm,
    qkv_own, qkv_far, out_own, out_far, up_own, up_far, down_own, down_far,
    keep_ref, send_ref,
    w_qkv, w_out, w_up, w_down,
    x_buf, inv_one, normed_buf, packed_buf, prob_buf, mixed_buf, after_buf, inv_two,
    normed_two_buf, slope_buf, hidden_buf, mask_buf, grads, score_buf, dpacked_buf,
    sdf_ref, gain_own_one, gain_own_two, counts_ref, load_sem, store_sem,
):
    micro = lax.axis_index("pipe")
    shard = lax.axis_index("tok")
    part = lax.rem(shard, GROUP)
    first = shard - part
    loads = []
    for number, (own, far, held) in enumerate(
        ((qkv_own, qkv_far, w_qkv), (out_own, out_far, w_out), (up_own, up_far, w_up), (down_own, down_far, w_down))
    ):
        loads.append(pltpu.make_async_copy(own.at[0], held.at[micro], load_sem.at[2 * number]))
        loads.append(pltpu.make_async_copy(far.at[0], held.at[1 - micro], load_sem.at[2 * number + 1]))
    small = [
        pltpu.make_async_copy(source, held, load_sem.at[8 + number])
        for number, (source, held) in enumerate(
            (
                (sdf_hbm, sdf_ref),
                (gain_own_one_hbm, gain_own_one),
                (gain_own_two_hbm, gain_own_two),
                (counts_hbm, counts_ref),
            )
        )
    ]
    for load in small + loads:
        load.start()
    for load in small:
        load.wait()

    own_is_first = micro == 0

    def gain(section, which):
        own = (gain_own_one, gain_own_two)[which][...]
        far = (gain_far_one, gain_far_two)[which][...]
        mine = own_is_first if section == 0 else jnp.logical_not(own_is_first)
        return jnp.where(mine, own, far)

    row_i = iota((ROWS, WIDTH), 0)
    col_i = iota((ROWS, WIDTH), 1)
    same_head = jnp.where(row_i // WIN == col_i // HEAD, 1.0, 0.0).astype(BF)
    swapped = row_i % WIN // 4 * WIN + row_i // WIN * 4 + row_i % 4
    swap = jnp.where(swapped == col_i, 1.0, 0.0).astype(BF)

    def exchange(value):
        return nn(swap, value).astype(BF)

    lane = iota((1, WIDTH), 1)
    key = lane % WIN
    count_of = [counts_ref[micro, first + s] for s in range(GROUP)]
    lane_count = jnp.zeros((1, WIDTH), jnp.int32)
    for s in range(GROUP):
        lane_count = jnp.where(key // 4 == s, count_of[s], lane_count)
    fills = ([], [])
    for w in range(GROUP):
        dilated = part * WIN + w * 4 + key % 4 < lane_count
        plain = part * WIN + key < count_of[w]
        mask_buf[0, w : w + 1, :] = jnp.where(dilated, 1.0, 0.0)
        most = functools.reduce(jnp.maximum, count_of)
        fills[0].append(jnp.where(part * WIN + w * 4 < most, -1e30, 0.0))
        fills[1].append(jnp.where(part * WIN < count_of[w], -1e30, 0.0))
        mask_buf[1, w : w + 1, :] = jnp.where(plain, 1.0, 0.0)

    def expand(value):
        return jnp.concatenate([value] * H, axis=0) * same_head

    def window(value, w):
        return value[w * WIN : (w + 1) * WIN]

    def store_grad(stream, place, value):
        for i in range(ROWS // SLAB):
            slab = place * (ROWS // SLAB) + i
            base = slab % 5 * SLAB
            grads[stream, slab // 5, base : base + SLAB, :] = value[i * SLAB : (i + 1) * SLAB].astype(BF)

    def store_wide(stream, place, value):
        store_grad(stream, place, value[:, :128])
        store_grad(stream, place + 1, value[:, 128:])

    stat_row = iota((8, 128), 0)
    for stream in range(2):
        grads[stream, :, CHUNK:CHUNK_PAD, :] = jnp.zeros((64, CHUNK_PAD - CHUNK, 128), BF)

    def store_stats(stream, lines):
        halves = []
        for line in lines:
            halves += [line[:, i : i + 128] for i in range(0, line.shape[1], 128)]
        for c, line in enumerate(halves):
            high, low = split_two(line)
            both = jnp.where(
                stat_row == 2 * micro, high.astype(F32), jnp.where(stat_row == 2 * micro + 1, low.astype(F32), 0.0)
            )
            grads[stream, STAT_AT + c, CHUNK:CHUNK_PAD, :] = both.astype(BF)

    stores = []

    def send_out(stream, first_chunk, last_chunk):
        number = len(stores)
        chunks = pl.ds(first_chunk, last_chunk - first_chunk)
        copies = [
            pltpu.make_async_copy(grads.at[stream, chunks], ref.at[chunks], store_sem.at[number])
            for ref in (keep_ref, send_ref)
        ]
        stores.append(copies[0])
        pl.when(micro == stream)(copies[0].start)
        pl.when(micro != stream)(copies[1].start)

    def forward(k):
        x = x_buf[k].astype(F32)
        inv = lax.rsqrt(jnp.mean(x * x, axis=-1, keepdims=True) + EPS)
        inv_one[k] = inv
        normed = (x * inv * gain(k, 0)).astype(BF)
        normed_buf[k] = normed
        if k == 0:
            loads[0].wait()
            loads[1].wait()
        for j in range(3):
            packed_buf[k, j] = nn(normed, w_qkv[k, :, j * WIDTH : (j + 1) * WIDTH]).astype(BF)
        for w in range(GROUP):
            rows = slice(w * WIN, (w + 1) * WIN)
            scores = nt(packed_buf[k, 0, rows, :], expand(packed_buf[k, 1, rows, :]))
            score_buf[rows, :] = jnp.where(mask_buf[k, w : w + 1, :] > 0.5, scores * HEAD**-0.5, fills[k][w])
        scores = score_buf[...]
        weights = jnp.exp(scores - group_max(scores, same_head))
        prob = weights / group_sum(weights, same_head)
        prob_buf[k] = prob
        prob_low = prob.astype(BF)
        for w in range(GROUP):
            rows = slice(w * WIN, (w + 1) * WIN)
            mixed_buf[k, rows, :] = nn(window(prob_low, w), expand(packed_buf[k, 2, rows, :])).astype(BF)
        if k == 0:
            loads[2].wait()
            loads[3].wait()
        after = x + nn(mixed_buf[k], w_out[k])
        after_buf[k] = after
        inv = lax.rsqrt(jnp.mean(after * after, axis=-1, keepdims=True) + EPS)
        inv_two[k] = inv
        normed_two = (after * inv * gain(k, 1)).astype(BF)
        normed_two_buf[k] = normed_two
        if k == 0:
            for load in loads[4:]:
                load.wait()
        total = after
        for j in range(4):
            cols = slice(j * WIDTH, (j + 1) * WIDTH)
            up = nn(normed_two, w_up[k, :, cols])
            root = math.sqrt(2.0 / math.pi)
            square = up * up
            half = 0.5 * jnp.tanh(up * (root + (root * 0.044715) * square)) + 0.5
            hidden = (up * half).astype(BF)
            hidden_buf[k, j] = hidden
            bend = up * (2 * root + (6 * root * 0.044715) * square)
            slope_buf[k, j] = half * (1.0 + bend * (1.0 - half))
            total = total + nn(hidden, w_down[k, cols, :])
        return total.astype(BF)

    def norm_back(grad, value, inv, gain_row):
        gain_grad = jnp.sum(grad * value * inv, axis=0, keepdims=True)
        scaled = grad * gain_row
        inner = jnp.mean(scaled * value, axis=-1, keepdims=True)
        return inv * (scaled - value * (inv * inv * inner)), gain_grad

    def backward(k, out_grad, slope, pulled):
        back = None
        down_lines = []
        for j in (2, 3, 0, 1):
            cols = slice(j * WIDTH, (j + 1) * WIDTH)
            if k == 0:
                stream, place = (1, 12 + 2 * j) if j >= 2 else (0, 16 + 2 * j)
                out_low = out_grad.astype(BF)
                store_wide(stream, place, tn(hidden_buf[k, j], out_low))
                hidden_grad = nt(out_low, w_down[k, cols, :]).astype(BF).astype(F32)
            else:
                down_lines.append(jnp.sum(hidden_buf[k, j].astype(F32) * slope, axis=0, keepdims=True))
                hidden_grad = slope * pulled[j]
            up_grad = (slope_buf[k, j] * hidden_grad).astype(BF)
            store_wide(k, 2 * j, tn(normed_two_buf[k], up_grad))
            term = nt(up_grad, w_up[k, :, cols])
            back = term if back is None else back + term
            if k == 0 and j == 3:
                send_out(1, 51, 64)
        if k == 0:
            send_out(0, 0, 25)
            send_out(0, 52, 64)
        normed_two_grad = back.astype(BF).astype(F32)
        res_grad, gain_two_grad = norm_back(normed_two_grad, after_buf[k], inv_two[k], gain(k, 1))
        after_grad = out_grad + res_grad
        after_low = after_grad.astype(BF)
        store_wide(k, 8, tn(mixed_buf[k], after_low))
        mixed_grad = nt(after_low, w_out[k]).astype(BF)
        for w in range(GROUP):
            rows = slice(w * WIN, (w + 1) * WIN)
            score_buf[rows, :] = nt(window(mixed_grad, w), expand(packed_buf[k, 2, rows, :]))
        prob = prob_buf[k]
        prob_low = prob.astype(BF)
        prob_grad = score_buf[...].astype(BF).astype(F32)
        flow = prob * prob_grad
        score_grad = (flow - prob * group_sum(flow, same_head)) * HEAD**-0.5

        lane_head = iota((WIN, 128), 1) // HEAD

        def fold(left, right):
            halves = []
            for side in range(2):
                cols = slice(side * 128, (side + 1) * 128)
                value = tn(left[:, cols], right[:, cols])
                total = window(value, 3)
                for h in range(3):
                    total = jnp.where(lane_head == h, window(value, h), total)
                halves.append(total.astype(BF))
            return jnp.concatenate(halves, axis=1)

        for w in range(GROUP):
            rows = slice(w * WIN, (w + 1) * WIN)
            grad_w = jnp.where(mask_buf[k, w : w + 1, :] > 0.5, window(score_grad, w), 0.0).astype(BF)
            dpacked_buf[0, rows, :] = nn(grad_w, expand(packed_buf[k, 1, rows, :])).astype(BF)
            dpacked_buf[1, rows, :] = fold(grad_w, packed_buf[k, 0, rows, :])
            dpacked_buf[2, rows, :] = fold(window(prob_low, w), window(mixed_grad, w))
        back = None
        for j in range(3):
            piece = dpacked_buf[j]
            store_wide(k, 10 + 2 * j, tn(normed_buf[k], piece))
            term = nt(piece, w_qkv[k, :, j * WIDTH : (j + 1) * WIDTH])
            back = term if back is None else back + term
        normed_grad = back.astype(BF).astype(F32)
        in_res, gain_one_grad = norm_back(normed_grad, x_buf[k].astype(F32), inv_one[k], gain(k, 0))
        return (after_grad + in_res).astype(BF), gain_one_grad, gain_two_grad, down_lines[2:] + down_lines[:2]

    received = received_ref[:, 0:WIN, :].reshape(ROWS, WIDTH)
    x_buf[0] = exchange(received)
    x_buf[1] = exchange(forward(0))
    section_one = forward(1).astype(F32)

    pieces = []
    lane_w = iota((WIN, WIDTH), 1)
    row_w = iota((WIN, WIDTH), 0)
    valid_pieces = []
    for s in range(GROUP):
        parts = received_ref[s, WIN : WIN + 8, :].astype(F32)
        line = parts[0:1] + parts[1:2] + parts[2:3]
        chosen = jnp.where(lane_w == part * WIN + row_w, line, 0.0)
        pieces.append(jnp.sum(chosen, axis=-1, keepdims=True))
        valid_pieces.append(part * WIN + iota((WIN, 1), 0) < count_of[s])
    target = jnp.concatenate(pieces, axis=0)
    valid = jnp.concatenate([jnp.where(v, 1.0, 0.0) for v in valid_pieces], axis=0)
    sdf = sdf_ref[...]
    predicted = jnp.sum(section_one * sdf, axis=-1, keepdims=True)
    residue = jnp.where(valid > 0.5, predicted - target, 0.0)
    slope = 2.0 * residue / math.sqrt(3 * ROWS * 64 // 4)
    loss = jnp.sum(residue * residue, axis=0, keepdims=True)
    sdf_grad = jnp.sum(slope * section_one, axis=0, keepdims=True)
    high = sdf.astype(BF).astype(F32)
    middle = (sdf - high).astype(BF).astype(F32)
    row = iota((16, WIDTH), 0)
    parts = jnp.where(row == 0, high, jnp.where(row == 1, middle, jnp.where(row == 2, sdf - high - middle, 0.0)))
    parts = parts.astype(BF)
    pulled = [
        jnp.sum(nt(parts, w_down[1, j * WIDTH : (j + 1) * WIDTH, :]), axis=0, keepdims=True) for j in range(4)
    ]
    loss_row = jnp.broadcast_to(loss, (1, 128))
    middle_grad, gain_one, gain_two, down_lines = backward(1, slope * sdf, slope, pulled)
    store_stats(1, [gain_one, gain_two, sdf_grad, loss_row] + down_lines)
    send_out(1, 0, 51)
    unused, gain_one, gain_two, none = backward(0, exchange(middle_grad).astype(F32), None, None)
    del unused, none
    store_stats(0, [gain_one, gain_two, sdf_grad, loss_row])
    send_out(0, 25, 52)
    for store in stores:
        store.wait()


def wide(source, first_chunk, place, ref, row, col, slabs=range(ROWS // SLAB)):
    for side in range(2):
        for i in slabs:
            slab = (place + side) * (ROWS // SLAB) + i
            low = slab % 5 * SLAB
            piece = source[slab // 5 - first_chunk, low : low + SLAB, :].astype(F32)
            ref[row + i * SLAB : row + (i + 1) * SLAB, col + side * 128 : col + (side + 1) * 128] = piece


def unpack_kernel(
    in_ref, sdf_row_ref, loss_ref, sdf_ref, gain_one_ref, qkv_hbm, out_hbm, gain_two_ref, up_hbm, down_hbm,
    qkv_ref, out_ref, up_ref, down_ref, store_sem,
):
    micro = lax.axis_index("pipe")
    stores = []

    def store(source, target):
        copy = pltpu.make_async_copy(source, target, store_sem.at[len(stores)])
        copy.start()
        stores.append(copy)

    for ref, target, place, count in ((up_ref, up_hbm, 0, 4), (out_ref, out_hbm, 8, 1), (qkv_ref, qkv_hbm, 10, 3)):
        for quarter in range(4):
            for j in range(count):
                wide(in_ref, 0, place + 2 * j, ref, 0, j * WIDTH, range(4 * quarter, 4 * quarter + 4))
            rows = pl.ds(quarter * 64, 64)
            store(ref.at[rows], target.at[0, rows])
    lines = []
    for c in range(15):
        pair = in_ref[STAT_AT + c, CHUNK:CHUNK_PAD, :].astype(F32)
        lines.append(pair[0:1] + pair[1:2])
    for ref, c in ((gain_one_ref, 0), (gain_two_ref, 2), (sdf_ref, 4)):
        ref[0:1, 0:128] = lines[c]
        ref[0:1, 128:256] = lines[c + 1]
    loss_ref[0:1, :] = lines[6] / (2 * 12288)

    @pl.when(micro == 0)
    def _():
        for j in range(2):
            wide(in_ref, 0, 16 + 2 * j, down_ref, j * WIDTH, 0)

    @pl.when(micro == 1)
    def _():
        diagonal = iota((128, 128), 0) == iota((128, 128), 1)
        for c in range(8):
            column = jnp.sum(jnp.where(diagonal, lines[7 + c], 0.0), axis=1, keepdims=True)
            down_ref[c * 128 : (c + 1) * 128, :] = column * sdf_row_ref[...]

    for quarter in range(4):
        rows = pl.ds(quarter * WIDTH, WIDTH)
        store(down_ref.at[rows], down_hbm.at[0, rows])
    for copy in stores:
        copy.wait()


def finish_kernel(moved_hbm, down_in, down_out, moved_ref, half_ref, sem):
    del down_in

    @pl.when(lax.axis_index("pipe") == 0)
    def _():
        load = pltpu.make_async_copy(moved_hbm, moved_ref, sem.at[0])
        load.start()
        load.wait()
        for j in range(2):
            wide(moved_ref, 51, 16 + 2 * j, half_ref, j * WIDTH, 0)
        store = pltpu.make_async_copy(half_ref, down_out.at[0, pl.ds(2 * WIDTH, 2 * WIDTH)], sem.at[1])
        store.start()
        store.wait()


def fix(value):
    return pltpu.with_memory_space_constraint(value, pltpu.HBM)


def swap_pipe(value):
    return lax.ppermute(value, "pipe", [(0, 1), (1, 0)])


VMEM = pl.BlockSpec(memory_space=pltpu.VMEM)
ANY = pl.BlockSpec(memory_space=pl.ANY)
HBM = pl.BlockSpec(memory_space=pltpu.HBM)


def shards(
    features, coarse, parent, counts, target, gain_attn, w_qkv, w_out, gain_mlp, w_up, w_down, w_sdf
):
    rank_count = lax.axis_size("tok")
    rim = lax.ppermute(coarse[:, -1:, :], "tok", [(i, i + 1) for i in range(rank_count - 1)])
    arrived = []
    for value in (gain_attn, gain_mlp, w_qkv, w_out, w_up, w_down):
        arrived.append(swap_pipe(value))
    gains_far = arrived[:2]
    qkv_far, out_far, up_far, down_far = arrived[2:]
    outgoing = pl.pallas_call(
        embed_kernel,
        out_shape=jax.ShapeDtypeStruct((GROUP, SEND_ROWS, WIDTH), BF),
        in_specs=[HBM, HBM, VMEM, HBM, HBM],
        out_specs=VMEM,
        scratch_shapes=[
            pltpu.VMEM((ROWS, WIDTH), BF),
            pltpu.VMEM((64, WIDTH), BF),
            pltpu.VMEM((2, ROWS), jnp.int32),
            pltpu.VMEM((2, ROWS), F32),
            pltpu.SemaphoreType.DMA((4,)),
        ],
        name="embed",
        compiler_params=pltpu.CompilerParams(vmem_limit_bytes=4 * 2**20),
    )(fix(features), fix(coarse), rim, fix(parent), fix(target))
    groups = [[b * GROUP + i for i in range(GROUP)] for b in range(rank_count // GROUP)]
    received = lax.all_to_all(outgoing, "tok", 0, 0, axis_index_groups=groups, tiled=True)
    packet = jax.ShapeDtypeStruct((64, CHUNK_PAD, 128), BF)
    keep, send = pl.pallas_call(
        step_kernel,
        out_shape=(packet, packet),
        in_specs=[HBM] + [VMEM] * 3 + [HBM] * 3 + [HBM, ANY] * 4,
        out_specs=(ANY, ANY),
        scratch_shapes=[
            pltpu.VMEM((2, WIDTH, 3 * WIDTH), BF),
            pltpu.VMEM((2, WIDTH, WIDTH), BF),
            pltpu.VMEM((2, WIDTH, FF), BF),
            pltpu.VMEM((2, FF, WIDTH), BF),
            pltpu.VMEM((2, ROWS, WIDTH), BF),
            pltpu.VMEM((2, ROWS, 1), F32),
            pltpu.VMEM((2, ROWS, WIDTH), BF),
            pltpu.VMEM((2, 3, ROWS, WIDTH), BF),
            pltpu.VMEM((2, ROWS, WIDTH), F32),
            pltpu.VMEM((2, ROWS, WIDTH), BF),
            pltpu.VMEM((2, ROWS, WIDTH), F32),
            pltpu.VMEM((2, ROWS, 1), F32),
            pltpu.VMEM((2, ROWS, WIDTH), BF),
            pltpu.VMEM((2, 4, ROWS, WIDTH), F32),
            pltpu.VMEM((2, 4, ROWS, WIDTH), BF),
            pltpu.VMEM((2, GROUP, WIDTH), F32),
            pltpu.VMEM((2, 64, CHUNK_PAD, 128), BF),
            pltpu.VMEM((ROWS, WIDTH), F32),
            pltpu.VMEM((3, ROWS, WIDTH), BF),
            pltpu.VMEM((1, WIDTH), F32),
            pltpu.VMEM((1, WIDTH), F32),
            pltpu.VMEM((1, WIDTH), F32),
            pltpu.SMEM((2, 64), jnp.int32),
            pltpu.SemaphoreType.DMA((12,)),
            pltpu.SemaphoreType.DMA((5,)),
        ],
        name="step",
        compiler_params=pltpu.CompilerParams(vmem_limit_bytes=32 * 2**20),
    )(fix(counts), received, *gains_far, fix(w_sdf[None]), fix(gain_attn), fix(gain_mlp), fix(w_qkv), qkv_far, fix(w_out), out_far, fix(w_up), up_far, fix(w_down), down_far)
    far = swap_pipe(send)
    total = (keep.astype(F32) + far.astype(F32)).astype(BF)
    shares = lax.all_to_all(total, "tok", 0, 0, tiled=True)
    summed = jnp.sum(shares.astype(F32), axis=0)
    stat = jnp.sum(summed[CHUNK : CHUNK + 4], axis=0, keepdims=True)
    high = lax.reduce_precision(stat, 8, 7)
    row = iota((CHUNK_PAD, 128), 0)
    tail = jnp.where(row == CHUNK, high, jnp.where(row == CHUNK + 1, stat - high, 0.0))
    summed = jnp.where(row < CHUNK, summed, tail).astype(BF)
    gathered = lax.all_to_all(
        jnp.broadcast_to(summed[None], (rank_count, CHUNK_PAD, 128)), "tok", 0, 0, tiled=True
    )
    moved = lax.ppermute(gathered[51:64], "pipe", [(1, 0)])
    loss, sdf, gain_one, qkv, out, gain_two, up, down = pl.pallas_call(
        unpack_kernel,
        out_shape=(
            jax.ShapeDtypeStruct((1, 128), F32),
            jax.ShapeDtypeStruct((1, WIDTH), F32),
            jax.ShapeDtypeStruct((1, WIDTH), F32),
            jax.ShapeDtypeStruct((1, WIDTH, 3 * WIDTH), F32),
            jax.ShapeDtypeStruct((1, WIDTH, WIDTH), F32),
            jax.ShapeDtypeStruct((1, WIDTH), F32),
            jax.ShapeDtypeStruct((1, WIDTH, FF), F32),
            jax.ShapeDtypeStruct((1, FF, WIDTH), F32),
        ),
        in_specs=[VMEM, VMEM],
        out_specs=(VMEM, VMEM, VMEM, HBM, HBM, VMEM, HBM, HBM),
        scratch_shapes=[
            pltpu.VMEM((WIDTH, 3 * WIDTH), F32),
            pltpu.VMEM((WIDTH, WIDTH), F32),
            pltpu.VMEM((WIDTH, FF), F32),
            pltpu.VMEM((FF, WIDTH), F32),
            pltpu.SemaphoreType.DMA((16,)),
        ],
        name="unpack",
        compiler_params=pltpu.CompilerParams(vmem_limit_bytes=16 * 2**20),
    )(gathered, fix(w_sdf[None]))
    down = pl.pallas_call(
        finish_kernel,
        out_shape=jax.ShapeDtypeStruct((1, FF, WIDTH), F32),
        in_specs=[ANY, HBM],
        out_specs=HBM,
        scratch_shapes=[
            pltpu.VMEM((13, CHUNK_PAD, 128), BF),
            pltpu.VMEM((2 * WIDTH, WIDTH), F32),
            pltpu.SemaphoreType.DMA((2,)),
        ],
        input_output_aliases={1: 0},
        name="finish",
        compiler_params=pltpu.CompilerParams(vmem_limit_bytes=16 * 2**20),
    )(moved, down)
    return loss[0, 0], sdf[0], gain_one, qkv, out, gain_two, up, down


def solution(mesh):
    return jax.shard_map(
        shards,
        mesh=mesh,
        in_specs=(
            P(None, "tok", None),
            P(None, "tok", None),
            P(None, "tok"),
            P(),
            P(None, "tok"),
            P("pipe", None),
            P("pipe", None, None),
            P("pipe", None, None),
            P("pipe", None),
            P("pipe", None, None),
            P("pipe", None, None),
            P(),
        ),
        out_specs=(
            P(),
            P(),
            P("pipe", None),
            P("pipe", None, None),
            P("pipe", None, None),
            P("pipe", None),
            P("pipe", None, None),
            P("pipe", None, None),
        ),
        check_vma=False,
    )
```

```python
import functools
import math

import jax
import jax.numpy as jnp
from jax import lax
from jax.experimental import pallas as pl
from jax.experimental.pallas import tpu as pltpu
from jax.sharding import PartitionSpec as P


H = 8
WIN = 32
GROUP = 8
ROWS = 256
WIDTH = 256
FF = 1024
HEAD = WIDTH // H
EPS = 1e-06
CHUNK = 80
CHUNK_PAD = 88
SLAB = 16
STAT_AT = 25
SEND_ROWS = 40
BF = jnp.bfloat16
F32 = jnp.float32


def nn(a, b):
    return jnp.dot(a, b, preferred_element_type=F32)


def nt(a, b):
    return lax.dot_general(a, b, (((1,), (1,)), ((), ())), preferred_element_type=F32)


def tn(a, b):
    return lax.dot_general(a, b, (((0,), (0,)), ((), ())), preferred_element_type=F32)


def iota(shape, dim):
    return lax.broadcasted_iota(jnp.int32, shape, dim)


def split_two(value):
    high = value.astype(BF)
    low = (value - high.astype(F32)).astype(BF)
    return high, low


def embed_kernel(
    features_hbm, coarse_hbm, parent_hbm, target_hbm, out_ref, rim_hot_ref,
    features_ref, coarse_ref, parent_ref, target_ref, load_sem,
):
    micro = lax.axis_index("pipe")
    shard = lax.axis_index("tok")
    loads = [
        pltpu.make_async_copy(source, held, load_sem.at[number])
        for number, (source, held) in enumerate(
            (
                (features_hbm.at[micro], features_ref),
                (coarse_hbm.at[micro], coarse_ref),
                (parent_hbm, parent_ref),
                (target_hbm, target_ref),
            )
        )
    ]
    for load in loads:
        load.start()
    for load in loads:
        load.wait()
    local = parent_ref[pl.ds(micro, 1), :] - shard * 64
    own_hot = jnp.where(iota((64, ROWS), 0) == local, 1.0, 0.0).astype(BF)
    rim_hot_ref[...] = jnp.where((iota((16, ROWS), 0) == 0) & (local == -1), 1.0, 0.0).astype(BF)
    embedded = (features_ref[...].astype(F32) + tn(own_hot, coarse_ref[...])).astype(BF)
    target = jnp.broadcast_to(target_ref[pl.ds(micro, 1), :], (8, ROWS))
    high = target.astype(BF).astype(F32)
    middle = (target - high).astype(BF).astype(F32)
    low = target - high - middle
    row = iota((8, ROWS), 0)
    extra = jnp.where(row == 0, high, jnp.where(row == 1, middle, jnp.where(row == 2, low, 0.0)))
    extra = extra.astype(BF)
    for part in range(GROUP):
        out_ref[part, 0:WIN, :] = embedded[part * WIN : (part + 1) * WIN]
        out_ref[part, WIN:SEND_ROWS, :] = extra


def rim_kernel(embedded_ref, rim_hot_ref, rim_ref, out_ref):
    rim = jnp.broadcast_to(rim_ref[lax.axis_index("pipe")], (16, WIDTH))
    lifted = tn(rim_hot_ref[...], rim)
    for part in range(GROUP):
        rows = slice(part * WIN, (part + 1) * WIN)
        out_ref[part, 0:WIN, :] = (embedded_ref[part, 0:WIN, :].astype(F32) + lifted[rows]).astype(BF)
        out_ref[part, WIN:SEND_ROWS, :] = embedded_ref[part, WIN:SEND_ROWS, :]


def group_max(values, same_head):
    lane = iota((1, 128), 1)
    halves = []
    for side in range(2):
        half = values[:, side * 128 : (side + 1) * 128]
        for step in (1, 2, 4, 8, 16):
            half = jnp.maximum(half, pltpu.roll(half, step, 1))
        halves.append(jnp.where(lane % WIN == WIN - 1, half, 0.0))
    return group_sum(jnp.concatenate(halves, axis=1), same_head)


def group_sum(values, same_head):
    high, low = split_two(values)
    return nn(high, same_head) + nn(low, same_head)


def step_kernel(
    counts_hbm, received_ref, gain_far_one, gain_far_two, sdf_hbm, gain_own_one_hbm, gain_own_two_hbm,
    qkv_own, qkv_far, out_own, out_far, up_own, up_far, down_own, down_far,
    keep_ref, send_ref,
    w_qkv, w_out, w_up, w_down,
    x_buf, inv_one, normed_buf, packed_buf, prob_buf, mixed_buf, after_buf, inv_two,
    normed_two_buf, slope_buf, hidden_buf, mask_buf, grads, score_buf, dpacked_buf,
    sdf_ref, gain_own_one, gain_own_two, counts_ref, load_sem, store_sem,
):
    micro = lax.axis_index("pipe")
    shard = lax.axis_index("tok")
    part = lax.rem(shard, GROUP)
    first = shard - part
    loads = []
    for number, (own, far, held) in enumerate(
        ((qkv_own, qkv_far, w_qkv), (out_own, out_far, w_out), (up_own, up_far, w_up), (down_own, down_far, w_down))
    ):
        loads.append(pltpu.make_async_copy(own.at[0], held.at[micro], load_sem.at[2 * number]))
        loads.append(pltpu.make_async_copy(far.at[0], held.at[1 - micro], load_sem.at[2 * number + 1]))
    small = [
        pltpu.make_async_copy(source, held, load_sem.at[8 + number])
        for number, (source, held) in enumerate(
            (
                (sdf_hbm, sdf_ref),
                (gain_own_one_hbm, gain_own_one),
                (gain_own_two_hbm, gain_own_two),
                (counts_hbm, counts_ref),
            )
        )
    ]
    for load in small + loads:
        load.start()
    for load in small:
        load.wait()

    own_is_first = micro == 0

    def gain(section, which):
        own = (gain_own_one, gain_own_two)[which][...]
        far = (gain_far_one, gain_far_two)[which][...]
        mine = own_is_first if section == 0 else jnp.logical_not(own_is_first)
        return jnp.where(mine, own, far)

    row_i = iota((ROWS, WIDTH), 0)
    col_i = iota((ROWS, WIDTH), 1)
    same_head = jnp.where(row_i // WIN == col_i // HEAD, 1.0, 0.0).astype(BF)
    swapped = row_i % WIN // 4 * WIN + row_i // WIN * 4 + row_i % 4
    swap = jnp.where(swapped == col_i, 1.0, 0.0).astype(BF)

    def exchange(value):
        return nn(swap, value).astype(BF)

    lane = iota((1, WIDTH), 1)
    key = lane % WIN
    count_of = [counts_ref[micro, first + s] for s in range(GROUP)]
    lane_count = jnp.zeros((1, WIDTH), jnp.int32)
    for s in range(GROUP):
        lane_count = jnp.where(key // 4 == s, count_of[s], lane_count)
    fills = ([], [])
    for w in range(GROUP):
        dilated = part * WIN + w * 4 + key % 4 < lane_count
        plain = part * WIN + key < count_of[w]
        mask_buf[0, w : w + 1, :] = jnp.where(dilated, 1.0, 0.0)
        most = functools.reduce(jnp.maximum, count_of)
        fills[0].append(jnp.where(part * WIN + w * 4 < most, -1e30, 0.0))
        fills[1].append(jnp.where(part * WIN < count_of[w], -1e30, 0.0))
        mask_buf[1, w : w + 1, :] = jnp.where(plain, 1.0, 0.0)

    def expand(value):
        return jnp.concatenate([value] * H, axis=0) * same_head

    def window(value, w):
        return value[w * WIN : (w + 1) * WIN]

    def store_grad(stream, place, value):
        for i in range(ROWS // SLAB):
            slab = place * (ROWS // SLAB) + i
            base = slab % 5 * SLAB
            grads[stream, slab // 5, base : base + SLAB, :] = value[i * SLAB : (i + 1) * SLAB].astype(BF)

    def store_wide(stream, place, value):
        store_grad(stream, place, value[:, :128])
        store_grad(stream, place + 1, value[:, 128:])

    stat_row = iota((8, 128), 0)
    for stream in range(2):
        grads[stream, :, CHUNK:CHUNK_PAD, :] = jnp.zeros((64, CHUNK_PAD - CHUNK, 128), BF)

    def store_stats(stream, lines):
        halves = []
        for line in lines:
            halves += [line[:, i : i + 128] for i in range(0, line.shape[1], 128)]
        for c, line in enumerate(halves):
            high, low = split_two(line)
            both = jnp.where(
                stat_row == 2 * micro, high.astype(F32), jnp.where(stat_row == 2 * micro + 1, low.astype(F32), 0.0)
            )
            grads[stream, STAT_AT + c, CHUNK:CHUNK_PAD, :] = both.astype(BF)

    stores = []

    def send_out(stream, first_chunk, last_chunk):
        number = len(stores)
        chunks = pl.ds(first_chunk, last_chunk - first_chunk)
        copies = [
            pltpu.make_async_copy(grads.at[stream, chunks], ref.at[chunks], store_sem.at[number])
            for ref in (keep_ref, send_ref)
        ]
        stores.append(copies[0])
        pl.when(micro == stream)(copies[0].start)
        pl.when(micro != stream)(copies[1].start)

    def forward(k):
        x = x_buf[k].astype(F32)
        inv = lax.rsqrt(jnp.mean(x * x, axis=-1, keepdims=True) + EPS)
        inv_one[k] = inv
        normed = (x * inv * gain(k, 0)).astype(BF)
        normed_buf[k] = normed
        if k == 0:
            loads[0].wait()
            loads[1].wait()
        for j in range(3):
            packed_buf[k, j] = nn(normed, w_qkv[k, :, j * WIDTH : (j + 1) * WIDTH]).astype(BF)
        for w in range(GROUP):
            rows = slice(w * WIN, (w + 1) * WIN)
            scores = nt(packed_buf[k, 0, rows, :], expand(packed_buf[k, 1, rows, :]))
            score_buf[rows, :] = jnp.where(mask_buf[k, w : w + 1, :] > 0.5, scores * HEAD**-0.5, fills[k][w])
        scores = score_buf[...]
        weights = jnp.exp(scores - group_max(scores, same_head))
        prob = weights / group_sum(weights, same_head)
        prob_buf[k] = prob
        prob_low = prob.astype(BF)
        for w in range(GROUP):
            rows = slice(w * WIN, (w + 1) * WIN)
            mixed_buf[k, rows, :] = nn(window(prob_low, w), expand(packed_buf[k, 2, rows, :])).astype(BF)
        if k == 0:
            loads[2].wait()
            loads[3].wait()
        after = x + nn(mixed_buf[k], w_out[k])
        after_buf[k] = after
        inv = lax.rsqrt(jnp.mean(after * after, axis=-1, keepdims=True) + EPS)
        inv_two[k] = inv
        normed_two = (after * inv * gain(k, 1)).astype(BF)
        normed_two_buf[k] = normed_two
        if k == 0:
            for load in loads[4:]:
                load.wait()
        total = after
        for j in range(4):
            cols = slice(j * WIDTH, (j + 1) * WIDTH)
            up = nn(normed_two, w_up[k, :, cols])
            root = math.sqrt(2.0 / math.pi)
            square = up * up
            half = 0.5 * jnp.tanh(up * (root + (root * 0.044715) * square)) + 0.5
            hidden = (up * half).astype(BF)
            hidden_buf[k, j] = hidden
            bend = up * (2 * root + (6 * root * 0.044715) * square)
            slope_buf[k, j] = half * (1.0 + bend * (1.0 - half))
            total = total + nn(hidden, w_down[k, cols, :])
        return total.astype(BF)

    def norm_back(grad, value, inv, gain_row):
        gain_grad = jnp.sum(grad * value * inv, axis=0, keepdims=True)
        scaled = grad * gain_row
        inner = jnp.mean(scaled * value, axis=-1, keepdims=True)
        return inv * (scaled - value * (inv * inv * inner)), gain_grad

    def backward(k, out_grad, slope, pulled):
        back = None
        down_lines = []
        for j in (2, 3, 0, 1):
            cols = slice(j * WIDTH, (j + 1) * WIDTH)
            if k == 0:
                stream, place = (1, 12 + 2 * j) if j >= 2 else (0, 16 + 2 * j)
                out_low = out_grad.astype(BF)
                store_wide(stream, place, tn(hidden_buf[k, j], out_low))
                hidden_grad = nt(out_low, w_down[k, cols, :]).astype(BF).astype(F32)
            else:
                down_lines.append(jnp.sum(hidden_buf[k, j].astype(F32) * slope, axis=0, keepdims=True))
                hidden_grad = slope * pulled[j]
            up_grad = (slope_buf[k, j] * hidden_grad).astype(BF)
            store_wide(k, 2 * j, tn(normed_two_buf[k], up_grad))
            term = nt(up_grad, w_up[k, :, cols])
            back = term if back is None else back + term
            if k == 0 and j == 3:
                send_out(1, 51, 64)
        if k == 0:
            send_out(0, 0, 25)
            send_out(0, 52, 64)
        normed_two_grad = back.astype(BF).astype(F32)
        res_grad, gain_two_grad = norm_back(normed_two_grad, after_buf[k], inv_two[k], gain(k, 1))
        after_grad = out_grad + res_grad
        after_low = after_grad.astype(BF)
        store_wide(k, 8, tn(mixed_buf[k], after_low))
        mixed_grad = nt(after_low, w_out[k]).astype(BF)
        for w in range(GROUP):
            rows = slice(w * WIN, (w + 1) * WIN)
            score_buf[rows, :] = nt(window(mixed_grad, w), expand(packed_buf[k, 2, rows, :]))
        prob = prob_buf[k]
        prob_low = prob.astype(BF)
        prob_grad = score_buf[...].astype(BF).astype(F32)
        flow = prob * prob_grad
        score_grad = (flow - prob * group_sum(flow, same_head)) * HEAD**-0.5

        lane_head = iota((WIN, 128), 1) // HEAD

        def fold(left, right):
            halves = []
            for side in range(2):
                cols = slice(side * 128, (side + 1) * 128)
                value = tn(left[:, cols], right[:, cols])
                total = window(value, 3)
                for h in range(3):
                    total = jnp.where(lane_head == h, window(value, h), total)
                halves.append(total.astype(BF))
            return jnp.concatenate(halves, axis=1)

        for w in range(GROUP):
            rows = slice(w * WIN, (w + 1) * WIN)
            grad_w = jnp.where(mask_buf[k, w : w + 1, :] > 0.5, window(score_grad, w), 0.0).astype(BF)
            dpacked_buf[0, rows, :] = nn(grad_w, expand(packed_buf[k, 1, rows, :])).astype(BF)
            dpacked_buf[1, rows, :] = fold(grad_w, packed_buf[k, 0, rows, :])
            dpacked_buf[2, rows, :] = fold(window(prob_low, w), window(mixed_grad, w))
        back = None
        for j in range(3):
            piece = dpacked_buf[j]
            store_wide(k, 10 + 2 * j, tn(normed_buf[k], piece))
            term = nt(piece, w_qkv[k, :, j * WIDTH : (j + 1) * WIDTH])
            back = term if back is None else back + term
        normed_grad = back.astype(BF).astype(F32)
        in_res, gain_one_grad = norm_back(normed_grad, x_buf[k].astype(F32), inv_one[k], gain(k, 0))
        return (after_grad + in_res).astype(BF), gain_one_grad, gain_two_grad, down_lines[2:] + down_lines[:2]

    received = received_ref[:, 0:WIN, :].reshape(ROWS, WIDTH)
    x_buf[0] = exchange(received)
    x_buf[1] = exchange(forward(0))
    section_one = forward(1).astype(F32)

    pieces = []
    lane_w = iota((WIN, WIDTH), 1)
    row_w = iota((WIN, WIDTH), 0)
    valid_pieces = []
    for s in range(GROUP):
        parts = received_ref[s, WIN : WIN + 8, :].astype(F32)
        line = parts[0:1] + parts[1:2] + parts[2:3]
        chosen = jnp.where(lane_w == part * WIN + row_w, line, 0.0)
        pieces.append(jnp.sum(chosen, axis=-1, keepdims=True))
        valid_pieces.append(part * WIN + iota((WIN, 1), 0) < count_of[s])
    target = jnp.concatenate(pieces, axis=0)
    valid = jnp.concatenate([jnp.where(v, 1.0, 0.0) for v in valid_pieces], axis=0)
    sdf = sdf_ref[...]
    predicted = jnp.sum(section_one * sdf, axis=-1, keepdims=True)
    residue = jnp.where(valid > 0.5, predicted - target, 0.0)
    slope = 2.0 * residue / math.sqrt(3 * ROWS * 64 // 4)
    loss = jnp.sum(residue * residue, axis=0, keepdims=True)
    sdf_grad = jnp.sum(slope * section_one, axis=0, keepdims=True)
    high = sdf.astype(BF).astype(F32)
    middle = (sdf - high).astype(BF).astype(F32)
    row = iota((16, WIDTH), 0)
    parts = jnp.where(row == 0, high, jnp.where(row == 1, middle, jnp.where(row == 2, sdf - high - middle, 0.0)))
    parts = parts.astype(BF)
    pulled = [
        jnp.sum(nt(parts, w_down[1, j * WIDTH : (j + 1) * WIDTH, :]), axis=0, keepdims=True) for j in range(4)
    ]
    loss_row = jnp.broadcast_to(loss, (1, 128))
    middle_grad, gain_one, gain_two, down_lines = backward(1, slope * sdf, slope, pulled)
    store_stats(1, [gain_one, gain_two, sdf_grad, loss_row] + down_lines)
    send_out(1, 0, 51)
    unused, gain_one, gain_two, none = backward(0, exchange(middle_grad).astype(F32), None, None)
    del unused, none
    store_stats(0, [gain_one, gain_two, sdf_grad, loss_row])
    send_out(0, 25, 52)
    for store in stores:
        store.wait()


def wide(source, first_chunk, place, ref, row, col, slabs=range(ROWS // SLAB)):
    for side in range(2):
        for i in slabs:
            slab = (place + side) * (ROWS // SLAB) + i
            low = slab % 5 * SLAB
            piece = source[slab // 5 - first_chunk, low : low + SLAB, :].astype(F32)
            ref[row + i * SLAB : row + (i + 1) * SLAB, col + side * 128 : col + (side + 1) * 128] = piece


def unpack_kernel(
    in_ref, sdf_row_ref, loss_ref, sdf_ref, gain_one_ref, qkv_hbm, out_hbm, gain_two_ref, up_hbm, down_hbm,
    qkv_ref, out_ref, up_ref, down_ref, store_sem,
):
    micro = lax.axis_index("pipe")
    stores = []

    def store(source, target):
        copy = pltpu.make_async_copy(source, target, store_sem.at[len(stores)])
        copy.start()
        stores.append(copy)

    lines = []
    for c in range(15):
        pair = in_ref[STAT_AT + c, CHUNK:CHUNK_PAD, :].astype(F32)
        lines.append(pair[0:1] + pair[1:2])
    for ref, c in ((gain_one_ref, 0), (gain_two_ref, 2), (sdf_ref, 4)):
        ref[0:1, 0:128] = lines[c]
        ref[0:1, 128:256] = lines[c + 1]
    loss_ref[0:1, :] = lines[6] / (2 * 12288)

    @pl.when(micro == 0)
    def _():
        for j in range(2):
            wide(in_ref, 0, 16 + 2 * j, down_ref, j * WIDTH, 0)

    @pl.when(micro == 1)
    def _():
        diagonal = iota((128, 128), 0) == iota((128, 128), 1)
        for c in range(8):
            column = jnp.sum(jnp.where(diagonal, lines[7 + c], 0.0), axis=1, keepdims=True)
            down_ref[c * 128 : (c + 1) * 128, :] = column * sdf_row_ref[...]

    store(down_ref.at[pl.ds(0, 2 * WIDTH)], down_hbm.at[0, pl.ds(0, 2 * WIDTH)])
    rows = pl.ds(2 * WIDTH, 2 * WIDTH)
    last = pltpu.make_async_copy(down_ref.at[rows], down_hbm.at[0, rows], store_sem.at[13])
    pl.when(micro == 1)(last.start)
    for ref, target, place, count in ((up_ref, up_hbm, 0, 4), (out_ref, out_hbm, 8, 1), (qkv_ref, qkv_hbm, 10, 3)):
        for quarter in range(4):
            for j in range(count):
                wide(in_ref, 0, place + 2 * j, ref, 0, j * WIDTH, range(4 * quarter, 4 * quarter + 4))
            rows = pl.ds(quarter * 64, 64)
            store(ref.at[rows], target.at[0, rows])
    pl.when(micro == 1)(last.wait)
    for copy in stores:
        copy.wait()


def finish_kernel(moved_hbm, down_in, down_out, moved_ref, half_ref, sem):
    del down_in

    @pl.when(lax.axis_index("pipe") == 0)
    def _():
        load = pltpu.make_async_copy(moved_hbm, moved_ref, sem.at[0])
        load.start()
        load.wait()
        for j in range(2):
            wide(moved_ref, 51, 16 + 2 * j, half_ref, j * WIDTH, 0)
        store = pltpu.make_async_copy(half_ref, down_out.at[0, pl.ds(2 * WIDTH, 2 * WIDTH)], sem.at[1])
        store.start()
        store.wait()


def fix(value):
    return pltpu.with_memory_space_constraint(value, pltpu.HBM)


def swap_pipe(value):
    return lax.ppermute(value, "pipe", [(0, 1), (1, 0)])


VMEM = pl.BlockSpec(memory_space=pltpu.VMEM)
ANY = pl.BlockSpec(memory_space=pl.ANY)
HBM = pl.BlockSpec(memory_space=pltpu.HBM)


def shards(
    features, coarse, parent, counts, target, gain_attn, w_qkv, w_out, gain_mlp, w_up, w_down, w_sdf
):
    rank_count = lax.axis_size("tok")
    rim = lax.ppermute(coarse[:, -1:, :], "tok", [(i, i + 1) for i in range(rank_count - 1)])
    arrived = []
    for value in (gain_attn, gain_mlp, w_qkv, w_out, w_up, w_down):
        arrived.append(swap_pipe(value))
    gains_far = arrived[:2]
    qkv_far, out_far, up_far, down_far = arrived[2:]
    embedded, rim_hot = pl.pallas_call(
        embed_kernel,
        out_shape=(
            jax.ShapeDtypeStruct((GROUP, SEND_ROWS, WIDTH), BF),
            jax.ShapeDtypeStruct((16, ROWS), BF),
        ),
        in_specs=[HBM] * 4,
        out_specs=(VMEM, VMEM),
        scratch_shapes=[
            pltpu.VMEM((ROWS, WIDTH), BF),
            pltpu.VMEM((64, WIDTH), BF),
            pltpu.VMEM((2, ROWS), jnp.int32),
            pltpu.VMEM((2, ROWS), F32),
            pltpu.SemaphoreType.DMA((4,)),
        ],
        name="embed",
        compiler_params=pltpu.CompilerParams(vmem_limit_bytes=4 * 2**20),
    )(fix(features), fix(coarse), fix(parent), fix(target))
    outgoing = pl.pallas_call(
        rim_kernel,
        out_shape=jax.ShapeDtypeStruct((GROUP, SEND_ROWS, WIDTH), BF),
        in_specs=[VMEM] * 3,
        out_specs=VMEM,
        name="add_rim",
        compiler_params=pltpu.CompilerParams(vmem_limit_bytes=4 * 2**20),
    )(embedded, rim_hot, rim)
    groups = [[b * GROUP + i for i in range(GROUP)] for b in range(rank_count // GROUP)]
    received = lax.all_to_all(outgoing, "tok", 0, 0, axis_index_groups=groups, tiled=True)
    packet = jax.ShapeDtypeStruct((64, CHUNK_PAD, 128), BF)
    keep, send = pl.pallas_call(
        step_kernel,
        out_shape=(packet, packet),
        in_specs=[HBM] + [VMEM] * 3 + [HBM] * 3 + [HBM, ANY] * 4,
        out_specs=(ANY, ANY),
        scratch_shapes=[
            pltpu.VMEM((2, WIDTH, 3 * WIDTH), BF),
            pltpu.VMEM((2, WIDTH, WIDTH), BF),
            pltpu.VMEM((2, WIDTH, FF), BF),
            pltpu.VMEM((2, FF, WIDTH), BF),
            pltpu.VMEM((2, ROWS, WIDTH), BF),
            pltpu.VMEM((2, ROWS, 1), F32),
            pltpu.VMEM((2, ROWS, WIDTH), BF),
            pltpu.VMEM((2, 3, ROWS, WIDTH), BF),
            pltpu.VMEM((2, ROWS, WIDTH), F32),
            pltpu.VMEM((2, ROWS, WIDTH), BF),
            pltpu.VMEM((2, ROWS, WIDTH), F32),
            pltpu.VMEM((2, ROWS, 1), F32),
            pltpu.VMEM((2, ROWS, WIDTH), BF),
            pltpu.VMEM((2, 4, ROWS, WIDTH), F32),
            pltpu.VMEM((2, 4, ROWS, WIDTH), BF),
            pltpu.VMEM((2, GROUP, WIDTH), F32),
            pltpu.VMEM((2, 64, CHUNK_PAD, 128), BF),
            pltpu.VMEM((ROWS, WIDTH), F32),
            pltpu.VMEM((3, ROWS, WIDTH), BF),
            pltpu.VMEM((1, WIDTH), F32),
            pltpu.VMEM((1, WIDTH), F32),
            pltpu.VMEM((1, WIDTH), F32),
            pltpu.SMEM((2, 64), jnp.int32),
            pltpu.SemaphoreType.DMA((12,)),
            pltpu.SemaphoreType.DMA((5,)),
        ],
        name="step",
        compiler_params=pltpu.CompilerParams(vmem_limit_bytes=32 * 2**20),
    )(fix(counts), received, *gains_far, fix(w_sdf[None]), fix(gain_attn), fix(gain_mlp), fix(w_qkv), qkv_far, fix(w_out), out_far, fix(w_up), up_far, fix(w_down), down_far)
    far = swap_pipe(send)
    total = (keep.astype(F32) + far.astype(F32)).astype(BF)
    shares = lax.all_to_all(total, "tok", 0, 0, tiled=True)
    summed = jnp.sum(shares.astype(F32), axis=0)
    stat = jnp.sum(summed[CHUNK : CHUNK + 4], axis=0, keepdims=True)
    high = lax.reduce_precision(stat, 8, 7)
    row = iota((CHUNK_PAD, 128), 0)
    tail = jnp.where(row == CHUNK, high, jnp.where(row == CHUNK + 1, stat - high, 0.0))
    summed = jnp.where(row < CHUNK, summed, tail).astype(BF)
    gathered = lax.all_to_all(
        jnp.broadcast_to(summed[None], (rank_count, CHUNK_PAD, 128)), "tok", 0, 0, tiled=True
    )
    moved = lax.ppermute(gathered[51:64], "pipe", [(1, 0)])
    loss, sdf, gain_one, qkv, out, gain_two, up, down = pl.pallas_call(
        unpack_kernel,
        out_shape=(
            jax.ShapeDtypeStruct((1, 128), F32),
            jax.ShapeDtypeStruct((1, WIDTH), F32),
            jax.ShapeDtypeStruct((1, WIDTH), F32),
            jax.ShapeDtypeStruct((1, WIDTH, 3 * WIDTH), F32),
            jax.ShapeDtypeStruct((1, WIDTH, WIDTH), F32),
            jax.ShapeDtypeStruct((1, WIDTH), F32),
            jax.ShapeDtypeStruct((1, WIDTH, FF), F32),
            jax.ShapeDtypeStruct((1, FF, WIDTH), F32),
        ),
        in_specs=[VMEM, VMEM],
        out_specs=(VMEM, VMEM, VMEM, HBM, HBM, VMEM, HBM, HBM),
        scratch_shapes=[
            pltpu.VMEM((WIDTH, 3 * WIDTH), F32),
            pltpu.VMEM((WIDTH, WIDTH), F32),
            pltpu.VMEM((WIDTH, FF), F32),
            pltpu.VMEM((FF, WIDTH), F32),
            pltpu.SemaphoreType.DMA((14,)),
        ],
        name="unpack",
        compiler_params=pltpu.CompilerParams(vmem_limit_bytes=16 * 2**20),
    )(gathered, fix(w_sdf[None]))
    down = pl.pallas_call(
        finish_kernel,
        out_shape=jax.ShapeDtypeStruct((1, FF, WIDTH), F32),
        in_specs=[ANY, HBM],
        out_specs=HBM,
        scratch_shapes=[
            pltpu.VMEM((13, CHUNK_PAD, 128), BF),
            pltpu.VMEM((2 * WIDTH, WIDTH), F32),
            pltpu.SemaphoreType.DMA((2,)),
        ],
        input_output_aliases={1: 0},
        name="finish",
        compiler_params=pltpu.CompilerParams(vmem_limit_bytes=16 * 2**20),
    )(moved, down)
    return loss[0, 0], sdf[0], gain_one, qkv, out, gain_two, up, down


def solution(mesh):
    return jax.shard_map(
        shards,
        mesh=mesh,
        in_specs=(
            P(None, "tok", None),
            P(None, "tok", None),
            P(None, "tok"),
            P(),
            P(None, "tok"),
            P("pipe", None),
            P("pipe", None, None),
            P("pipe", None, None),
            P("pipe", None),
            P("pipe", None, None),
            P("pipe", None, None),
            P(),
        ),
        out_specs=(
            P(),
            P(),
            P("pipe", None),
            P("pipe", None, None),
            P("pipe", None, None),
            P("pipe", None),
            P("pipe", None, None),
            P("pipe", None, None),
        ),
        check_vma=False,
    )
```

```python
import functools
import math

import jax
import jax.numpy as jnp
from jax import lax
from jax.experimental import pallas as pl
from jax.experimental.pallas import tpu as pltpu
from jax.sharding import PartitionSpec as P


H = 8
WIN = 32
GROUP = 8
ROWS = 256
WIDTH = 256
FF = 1024
HEAD = WIDTH // H
EPS = 1e-06
CHUNK = 80
CHUNK_PAD = 88
SLAB = 16
STAT_AT = 25
SEND_ROWS = 40
BF = jnp.bfloat16
F32 = jnp.float32


def nn(a, b):
    return jnp.dot(a, b, preferred_element_type=F32)


def nt(a, b):
    return lax.dot_general(a, b, (((1,), (1,)), ((), ())), preferred_element_type=F32)


def tn(a, b):
    return lax.dot_general(a, b, (((0,), (0,)), ((), ())), preferred_element_type=F32)


def iota(shape, dim):
    return lax.broadcasted_iota(jnp.int32, shape, dim)


def split_two(value):
    high = value.astype(BF)
    low = (value - high.astype(F32)).astype(BF)
    return high, low


def embed_kernel(
    features_hbm, coarse_hbm, parent_hbm, target_hbm, out_ref, rim_hot_ref,
    features_ref, coarse_ref, parent_ref, target_ref, load_sem,
):
    micro = lax.axis_index("pipe")
    shard = lax.axis_index("tok")
    loads = [
        pltpu.make_async_copy(source, held, load_sem.at[number])
        for number, (source, held) in enumerate(
            (
                (features_hbm.at[micro], features_ref),
                (coarse_hbm.at[micro], coarse_ref),
                (parent_hbm, parent_ref),
                (target_hbm, target_ref),
            )
        )
    ]
    for load in loads:
        load.start()
    for load in loads:
        load.wait()
    local = parent_ref[pl.ds(micro, 1), :] - shard * 64
    own_hot = jnp.where(iota((64, ROWS), 0) == local, 1.0, 0.0).astype(BF)
    rim_hot_ref[...] = jnp.where((iota((16, ROWS), 0) == 0) & (local == -1), 1.0, 0.0).astype(BF)
    embedded = (features_ref[...].astype(F32) + tn(own_hot, coarse_ref[...])).astype(BF)
    target = jnp.broadcast_to(target_ref[pl.ds(micro, 1), :], (8, ROWS))
    high = target.astype(BF).astype(F32)
    middle = (target - high).astype(BF).astype(F32)
    low = target - high - middle
    row = iota((8, ROWS), 0)
    extra = jnp.where(row == 0, high, jnp.where(row == 1, middle, jnp.where(row == 2, low, 0.0)))
    extra = extra.astype(BF)
    for part in range(GROUP):
        out_ref[part, 0:WIN, :] = embedded[part * WIN : (part + 1) * WIN]
        out_ref[part, WIN:SEND_ROWS, :] = extra


def rim_kernel(embedded_ref, rim_hot_ref, rim_ref, out_ref):
    rim = jnp.broadcast_to(rim_ref[lax.axis_index("pipe")], (16, WIDTH))
    lifted = tn(rim_hot_ref[...], rim)
    for part in range(GROUP):
        rows = slice(part * WIN, (part + 1) * WIN)
        out_ref[part, 0:WIN, :] = (embedded_ref[part, 0:WIN, :].astype(F32) + lifted[rows]).astype(BF)
        out_ref[part, WIN:SEND_ROWS, :] = embedded_ref[part, WIN:SEND_ROWS, :]


def group_max(values, same_head):
    lane = iota((1, 128), 1)
    halves = []
    for side in range(2):
        half = values[:, side * 128 : (side + 1) * 128]
        for step in (1, 2, 4, 8, 16):
            half = jnp.maximum(half, pltpu.roll(half, step, 1))
        halves.append(jnp.where(lane % WIN == WIN - 1, half, 0.0))
    return group_sum(jnp.concatenate(halves, axis=1), same_head)


def group_sum(values, same_head):
    high, low = split_two(values)
    return nn(high, same_head) + nn(low, same_head)


def arrange_kernel(
    gain_far_one, gain_far_two, counts_hbm, sdf_hbm, gain_own_one_hbm, gain_own_two_hbm,
    qkv_own, qkv_far, out_own, out_far, up_own, up_far, down_own, down_far,
    w_qkv, w_out, w_up, w_down, mask_ref, fill_ref, rows_ref,
    sdf_ref, gain_own_one, gain_own_two, counts_ref, load_sem,
):
    micro = lax.axis_index("pipe")
    shard = lax.axis_index("tok")
    part = lax.rem(shard, GROUP)
    first = shard - part
    moves = [
        (sdf_hbm, sdf_ref),
        (gain_own_one_hbm, gain_own_one),
        (gain_own_two_hbm, gain_own_two),
        (counts_hbm, counts_ref),
    ]
    for own, far, held in (
        (qkv_own, qkv_far, w_qkv), (out_own, out_far, w_out), (up_own, up_far, w_up), (down_own, down_far, w_down)
    ):
        moves += [(own.at[0], held.at[micro]), (far.at[0], held.at[1 - micro])]
    loads = [
        pltpu.make_async_copy(source, held, load_sem.at[number]) for number, (source, held) in enumerate(moves)
    ]
    for load in loads:
        load.start()
    for load in loads[:4]:
        load.wait()
    own_is_first = micro == 0
    row = iota((8, WIDTH), 0)
    rows = jnp.where(row == 4, sdf_ref[...], 0.0)
    for which, (own, far) in enumerate(((gain_own_one, gain_far_one), (gain_own_two, gain_far_two))):
        rows = jnp.where(row == which, jnp.where(own_is_first, own[...], far[...]), rows)
        rows = jnp.where(row == 2 + which, jnp.where(own_is_first, far[...], own[...]), rows)
    rows_ref[...] = rows
    key = iota((1, WIDTH), 1) % WIN
    count_of = [counts_ref[micro, first + s] for s in range(GROUP)]
    most = functools.reduce(jnp.maximum, count_of)
    lane_count = jnp.zeros((1, WIDTH), jnp.int32)
    for s in range(GROUP):
        lane_count = jnp.where(key // 4 == s, count_of[s], lane_count)
    for w in range(GROUP):
        dilated = part * WIN + w * 4 + key % 4 < lane_count
        plain = part * WIN + key < count_of[w]
        mask_ref[0, w : w + 1, :] = jnp.where(dilated, 1.0, 0.0)
        mask_ref[1, w : w + 1, :] = jnp.where(plain, 1.0, 0.0)
        blank = jnp.zeros((1, WIDTH), F32)
        fill_ref[0, w : w + 1, :] = jnp.where(part * WIN + w * 4 < most, blank - 1e30, blank)
        fill_ref[1, w : w + 1, :] = jnp.where(part * WIN < count_of[w], blank - 1e30, blank)
    for load in loads[4:]:
        load.wait()


def step_kernel(
    received_ref, w_qkv, w_out, w_up, w_down, mask_buf, fill_buf, rows_ref,
    keep_ref, send_ref,
    x_buf, inv_one, normed_buf, packed_buf, prob_buf, mixed_buf, after_buf, inv_two,
    normed_two_buf, slope_buf, hidden_buf, grads, score_buf, dpacked_buf, store_sem,
):
    micro = lax.axis_index("pipe")
    part = lax.rem(lax.axis_index("tok"), GROUP)

    def gain(section, which):
        number = 2 * section + which
        return rows_ref[number : number + 1, :]

    row_i = iota((ROWS, WIDTH), 0)
    col_i = iota((ROWS, WIDTH), 1)
    same_head = jnp.where(row_i // WIN == col_i // HEAD, 1.0, 0.0).astype(BF)
    swapped = row_i % WIN // 4 * WIN + row_i // WIN * 4 + row_i % 4
    swap = jnp.where(swapped == col_i, 1.0, 0.0).astype(BF)

    def exchange(value):
        return nn(swap, value).astype(BF)

    def expand(value):
        return jnp.concatenate([value] * H, axis=0) * same_head

    def window(value, w):
        return value[w * WIN : (w + 1) * WIN]

    def store_grad(stream, place, value):
        for i in range(ROWS // SLAB):
            slab = place * (ROWS // SLAB) + i
            base = slab % 5 * SLAB
            grads[stream, slab // 5, base : base + SLAB, :] = value[i * SLAB : (i + 1) * SLAB].astype(BF)

    def store_wide(stream, place, value):
        store_grad(stream, place, value[:, :128])
        store_grad(stream, place + 1, value[:, 128:])

    stat_row = iota((8, 128), 0)
    for stream in range(2):
        grads[stream, :, CHUNK:CHUNK_PAD, :] = jnp.zeros((64, CHUNK_PAD - CHUNK, 128), BF)

    def store_stats(stream, lines):
        halves = []
        for line in lines:
            halves += [line[:, i : i + 128] for i in range(0, line.shape[1], 128)]
        for c, line in enumerate(halves):
            high, low = split_two(line)
            both = jnp.where(
                stat_row == 2 * micro, high.astype(F32), jnp.where(stat_row == 2 * micro + 1, low.astype(F32), 0.0)
            )
            grads[stream, STAT_AT + c, CHUNK:CHUNK_PAD, :] = both.astype(BF)

    stores = []

    def send_out(stream, first_chunk, last_chunk):
        number = len(stores)
        chunks = pl.ds(first_chunk, last_chunk - first_chunk)
        copies = [
            pltpu.make_async_copy(grads.at[stream, chunks], ref.at[chunks], store_sem.at[number])
            for ref in (keep_ref, send_ref)
        ]
        stores.append(copies[0])
        pl.when(micro == stream)(copies[0].start)
        pl.when(micro != stream)(copies[1].start)

    def forward(k):
        x = x_buf[k].astype(F32)
        inv = lax.rsqrt(jnp.mean(x * x, axis=-1, keepdims=True) + EPS)
        inv_one[k] = inv
        normed = (x * inv * gain(k, 0)).astype(BF)
        normed_buf[k] = normed
        for j in range(3):
            packed_buf[k, j] = nn(normed, w_qkv[k, :, j * WIDTH : (j + 1) * WIDTH]).astype(BF)
        for w in range(GROUP):
            rows = slice(w * WIN, (w + 1) * WIN)
            scores = nt(packed_buf[k, 0, rows, :], expand(packed_buf[k, 1, rows, :]))
            score_buf[rows, :] = jnp.where(mask_buf[k, w : w + 1, :] > 0.5, scores * HEAD**-0.5, fill_buf[k, w : w + 1, :])
        scores = score_buf[...]
        weights = jnp.exp(scores - group_max(scores, same_head))
        prob = weights / group_sum(weights, same_head)
        prob_buf[k] = prob
        prob_low = prob.astype(BF)
        for w in range(GROUP):
            rows = slice(w * WIN, (w + 1) * WIN)
            mixed_buf[k, rows, :] = nn(window(prob_low, w), expand(packed_buf[k, 2, rows, :])).astype(BF)
        after = x + nn(mixed_buf[k], w_out[k])
        after_buf[k] = after
        inv = lax.rsqrt(jnp.mean(after * after, axis=-1, keepdims=True) + EPS)
        inv_two[k] = inv
        normed_two = (after * inv * gain(k, 1)).astype(BF)
        normed_two_buf[k] = normed_two
        total = after
        for j in range(4):
            cols = slice(j * WIDTH, (j + 1) * WIDTH)
            up = nn(normed_two, w_up[k, :, cols])
            root = math.sqrt(2.0 / math.pi)
            square = up * up
            half = 0.5 * jnp.tanh(up * (root + (root * 0.044715) * square)) + 0.5
            hidden = (up * half).astype(BF)
            hidden_buf[k, j] = hidden
            bend = up * (2 * root + (6 * root * 0.044715) * square)
            slope_buf[k, j] = half * (1.0 + bend * (1.0 - half))
            total = total + nn(hidden, w_down[k, cols, :])
        return total.astype(BF)

    def norm_back(grad, value, inv, gain_row):
        gain_grad = jnp.sum(grad * value * inv, axis=0, keepdims=True)
        scaled = grad * gain_row
        inner = jnp.mean(scaled * value, axis=-1, keepdims=True)
        return inv * (scaled - value * (inv * inv * inner)), gain_grad

    def backward(k, out_grad, slope, pulled):
        back = None
        down_lines = []
        for j in (2, 3, 0, 1):
            cols = slice(j * WIDTH, (j + 1) * WIDTH)
            if k == 0:
                stream, place = (1, 12 + 2 * j) if j >= 2 else (0, 16 + 2 * j)
                out_low = out_grad.astype(BF)
                store_wide(stream, place, tn(hidden_buf[k, j], out_low))
                hidden_grad = nt(out_low, w_down[k, cols, :]).astype(BF).astype(F32)
            else:
                down_lines.append(jnp.sum(hidden_buf[k, j].astype(F32) * slope, axis=0, keepdims=True))
                hidden_grad = slope * pulled[j]
            up_grad = (slope_buf[k, j] * hidden_grad).astype(BF)
            store_wide(k, 2 * j, tn(normed_two_buf[k], up_grad))
            term = nt(up_grad, w_up[k, :, cols])
            back = term if back is None else back + term
            if k == 0 and j == 3:
                send_out(1, 51, 64)
        if k == 0:
            send_out(0, 0, 25)
            send_out(0, 52, 64)
        normed_two_grad = back.astype(BF).astype(F32)
        res_grad, gain_two_grad = norm_back(normed_two_grad, after_buf[k], inv_two[k], gain(k, 1))
        after_grad = out_grad + res_grad
        after_low = after_grad.astype(BF)
        store_wide(k, 8, tn(mixed_buf[k], after_low))
        mixed_grad = nt(after_low, w_out[k]).astype(BF)
        for w in range(GROUP):
            rows = slice(w * WIN, (w + 1) * WIN)
            score_buf[rows, :] = nt(window(mixed_grad, w), expand(packed_buf[k, 2, rows, :]))
        prob = prob_buf[k]
        prob_low = prob.astype(BF)
        prob_grad = score_buf[...].astype(BF).astype(F32)
        flow = prob * prob_grad
        score_grad = (flow - prob * group_sum(flow, same_head)) * HEAD**-0.5

        lane_head = iota((WIN, 128), 1) // HEAD

        def fold(left, right):
            halves = []
            for side in range(2):
                cols = slice(side * 128, (side + 1) * 128)
                value = tn(left[:, cols], right[:, cols])
                total = window(value, 3)
                for h in range(3):
                    total = jnp.where(lane_head == h, window(value, h), total)
                halves.append(total.astype(BF))
            return jnp.concatenate(halves, axis=1)

        for w in range(GROUP):
            rows = slice(w * WIN, (w + 1) * WIN)
            grad_w = jnp.where(mask_buf[k, w : w + 1, :] > 0.5, window(score_grad, w), 0.0).astype(BF)
            dpacked_buf[0, rows, :] = nn(grad_w, expand(packed_buf[k, 1, rows, :])).astype(BF)
            dpacked_buf[1, rows, :] = fold(grad_w, packed_buf[k, 0, rows, :])
            dpacked_buf[2, rows, :] = fold(window(prob_low, w), window(mixed_grad, w))
        back = None
        for j in range(3):
            piece = dpacked_buf[j]
            store_wide(k, 10 + 2 * j, tn(normed_buf[k], piece))
            term = nt(piece, w_qkv[k, :, j * WIDTH : (j + 1) * WIDTH])
            back = term if back is None else back + term
        normed_grad = back.astype(BF).astype(F32)
        in_res, gain_one_grad = norm_back(normed_grad, x_buf[k].astype(F32), inv_one[k], gain(k, 0))
        return (after_grad + in_res).astype(BF), gain_one_grad, gain_two_grad, down_lines[2:] + down_lines[:2]

    received = received_ref[:, 0:WIN, :].reshape(ROWS, WIDTH)
    x_buf[0] = exchange(received)
    x_buf[1] = exchange(forward(0))
    section_one = forward(1).astype(F32)

    pieces = []
    lane_w = iota((WIN, WIDTH), 1)
    row_w = iota((WIN, WIDTH), 0)
    valid_pieces = []
    for s in range(GROUP):
        parts = received_ref[s, WIN : WIN + 8, :].astype(F32)
        line = parts[0:1] + parts[1:2] + parts[2:3]
        chosen = jnp.where(lane_w == part * WIN + row_w, line, 0.0)
        pieces.append(jnp.sum(chosen, axis=-1, keepdims=True))
        valid_pieces.append(
            jnp.sum(jnp.where(lane_w == row_w, mask_buf[1, s : s + 1, :], 0.0), axis=-1, keepdims=True)
        )
    target = jnp.concatenate(pieces, axis=0)
    valid = jnp.concatenate(valid_pieces, axis=0)
    sdf = rows_ref[4:5, :]
    predicted = jnp.sum(section_one * sdf, axis=-1, keepdims=True)
    residue = jnp.where(valid > 0.5, predicted - target, 0.0)
    slope = 2.0 * residue / math.sqrt(3 * ROWS * 64 // 4)
    loss = jnp.sum(residue * residue, axis=0, keepdims=True)
    sdf_grad = jnp.sum(slope * section_one, axis=0, keepdims=True)
    high = sdf.astype(BF).astype(F32)
    middle = (sdf - high).astype(BF).astype(F32)
    row = iota((16, WIDTH), 0)
    parts = jnp.where(row == 0, high, jnp.where(row == 1, middle, jnp.where(row == 2, sdf - high - middle, 0.0)))
    parts = parts.astype(BF)
    pulled = [
        jnp.sum(nt(parts, w_down[1, j * WIDTH : (j + 1) * WIDTH, :]), axis=0, keepdims=True) for j in range(4)
    ]
    loss_row = jnp.broadcast_to(loss, (1, 128))
    middle_grad, gain_one, gain_two, down_lines = backward(1, slope * sdf, slope, pulled)
    store_stats(1, [gain_one, gain_two, sdf_grad, loss_row] + down_lines)
    send_out(1, 0, 51)
    unused, gain_one, gain_two, none = backward(0, exchange(middle_grad).astype(F32), None, None)
    del unused, none
    store_stats(0, [gain_one, gain_two, sdf_grad, loss_row])
    send_out(0, 25, 52)
    for store in stores:
        store.wait()


def wide(source, first_chunk, place, ref, row, col, slabs=range(ROWS // SLAB)):
    for side in range(2):
        for i in slabs:
            slab = (place + side) * (ROWS // SLAB) + i
            low = slab % 5 * SLAB
            piece = source[slab // 5 - first_chunk, low : low + SLAB, :].astype(F32)
            ref[row + i * SLAB : row + (i + 1) * SLAB, col + side * 128 : col + (side + 1) * 128] = piece


def unpack_kernel(
    in_ref, sdf_row_ref, loss_ref, sdf_ref, gain_one_ref, qkv_hbm, out_hbm, gain_two_ref, up_hbm, down_hbm,
    qkv_ref, out_ref, up_ref, down_ref, store_sem,
):
    micro = lax.axis_index("pipe")
    stores = []

    def store(source, target):
        copy = pltpu.make_async_copy(source, target, store_sem.at[len(stores)])
        copy.start()
        stores.append(copy)

    lines = []
    for c in range(15):
        pair = in_ref[STAT_AT + c, CHUNK:CHUNK_PAD, :].astype(F32)
        lines.append(pair[0:1] + pair[1:2])
    for ref, c in ((gain_one_ref, 0), (gain_two_ref, 2), (sdf_ref, 4)):
        ref[0:1, 0:128] = lines[c]
        ref[0:1, 128:256] = lines[c + 1]
    loss_ref[0:1, :] = lines[6] / (2 * 12288)

    @pl.when(micro == 0)
    def _():
        for j in range(2):
            wide(in_ref, 0, 16 + 2 * j, down_ref, j * WIDTH, 0)

    @pl.when(micro == 1)
    def _():
        diagonal = iota((128, 128), 0) == iota((128, 128), 1)
        for c in range(8):
            column = jnp.sum(jnp.where(diagonal, lines[7 + c], 0.0), axis=1, keepdims=True)
            down_ref[c * 128 : (c + 1) * 128, :] = column * sdf_row_ref[...]

    store(down_ref.at[pl.ds(0, 2 * WIDTH)], down_hbm.at[0, pl.ds(0, 2 * WIDTH)])
    rows = pl.ds(2 * WIDTH, 2 * WIDTH)
    last = pltpu.make_async_copy(down_ref.at[rows], down_hbm.at[0, rows], store_sem.at[13])
    pl.when(micro == 1)(last.start)
    for ref, target, place, count in ((up_ref, up_hbm, 0, 4), (out_ref, out_hbm, 8, 1), (qkv_ref, qkv_hbm, 10, 3)):
        for quarter in range(4):
            for j in range(count):
                wide(in_ref, 0, place + 2 * j, ref, 0, j * WIDTH, range(4 * quarter, 4 * quarter + 4))
            rows = pl.ds(quarter * 64, 64)
            store(ref.at[rows], target.at[0, rows])
    pl.when(micro == 1)(last.wait)
    for copy in stores:
        copy.wait()


def finish_kernel(moved_hbm, down_in, down_out, moved_ref, half_ref, sem):
    del down_in

    @pl.when(lax.axis_index("pipe") == 0)
    def _():
        load = pltpu.make_async_copy(moved_hbm, moved_ref, sem.at[0])
        load.start()
        load.wait()
        for j in range(2):
            wide(moved_ref, 51, 16 + 2 * j, half_ref, j * WIDTH, 0)
        store = pltpu.make_async_copy(half_ref, down_out.at[0, pl.ds(2 * WIDTH, 2 * WIDTH)], sem.at[1])
        store.start()
        store.wait()


def fix(value):
    return pltpu.with_memory_space_constraint(value, pltpu.HBM)


def swap_pipe(value):
    return lax.ppermute(value, "pipe", [(0, 1), (1, 0)])


VMEM = pl.BlockSpec(memory_space=pltpu.VMEM)
ANY = pl.BlockSpec(memory_space=pl.ANY)
HBM = pl.BlockSpec(memory_space=pltpu.HBM)


def shards(
    features, coarse, parent, counts, target, gain_attn, w_qkv, w_out, gain_mlp, w_up, w_down, w_sdf
):
    rank_count = lax.axis_size("tok")
    rim = lax.ppermute(coarse[:, -1:, :], "tok", [(i, i + 1) for i in range(rank_count - 1)])
    arrived = []
    for value in (gain_attn, gain_mlp, w_qkv, w_out, w_up, w_down):
        arrived.append(swap_pipe(value))
    gains_far = arrived[:2]
    qkv_far, out_far, up_far, down_far = arrived[2:]
    embedded, rim_hot = pl.pallas_call(
        embed_kernel,
        out_shape=(
            jax.ShapeDtypeStruct((GROUP, SEND_ROWS, WIDTH), BF),
            jax.ShapeDtypeStruct((16, ROWS), BF),
        ),
        in_specs=[HBM] * 4,
        out_specs=(VMEM, VMEM),
        scratch_shapes=[
            pltpu.VMEM((ROWS, WIDTH), BF),
            pltpu.VMEM((64, WIDTH), BF),
            pltpu.VMEM((2, ROWS), jnp.int32),
            pltpu.VMEM((2, ROWS), F32),
            pltpu.SemaphoreType.DMA((4,)),
        ],
        name="embed",
        compiler_params=pltpu.CompilerParams(vmem_limit_bytes=4 * 2**20),
    )(fix(features), fix(coarse), fix(parent), fix(target))
    outgoing = pl.pallas_call(
        rim_kernel,
        out_shape=jax.ShapeDtypeStruct((GROUP, SEND_ROWS, WIDTH), BF),
        in_specs=[VMEM] * 3,
        out_specs=VMEM,
        name="add_rim",
        compiler_params=pltpu.CompilerParams(vmem_limit_bytes=4 * 2**20),
    )(embedded, rim_hot, rim)
    groups = [[b * GROUP + i for i in range(GROUP)] for b in range(rank_count // GROUP)]
    received = lax.all_to_all(outgoing, "tok", 0, 0, axis_index_groups=groups, tiled=True)
    packet = jax.ShapeDtypeStruct((64, CHUNK_PAD, 128), BF)
    arranged = pl.pallas_call(
        arrange_kernel,
        out_shape=(
            jax.ShapeDtypeStruct((2, WIDTH, 3 * WIDTH), BF),
            jax.ShapeDtypeStruct((2, WIDTH, WIDTH), BF),
            jax.ShapeDtypeStruct((2, WIDTH, FF), BF),
            jax.ShapeDtypeStruct((2, FF, WIDTH), BF),
            jax.ShapeDtypeStruct((2, GROUP, WIDTH), F32),
            jax.ShapeDtypeStruct((2, GROUP, WIDTH), F32),
            jax.ShapeDtypeStruct((8, WIDTH), F32),
        ),
        in_specs=[VMEM] * 2 + [HBM] * 4 + [HBM] * 8,
        out_specs=(VMEM,) * 7,
        scratch_shapes=[
            pltpu.VMEM((1, WIDTH), F32),
            pltpu.VMEM((1, WIDTH), F32),
            pltpu.VMEM((1, WIDTH), F32),
            pltpu.SMEM((2, 64), jnp.int32),
            pltpu.SemaphoreType.DMA((12,)),
        ],
        name="arrange",
        compiler_params=pltpu.CompilerParams(vmem_limit_bytes=8 * 2**20),
    )(
        *gains_far, fix(counts), fix(w_sdf[None]), fix(gain_attn), fix(gain_mlp),
        fix(w_qkv), fix(qkv_far), fix(w_out), fix(out_far), fix(w_up), fix(up_far), fix(w_down), fix(down_far),
    )
    keep, send = pl.pallas_call(
        step_kernel,
        out_shape=(packet, packet),
        in_specs=[VMEM] * 8,
        out_specs=(ANY, ANY),
        scratch_shapes=[
            pltpu.VMEM((2, ROWS, WIDTH), BF),
            pltpu.VMEM((2, ROWS, 1), F32),
            pltpu.VMEM((2, ROWS, WIDTH), BF),
            pltpu.VMEM((2, 3, ROWS, WIDTH), BF),
            pltpu.VMEM((2, ROWS, WIDTH), F32),
            pltpu.VMEM((2, ROWS, WIDTH), BF),
            pltpu.VMEM((2, ROWS, WIDTH), F32),
            pltpu.VMEM((2, ROWS, 1), F32),
            pltpu.VMEM((2, ROWS, WIDTH), BF),
            pltpu.VMEM((2, 4, ROWS, WIDTH), F32),
            pltpu.VMEM((2, 4, ROWS, WIDTH), BF),
            pltpu.VMEM((2, 64, CHUNK_PAD, 128), BF),
            pltpu.VMEM((ROWS, WIDTH), F32),
            pltpu.VMEM((3, ROWS, WIDTH), BF),
            pltpu.SemaphoreType.DMA((5,)),
        ],
        name="step",
        compiler_params=pltpu.CompilerParams(vmem_limit_bytes=20 * 2**20),
    )(received, *arranged)
    far = swap_pipe(send)
    total = (keep.astype(F32) + far.astype(F32)).astype(BF)
    shares = lax.all_to_all(total, "tok", 0, 0, tiled=True)
    summed = jnp.sum(shares.astype(F32), axis=0)
    stat = jnp.sum(summed[CHUNK : CHUNK + 4], axis=0, keepdims=True)
    high = lax.reduce_precision(stat, 8, 7)
    row = iota((CHUNK_PAD, 128), 0)
    tail = jnp.where(row == CHUNK, high, jnp.where(row == CHUNK + 1, stat - high, 0.0))
    summed = jnp.where(row < CHUNK, summed, tail).astype(BF)
    gathered = lax.all_to_all(
        jnp.broadcast_to(summed[None], (rank_count, CHUNK_PAD, 128)), "tok", 0, 0, tiled=True
    )
    moved = lax.ppermute(gathered[51:64], "pipe", [(1, 0)])
    loss, sdf, gain_one, qkv, out, gain_two, up, down = pl.pallas_call(
        unpack_kernel,
        out_shape=(
            jax.ShapeDtypeStruct((1, 128), F32),
            jax.ShapeDtypeStruct((1, WIDTH), F32),
            jax.ShapeDtypeStruct((1, WIDTH), F32),
            jax.ShapeDtypeStruct((1, WIDTH, 3 * WIDTH), F32),
            jax.ShapeDtypeStruct((1, WIDTH, WIDTH), F32),
            jax.ShapeDtypeStruct((1, WIDTH), F32),
            jax.ShapeDtypeStruct((1, WIDTH, FF), F32),
            jax.ShapeDtypeStruct((1, FF, WIDTH), F32),
        ),
        in_specs=[VMEM, VMEM],
        out_specs=(VMEM, VMEM, VMEM, HBM, HBM, VMEM, HBM, HBM),
        scratch_shapes=[
            pltpu.VMEM((WIDTH, 3 * WIDTH), F32),
            pltpu.VMEM((WIDTH, WIDTH), F32),
            pltpu.VMEM((WIDTH, FF), F32),
            pltpu.VMEM((FF, WIDTH), F32),
            pltpu.SemaphoreType.DMA((14,)),
        ],
        name="unpack",
        compiler_params=pltpu.CompilerParams(vmem_limit_bytes=16 * 2**20),
    )(gathered, fix(w_sdf[None]))
    down = pl.pallas_call(
        finish_kernel,
        out_shape=jax.ShapeDtypeStruct((1, FF, WIDTH), F32),
        in_specs=[ANY, HBM],
        out_specs=HBM,
        scratch_shapes=[
            pltpu.VMEM((13, CHUNK_PAD, 128), BF),
            pltpu.VMEM((2 * WIDTH, WIDTH), F32),
            pltpu.SemaphoreType.DMA((2,)),
        ],
        input_output_aliases={1: 0},
        name="finish",
        compiler_params=pltpu.CompilerParams(vmem_limit_bytes=16 * 2**20),
    )(moved, down)
    return loss[0, 0], sdf[0], gain_one, qkv, out, gain_two, up, down


def solution(mesh):
    return jax.shard_map(
        shards,
        mesh=mesh,
        in_specs=(
            P(None, "tok", None),
            P(None, "tok", None),
            P(None, "tok"),
            P(),
            P(None, "tok"),
            P("pipe", None),
            P("pipe", None, None),
            P("pipe", None, None),
            P("pipe", None),
            P("pipe", None, None),
            P("pipe", None, None),
            P(),
        ),
        out_specs=(
            P(),
            P(),
            P("pipe", None),
            P("pipe", None, None),
            P("pipe", None, None),
            P("pipe", None),
            P("pipe", None, None),
            P("pipe", None, None),
        ),
        check_vma=False,
    )
```

```python
import functools
import math

import jax
import jax.numpy as jnp
from jax import lax
from jax.experimental import pallas as pl
from jax.experimental.pallas import tpu as pltpu
from jax.sharding import PartitionSpec as P


H = 8
WIN = 32
GROUP = 8
ROWS = 256
WIDTH = 256
FF = 1024
HEAD = WIDTH // H
EPS = 1e-06
CHUNK = 80
CHUNK_PAD = 88
SLAB = 16
STAT_AT = 25
SEND_ROWS = 40
BF = jnp.bfloat16
F32 = jnp.float32


def nn(a, b):
    return jnp.dot(a, b, preferred_element_type=F32)


def nt(a, b):
    return lax.dot_general(a, b, (((1,), (1,)), ((), ())), preferred_element_type=F32)


def tn(a, b):
    return lax.dot_general(a, b, (((0,), (0,)), ((), ())), preferred_element_type=F32)


def iota(shape, dim):
    return lax.broadcasted_iota(jnp.int32, shape, dim)


def split_two(value):
    high = value.astype(BF)
    low = (value - high.astype(F32)).astype(BF)
    return high, low


def embed_kernel(
    features_hbm, coarse_hbm, parent_hbm, target_hbm, out_ref, rim_hot_ref,
    features_ref, coarse_ref, parent_ref, target_ref, load_sem,
):
    micro = lax.axis_index("pipe")
    shard = lax.axis_index("tok")
    loads = [
        pltpu.make_async_copy(source, held, load_sem.at[number])
        for number, (source, held) in enumerate(
            (
                (features_hbm.at[micro], features_ref),
                (coarse_hbm.at[micro], coarse_ref),
                (parent_hbm, parent_ref),
                (target_hbm, target_ref),
            )
        )
    ]
    for load in loads:
        load.start()
    for load in loads:
        load.wait()
    local = parent_ref[pl.ds(micro, 1), :] - shard * 64
    own_hot = jnp.where(iota((64, ROWS), 0) == local, 1.0, 0.0).astype(BF)
    rim_hot_ref[...] = jnp.where((iota((16, ROWS), 0) == 0) & (local == -1), 1.0, 0.0).astype(BF)
    embedded = (features_ref[...].astype(F32) + tn(own_hot, coarse_ref[...])).astype(BF)
    target = jnp.broadcast_to(target_ref[pl.ds(micro, 1), :], (8, ROWS))
    high = target.astype(BF).astype(F32)
    middle = (target - high).astype(BF).astype(F32)
    low = target - high - middle
    row = iota((8, ROWS), 0)
    extra = jnp.where(row == 0, high, jnp.where(row == 1, middle, jnp.where(row == 2, low, 0.0)))
    extra = extra.astype(BF)
    for part in range(GROUP):
        out_ref[part, 0:WIN, :] = embedded[part * WIN : (part + 1) * WIN]
        out_ref[part, WIN:SEND_ROWS, :] = extra


def rim_kernel(embedded_ref, rim_hot_ref, rim_ref, out_ref):
    rim = jnp.broadcast_to(rim_ref[lax.axis_index("pipe")], (16, WIDTH))
    lifted = tn(rim_hot_ref[...], rim)
    for part in range(GROUP):
        rows = slice(part * WIN, (part + 1) * WIN)
        out_ref[part, 0:WIN, :] = (embedded_ref[part, 0:WIN, :].astype(F32) + lifted[rows]).astype(BF)
        out_ref[part, WIN:SEND_ROWS, :] = embedded_ref[part, WIN:SEND_ROWS, :]


def group_max(values, same_head):
    lane = iota((1, 128), 1)
    halves = []
    for side in range(2):
        half = values[:, side * 128 : (side + 1) * 128]
        for step in (1, 2, 4, 8, 16):
            half = jnp.maximum(half, pltpu.roll(half, step, 1))
        halves.append(jnp.where(lane % WIN == WIN - 1, half, 0.0))
    return group_sum(jnp.concatenate(halves, axis=1), same_head)


def group_sum(values, same_head):
    high, low = split_two(values)
    return nn(high, same_head) + nn(low, same_head)


def arrange_kernel(
    gain_far_one, gain_far_two, counts_hbm, sdf_hbm, gain_own_one_hbm, gain_own_two_hbm,
    qkv_own, qkv_far, out_own, out_far, up_own, up_far, down_own, down_far,
    w_qkv, w_out, w_up, w_down, mask_ref, fill_ref, rows_ref,
    sdf_ref, gain_own_one, gain_own_two, counts_ref, load_sem,
):
    micro = lax.axis_index("pipe")
    shard = lax.axis_index("tok")
    part = lax.rem(shard, GROUP)
    first = shard - part
    moves = [
        (sdf_hbm, sdf_ref),
        (gain_own_one_hbm, gain_own_one),
        (gain_own_two_hbm, gain_own_two),
        (counts_hbm, counts_ref),
    ]
    for own, far, held in (
        (qkv_own, qkv_far, w_qkv), (out_own, out_far, w_out), (up_own, up_far, w_up), (down_own, down_far, w_down)
    ):
        moves += [(own.at[0], held.at[micro]), (far.at[0], held.at[1 - micro])]
    loads = [
        pltpu.make_async_copy(source, held, load_sem.at[number]) for number, (source, held) in enumerate(moves)
    ]
    for load in loads:
        load.start()
    for load in loads[:4]:
        load.wait()
    own_is_first = micro == 0
    row = iota((8, WIDTH), 0)
    rows = jnp.where(row == 4, sdf_ref[...], 0.0)
    for which, (own, far) in enumerate(((gain_own_one, gain_far_one), (gain_own_two, gain_far_two))):
        rows = jnp.where(row == which, jnp.where(own_is_first, own[...], far[...]), rows)
        rows = jnp.where(row == 2 + which, jnp.where(own_is_first, far[...], own[...]), rows)
    rows_ref[...] = rows
    key = iota((1, WIDTH), 1) % WIN
    count_of = [counts_ref[micro, first + s] for s in range(GROUP)]
    most = functools.reduce(jnp.maximum, count_of)
    lane_count = jnp.zeros((1, WIDTH), jnp.int32)
    for s in range(GROUP):
        lane_count = jnp.where(key // 4 == s, count_of[s], lane_count)
    for w in range(GROUP):
        dilated = part * WIN + w * 4 + key % 4 < lane_count
        plain = part * WIN + key < count_of[w]
        mask_ref[0, w : w + 1, :] = jnp.where(dilated, 1.0, 0.0)
        mask_ref[1, w : w + 1, :] = jnp.where(plain, 1.0, 0.0)
        blank = jnp.zeros((1, WIDTH), F32)
        fill_ref[0, w : w + 1, :] = jnp.where(part * WIN + w * 4 < most, blank - 1e30, blank)
        fill_ref[1, w : w + 1, :] = jnp.where(part * WIN < count_of[w], blank - 1e30, blank)
    for load in loads[4:]:
        load.wait()


def step_kernel(
    received_ref, w_qkv, w_out, w_up, w_down, mask_buf, fill_buf, rows_ref,
    keep_ref, send_ref,
    x_buf, inv_one, normed_buf, packed_buf, prob_buf, mixed_buf, after_buf, inv_two,
    normed_two_buf, slope_buf, hidden_buf, grads, score_buf, dpacked_buf, store_sem,
):
    micro = lax.axis_index("pipe")
    part = lax.rem(lax.axis_index("tok"), GROUP)

    def gain(section, which):
        number = 2 * section + which
        return rows_ref[number : number + 1, :]

    row_i = iota((ROWS, WIDTH), 0)
    col_i = iota((ROWS, WIDTH), 1)
    same_head = jnp.where(row_i // WIN == col_i // HEAD, 1.0, 0.0).astype(BF)
    swapped = row_i % WIN // 4 * WIN + row_i // WIN * 4 + row_i % 4
    swap = jnp.where(swapped == col_i, 1.0, 0.0).astype(BF)

    def exchange(value):
        return nn(swap, value).astype(BF)

    def expand(value):
        return jnp.concatenate([value] * H, axis=0) * same_head

    def window(value, w):
        return value[w * WIN : (w + 1) * WIN]

    def store_grad(stream, place, value):
        for i in range(ROWS // SLAB):
            slab = place * (ROWS // SLAB) + i
            base = slab % 5 * SLAB
            grads[stream, slab // 5, base : base + SLAB, :] = value[i * SLAB : (i + 1) * SLAB].astype(BF)

    def store_wide(stream, place, value):
        store_grad(stream, place, value[:, :128])
        store_grad(stream, place + 1, value[:, 128:])

    stat_row = iota((8, 128), 0)
    for stream in range(2):
        grads[stream, :, CHUNK:CHUNK_PAD, :] = jnp.zeros((64, CHUNK_PAD - CHUNK, 128), BF)

    def store_stats(stream, lines):
        halves = []
        for line in lines:
            halves += [line[:, i : i + 128] for i in range(0, line.shape[1], 128)]
        for c, line in enumerate(halves):
            high, low = split_two(line)
            both = jnp.where(
                stat_row == 2 * micro, high.astype(F32), jnp.where(stat_row == 2 * micro + 1, low.astype(F32), 0.0)
            )
            grads[stream, STAT_AT + c, CHUNK:CHUNK_PAD, :] = both.astype(BF)

    stores = []

    def send_out(stream, first_chunk, last_chunk):
        number = len(stores)
        chunks = pl.ds(first_chunk, last_chunk - first_chunk)
        copies = [
            pltpu.make_async_copy(grads.at[stream, chunks], ref.at[chunks], store_sem.at[number])
            for ref in (keep_ref, send_ref)
        ]
        stores.append(copies[0])
        pl.when(micro == stream)(copies[0].start)
        pl.when(micro != stream)(copies[1].start)

    def forward(k):
        x = x_buf[k].astype(F32)
        inv = lax.rsqrt(jnp.mean(x * x, axis=-1, keepdims=True) + EPS)
        inv_one[k] = inv
        normed = (x * inv * gain(k, 0)).astype(BF)
        normed_buf[k] = normed
        for j in range(3):
            packed_buf[k, j] = nn(normed, w_qkv[k, :, j * WIDTH : (j + 1) * WIDTH]).astype(BF)
        for w in range(GROUP):
            rows = slice(w * WIN, (w + 1) * WIN)
            scores = nt(packed_buf[k, 0, rows, :], expand(packed_buf[k, 1, rows, :]))
            score_buf[rows, :] = jnp.where(mask_buf[k, w : w + 1, :] > 0.5, scores * HEAD**-0.5, fill_buf[k, w : w + 1, :])
        scores = score_buf[...]
        weights = jnp.exp(scores - group_max(scores, same_head))
        prob = weights / group_sum(weights, same_head)
        prob_buf[k] = prob
        prob_low = prob.astype(BF)
        for w in range(GROUP):
            rows = slice(w * WIN, (w + 1) * WIN)
            mixed_buf[k, rows, :] = nn(window(prob_low, w), expand(packed_buf[k, 2, rows, :])).astype(BF)
        after = x + nn(mixed_buf[k], w_out[k])
        after_buf[k] = after
        inv = lax.rsqrt(jnp.mean(after * after, axis=-1, keepdims=True) + EPS)
        inv_two[k] = inv
        normed_two = (after * inv * gain(k, 1)).astype(BF)
        normed_two_buf[k] = normed_two
        total = after
        for j in range(4):
            cols = slice(j * WIDTH, (j + 1) * WIDTH)
            up = nn(normed_two, w_up[k, :, cols])
            root = math.sqrt(2.0 / math.pi)
            square = up * up
            half = 0.5 * jnp.tanh(up * (root + (root * 0.044715) * square)) + 0.5
            hidden = (up * half).astype(BF)
            hidden_buf[k, j] = hidden
            bend = up * (2 * root + (6 * root * 0.044715) * square)
            slope_buf[k, j] = half * (1.0 + bend * (1.0 - half))
            total = total + nn(hidden, w_down[k, cols, :])
        return total.astype(BF)

    def norm_back(grad, value, inv, gain_row):
        gain_grad = jnp.sum(grad * value * inv, axis=0, keepdims=True)
        scaled = grad * gain_row
        inner = jnp.mean(scaled * value, axis=-1, keepdims=True)
        return inv * (scaled - value * (inv * inv * inner)), gain_grad

    def backward(k, out_grad, slope, pulled):
        back = None
        down_lines = []
        for j in (2, 3, 0, 1):
            cols = slice(j * WIDTH, (j + 1) * WIDTH)
            if k == 0:
                stream, place = (1, 12 + 2 * j) if j >= 2 else (0, 16 + 2 * j)
                out_low = out_grad.astype(BF)
                store_wide(stream, place, tn(hidden_buf[k, j], out_low))
                hidden_grad = nt(out_low, w_down[k, cols, :]).astype(BF).astype(F32)
            else:
                down_lines.append(jnp.sum(hidden_buf[k, j].astype(F32) * slope, axis=0, keepdims=True))
                hidden_grad = slope * pulled[j]
            up_grad = (slope_buf[k, j] * hidden_grad).astype(BF)
            store_wide(k, 2 * j, tn(normed_two_buf[k], up_grad))
            term = nt(up_grad, w_up[k, :, cols])
            back = term if back is None else back + term
            if k == 0 and j == 3:
                send_out(1, 51, 64)
        if k == 0:
            send_out(0, 0, 25)
            send_out(0, 52, 64)
        normed_two_grad = back.astype(BF).astype(F32)
        res_grad, gain_two_grad = norm_back(normed_two_grad, after_buf[k], inv_two[k], gain(k, 1))
        after_grad = out_grad + res_grad
        after_low = after_grad.astype(BF)
        store_wide(k, 8, tn(mixed_buf[k], after_low))
        mixed_grad = nt(after_low, w_out[k]).astype(BF)
        for w in range(GROUP):
            rows = slice(w * WIN, (w + 1) * WIN)
            score_buf[rows, :] = nt(window(mixed_grad, w), expand(packed_buf[k, 2, rows, :]))
        prob = prob_buf[k]
        prob_low = prob.astype(BF)
        prob_grad = score_buf[...].astype(BF).astype(F32)
        flow = prob * prob_grad
        score_grad = (flow - prob * group_sum(flow, same_head)) * HEAD**-0.5

        lane_head = iota((WIN, 128), 1) // HEAD

        def fold(left, right):
            halves = []
            for side in range(2):
                cols = slice(side * 128, (side + 1) * 128)
                value = tn(left[:, cols], right[:, cols])
                total = window(value, 3)
                for h in range(3):
                    total = jnp.where(lane_head == h, window(value, h), total)
                halves.append(total.astype(BF))
            return jnp.concatenate(halves, axis=1)

        for w in range(GROUP):
            rows = slice(w * WIN, (w + 1) * WIN)
            grad_w = jnp.where(mask_buf[k, w : w + 1, :] > 0.5, window(score_grad, w), 0.0).astype(BF)
            dpacked_buf[0, rows, :] = nn(grad_w, expand(packed_buf[k, 1, rows, :])).astype(BF)
            dpacked_buf[1, rows, :] = fold(grad_w, packed_buf[k, 0, rows, :])
            dpacked_buf[2, rows, :] = fold(window(prob_low, w), window(mixed_grad, w))
        back = None
        for j in range(3):
            piece = dpacked_buf[j]
            store_wide(k, 10 + 2 * j, tn(normed_buf[k], piece))
            term = nt(piece, w_qkv[k, :, j * WIDTH : (j + 1) * WIDTH])
            back = term if back is None else back + term
        normed_grad = back.astype(BF).astype(F32)
        in_res, gain_one_grad = norm_back(normed_grad, x_buf[k].astype(F32), inv_one[k], gain(k, 0))
        return (after_grad + in_res).astype(BF), gain_one_grad, gain_two_grad, down_lines[2:] + down_lines[:2]

    received = received_ref[:, 0:WIN, :].reshape(ROWS, WIDTH)
    x_buf[0] = exchange(received)
    x_buf[1] = exchange(forward(0))
    section_one = forward(1).astype(F32)

    pieces = []
    lane_w = iota((WIN, WIDTH), 1)
    row_w = iota((WIN, WIDTH), 0)
    valid_pieces = []
    for s in range(GROUP):
        parts = received_ref[s, WIN : WIN + 8, :].astype(F32)
        line = parts[0:1] + parts[1:2] + parts[2:3]
        chosen = jnp.where(lane_w == part * WIN + row_w, line, 0.0)
        pieces.append(jnp.sum(chosen, axis=-1, keepdims=True))
        valid_pieces.append(
            jnp.sum(jnp.where(lane_w == row_w, mask_buf[1, s : s + 1, :], 0.0), axis=-1, keepdims=True)
        )
    target = jnp.concatenate(pieces, axis=0)
    valid = jnp.concatenate(valid_pieces, axis=0)
    sdf = rows_ref[4:5, :]
    predicted = jnp.sum(section_one * sdf, axis=-1, keepdims=True)
    residue = jnp.where(valid > 0.5, predicted - target, 0.0)
    slope = 2.0 * residue / math.sqrt(3 * ROWS * 64 // 4)
    loss = jnp.sum(residue * residue, axis=0, keepdims=True)
    sdf_grad = jnp.sum(slope * section_one, axis=0, keepdims=True)
    high = sdf.astype(BF).astype(F32)
    middle = (sdf - high).astype(BF).astype(F32)
    row = iota((16, WIDTH), 0)
    parts = jnp.where(row == 0, high, jnp.where(row == 1, middle, jnp.where(row == 2, sdf - high - middle, 0.0)))
    parts = parts.astype(BF)
    pulled = [
        jnp.sum(nt(parts, w_down[1, j * WIDTH : (j + 1) * WIDTH, :]), axis=0, keepdims=True) for j in range(4)
    ]
    loss_row = jnp.broadcast_to(loss, (1, 128))
    middle_grad, gain_one, gain_two, down_lines = backward(1, slope * sdf, slope, pulled)
    store_stats(1, [gain_one, gain_two, sdf_grad, loss_row] + down_lines)
    send_out(1, 0, 51)
    unused, gain_one, gain_two, none = backward(0, exchange(middle_grad).astype(F32), None, None)
    del unused, none
    store_stats(0, [gain_one, gain_two, sdf_grad, loss_row])
    send_out(0, 25, 52)
    for store in stores:
        store.wait()


def wide(source, first_chunk, place, ref, row, col, slabs=range(ROWS // SLAB)):
    for side in range(2):
        for i in slabs:
            slab = (place + side) * (ROWS // SLAB) + i
            low = slab % 5 * SLAB
            piece = source[slab // 5 - first_chunk, low : low + SLAB, :].astype(F32)
            ref[row + i * SLAB : row + (i + 1) * SLAB, col + side * 128 : col + (side + 1) * 128] = piece


def unpack_kernel(
    in_ref, sdf_hbm, loss_ref, sdf_ref, gain_one_ref, qkv_hbm, out_hbm, gain_two_ref, up_hbm, down_hbm,
    qkv_ref, out_ref, up_ref, down_ref, sdf_row_ref, store_sem, load_sem,
):
    micro = lax.axis_index("pipe")
    stores = []

    def store(source, target):
        copy = pltpu.make_async_copy(source, target, store_sem.at[len(stores)])
        copy.start()
        stores.append(copy)

    load = pltpu.make_async_copy(sdf_hbm, sdf_row_ref, load_sem.at[0])
    load.start()
    for ref, target, place, count in ((up_ref, up_hbm, 0, 4), (out_ref, out_hbm, 8, 1), (qkv_ref, qkv_hbm, 10, 3)):
        for quarter in range(4):
            for j in range(count):
                wide(in_ref, 0, place + 2 * j, ref, 0, j * WIDTH, range(4 * quarter, 4 * quarter + 4))
            rows = pl.ds(quarter * 64, 64)
            store(ref.at[rows], target.at[0, rows])
    lines = []
    for c in range(15):
        pair = in_ref[STAT_AT + c, CHUNK:CHUNK_PAD, :].astype(F32)
        lines.append(pair[0:1] + pair[1:2])
    for ref, c in ((gain_one_ref, 0), (gain_two_ref, 2), (sdf_ref, 4)):
        ref[0:1, 0:128] = lines[c]
        ref[0:1, 128:256] = lines[c + 1]
    loss_ref[0:1, :] = lines[6] / (2 * 12288)

    load.wait()

    @pl.when(micro == 0)
    def _():
        for j in range(2):
            wide(in_ref, 0, 16 + 2 * j, down_ref, j * WIDTH, 0)

    @pl.when(micro == 1)
    def _():
        diagonal = iota((128, 128), 0) == iota((128, 128), 1)
        for c in range(8):
            column = jnp.sum(jnp.where(diagonal, lines[7 + c], 0.0), axis=1, keepdims=True)
            down_ref[c * 128 : (c + 1) * 128, :] = column * sdf_row_ref[...]

    store(down_ref.at[pl.ds(0, 2 * WIDTH)], down_hbm.at[0, pl.ds(0, 2 * WIDTH)])
    rows = pl.ds(2 * WIDTH, 2 * WIDTH)
    last = pltpu.make_async_copy(down_ref.at[rows], down_hbm.at[0, rows], store_sem.at[13])
    pl.when(micro == 1)(last.start)
    pl.when(micro == 1)(last.wait)
    for copy in stores:
        copy.wait()


def finish_kernel(moved_hbm, down_in, down_out, moved_ref, half_ref, sem):
    del down_in

    @pl.when(lax.axis_index("pipe") == 0)
    def _():
        load = pltpu.make_async_copy(moved_hbm, moved_ref, sem.at[0])
        load.start()
        load.wait()
        for j in range(2):
            wide(moved_ref, 51, 16 + 2 * j, half_ref, j * WIDTH, 0)
        store = pltpu.make_async_copy(half_ref, down_out.at[0, pl.ds(2 * WIDTH, 2 * WIDTH)], sem.at[1])
        store.start()
        store.wait()


def fix(value):
    return pltpu.with_memory_space_constraint(value, pltpu.HBM)


def swap_pipe(value):
    return lax.ppermute(value, "pipe", [(0, 1), (1, 0)])


VMEM = pl.BlockSpec(memory_space=pltpu.VMEM)
ANY = pl.BlockSpec(memory_space=pl.ANY)
HBM = pl.BlockSpec(memory_space=pltpu.HBM)


def shards(
    features, coarse, parent, counts, target, gain_attn, w_qkv, w_out, gain_mlp, w_up, w_down, w_sdf
):
    rank_count = lax.axis_size("tok")
    rim = lax.ppermute(coarse[:, -1:, :], "tok", [(i, i + 1) for i in range(rank_count - 1)])
    arrived = []
    for value in (gain_attn, gain_mlp, w_qkv, w_out, w_up, w_down):
        arrived.append(swap_pipe(value))
    gains_far = arrived[:2]
    qkv_far, out_far, up_far, down_far = arrived[2:]
    embedded, rim_hot = pl.pallas_call(
        embed_kernel,
        out_shape=(
            jax.ShapeDtypeStruct((GROUP, SEND_ROWS, WIDTH), BF),
            jax.ShapeDtypeStruct((16, ROWS), BF),
        ),
        in_specs=[HBM] * 4,
        out_specs=(VMEM, VMEM),
        scratch_shapes=[
            pltpu.VMEM((ROWS, WIDTH), BF),
            pltpu.VMEM((64, WIDTH), BF),
            pltpu.VMEM((2, ROWS), jnp.int32),
            pltpu.VMEM((2, ROWS), F32),
            pltpu.SemaphoreType.DMA((4,)),
        ],
        name="embed",
        compiler_params=pltpu.CompilerParams(vmem_limit_bytes=4 * 2**20),
    )(fix(features), fix(coarse), fix(parent), fix(target))
    outgoing = pl.pallas_call(
        rim_kernel,
        out_shape=jax.ShapeDtypeStruct((GROUP, SEND_ROWS, WIDTH), BF),
        in_specs=[VMEM] * 3,
        out_specs=VMEM,
        name="add_rim",
        compiler_params=pltpu.CompilerParams(vmem_limit_bytes=4 * 2**20),
    )(embedded, rim_hot, rim)
    groups = [[b * GROUP + i for i in range(GROUP)] for b in range(rank_count // GROUP)]
    received = lax.all_to_all(outgoing, "tok", 0, 0, axis_index_groups=groups, tiled=True)
    packet = jax.ShapeDtypeStruct((64, CHUNK_PAD, 128), BF)
    arranged = pl.pallas_call(
        arrange_kernel,
        out_shape=(
            jax.ShapeDtypeStruct((2, WIDTH, 3 * WIDTH), BF),
            jax.ShapeDtypeStruct((2, WIDTH, WIDTH), BF),
            jax.ShapeDtypeStruct((2, WIDTH, FF), BF),
            jax.ShapeDtypeStruct((2, FF, WIDTH), BF),
            jax.ShapeDtypeStruct((2, GROUP, WIDTH), F32),
            jax.ShapeDtypeStruct((2, GROUP, WIDTH), F32),
            jax.ShapeDtypeStruct((8, WIDTH), F32),
        ),
        in_specs=[VMEM] * 2 + [HBM] * 4 + [HBM] * 8,
        out_specs=(VMEM,) * 7,
        scratch_shapes=[
            pltpu.VMEM((1, WIDTH), F32),
            pltpu.VMEM((1, WIDTH), F32),
            pltpu.VMEM((1, WIDTH), F32),
            pltpu.SMEM((2, 64), jnp.int32),
            pltpu.SemaphoreType.DMA((12,)),
        ],
        name="arrange",
        compiler_params=pltpu.CompilerParams(vmem_limit_bytes=8 * 2**20),
    )(
        *gains_far, fix(counts), fix(w_sdf[None]), fix(gain_attn), fix(gain_mlp),
        fix(w_qkv), fix(qkv_far), fix(w_out), fix(out_far), fix(w_up), fix(up_far), fix(w_down), fix(down_far),
    )
    keep, send = pl.pallas_call(
        step_kernel,
        out_shape=(packet, packet),
        in_specs=[VMEM] * 8,
        out_specs=(ANY, ANY),
        scratch_shapes=[
            pltpu.VMEM((2, ROWS, WIDTH), BF),
            pltpu.VMEM((2, ROWS, 1), F32),
            pltpu.VMEM((2, ROWS, WIDTH), BF),
            pltpu.VMEM((2, 3, ROWS, WIDTH), BF),
            pltpu.VMEM((2, ROWS, WIDTH), F32),
            pltpu.VMEM((2, ROWS, WIDTH), BF),
            pltpu.VMEM((2, ROWS, WIDTH), F32),
            pltpu.VMEM((2, ROWS, 1), F32),
            pltpu.VMEM((2, ROWS, WIDTH), BF),
            pltpu.VMEM((2, 4, ROWS, WIDTH), F32),
            pltpu.VMEM((2, 4, ROWS, WIDTH), BF),
            pltpu.VMEM((2, 64, CHUNK_PAD, 128), BF),
            pltpu.VMEM((ROWS, WIDTH), F32),
            pltpu.VMEM((3, ROWS, WIDTH), BF),
            pltpu.SemaphoreType.DMA((5,)),
        ],
        name="step",
        compiler_params=pltpu.CompilerParams(vmem_limit_bytes=20 * 2**20),
    )(received, *arranged)
    far = swap_pipe(send)
    total = (keep.astype(F32) + far.astype(F32)).astype(BF)
    shares = lax.all_to_all(total, "tok", 0, 0, tiled=True)
    summed = jnp.sum(shares.astype(F32), axis=0)
    stat = jnp.sum(summed[CHUNK : CHUNK + 4], axis=0, keepdims=True)
    high = lax.reduce_precision(stat, 8, 7)
    row = iota((CHUNK_PAD, 128), 0)
    tail = jnp.where(row == CHUNK, high, jnp.where(row == CHUNK + 1, stat - high, 0.0))
    summed = jnp.where(row < CHUNK, summed, tail).astype(BF)
    gathered = lax.all_to_all(
        jnp.broadcast_to(summed[None], (rank_count, CHUNK_PAD, 128)), "tok", 0, 0, tiled=True
    )
    moved = lax.ppermute(gathered[51:64], "pipe", [(1, 0)])
    loss, sdf, gain_one, qkv, out, gain_two, up, down = pl.pallas_call(
        unpack_kernel,
        out_shape=(
            jax.ShapeDtypeStruct((1, 128), F32),
            jax.ShapeDtypeStruct((1, WIDTH), F32),
            jax.ShapeDtypeStruct((1, WIDTH), F32),
            jax.ShapeDtypeStruct((1, WIDTH, 3 * WIDTH), F32),
            jax.ShapeDtypeStruct((1, WIDTH, WIDTH), F32),
            jax.ShapeDtypeStruct((1, WIDTH), F32),
            jax.ShapeDtypeStruct((1, WIDTH, FF), F32),
            jax.ShapeDtypeStruct((1, FF, WIDTH), F32),
        ),
        in_specs=[VMEM, HBM],
        out_specs=(VMEM, VMEM, VMEM, HBM, HBM, VMEM, HBM, HBM),
        scratch_shapes=[
            pltpu.VMEM((WIDTH, 3 * WIDTH), F32),
            pltpu.VMEM((WIDTH, WIDTH), F32),
            pltpu.VMEM((WIDTH, FF), F32),
            pltpu.VMEM((FF, WIDTH), F32),
            pltpu.VMEM((1, WIDTH), F32),
            pltpu.SemaphoreType.DMA((14,)),
            pltpu.SemaphoreType.DMA((1,)),
        ],
        name="unpack",
        compiler_params=pltpu.CompilerParams(vmem_limit_bytes=16 * 2**20),
    )(gathered, fix(w_sdf[None]))
    down = pl.pallas_call(
        finish_kernel,
        out_shape=jax.ShapeDtypeStruct((1, FF, WIDTH), F32),
        in_specs=[ANY, HBM],
        out_specs=HBM,
        scratch_shapes=[
            pltpu.VMEM((13, CHUNK_PAD, 128), BF),
            pltpu.VMEM((2 * WIDTH, WIDTH), F32),
            pltpu.SemaphoreType.DMA((2,)),
        ],
        input_output_aliases={1: 0},
        name="finish",
        compiler_params=pltpu.CompilerParams(vmem_limit_bytes=16 * 2**20),
    )(moved, down)
    return loss[0, 0], sdf[0], gain_one, qkv, out, gain_two, up, down


def solution(mesh):
    return jax.shard_map(
        shards,
        mesh=mesh,
        in_specs=(
            P(None, "tok", None),
            P(None, "tok", None),
            P(None, "tok"),
            P(),
            P(None, "tok"),
            P("pipe", None),
            P("pipe", None, None),
            P("pipe", None, None),
            P("pipe", None),
            P("pipe", None, None),
            P("pipe", None, None),
            P(),
        ),
        out_specs=(
            P(),
            P(),
            P("pipe", None),
            P("pipe", None, None),
            P("pipe", None, None),
            P("pipe", None),
            P("pipe", None, None),
            P("pipe", None, None),
        ),
        check_vma=False,
    )
```
